256 devices in a mesh: strip: 16 (over z, core), sample: 16 (over y, x).
Axes of the slice: x: 4, y: 4, z: 8, core: 2. Of those that a mesh axis runs over, the one named last changes fastest.
Arguments:
- images: bfloat16 [16, 48, 108, 2048], P('sample', 'strip'), may hold values from -36 to 36
- w_point: bfloat16 [2048, 256], P('sample'), may hold values from -0.125 to 0.125
- w_atrous: bfloat16 [2048, 2304], P('sample'), may hold values from -0.046875 to 0.046875
- w_image: bfloat16 [2048, 256], P('sample'), may hold values from -0.125 to 0.125
- w_proj: bfloat16 [768, 256], P('sample'), may hold values from -0.21875 to 0.21875
- cotangent: bfloat16 [16, 48, 108, 256], P('sample', 'strip'), may hold values from -6 to 6
Outputs:
- result: bfloat16 [16, 48, 108, 256], P('sample', 'strip')
- input_grad: bfloat16 [16, 48, 108, 2048], P('sample', 'strip')
- grad_point: float32 [2048, 256], P('sample')
- grad_atrous: float32 [2048, 2304], P('sample')
- grad_image: float32 [2048, 256], P('sample')
- grad_proj: float32 [768, 256], P('sample')
The draws below stay inside these ranges and needn't reach their ends.
All inputs are finite; a program needn't handle non-finite values.
Results may differ from the reference program's by a relative error of at most 0.038.
Values may be sent and summed in bfloat16 or wider, within the bound.
A program may use at most 128 MiB of HBM per device.

```python
import math
import jax
import jax.numpy as jnp
from jax import lax

CIN = 2048
FEAT = 256
DILATION_RATE = 12
COLS = 108
SAMPLES = 16
HEIGHT = 48
N_STRIP = 16


def draw_images(key, part):
    key_list = jax.random.split(key, 5)
    full_shape = (SAMPLES, HEIGHT, COLS, CIN)
    rise_rows = 3.0 ** (jnp.arange(HEIGHT, dtype=jnp.float32) / (HEIGHT - 1))
    roughness = jnp.exp(jax.random.uniform(key_list[0], (HEIGHT, COLS), minval=0.0, maxval=math.log(10.0 / 3.0)))
    position = 0.3 * rise_rows[:, None] * roughness
    channel = jnp.exp(jax.random.uniform(key_list[1], (CIN,), minval=math.log(0.5), maxval=math.log(2.0)))
    offset = jax.random.uniform(key_list[2], (SAMPLES, CIN), minval=-1.0, maxval=1.0)
    noise_part = jax.random.truncated_normal(key_list[4], -3.0, 3.0, full_shape)
    core_part = offset[:, None, None, :] + noise_part
    values = position[None, :, :, None] * channel * core_part
    return values.astype(jnp.float32).astype(jnp.bfloat16)


def block_scale(key, shape, cuts, smallest, high):
    level = 1.0
    for dim, shards_of in cuts:
        draws = jax.random.uniform(jax.random.fold_in(jax.random.fold_in(key, 6), dim), (shards_of,), jnp.float32, smallest / len(cuts), high / len(cuts))
        level = level * jnp.repeat(jnp.exp(draws), shape[dim] // shards_of).reshape((-1,) + (1,) * (len(shape) - 1 - dim))
    return level


def gaussian(stream_key, dims, scale, reach, cuts=(), kind=jnp.bfloat16):
    level = block_scale(stream_key, dims, cuts, -0.22, 0.18) if cuts else 1.0
    entries = jax.random.normal(stream_key, dims, jnp.float32) * scale * level
    return jnp.minimum(jnp.maximum(entries, -reach), reach).astype(kind)


def setup_inputs(seed: int = 0) -> dict:
    seeds = jax.random.split(jax.random.key(seed), 7)
    return {
        "images": draw_images(jax.random.fold_in(seeds[6], 71), 0),
        "w_point": gaussian(seeds[1], (CIN, FEAT), CIN ** -0.5, 0.125, ((0, 16),)),
        "w_atrous": gaussian(seeds[2], (CIN, 9 * FEAT), (9 * CIN) ** -0.5, 0.046875, ((0, 16),)),
        "w_image": gaussian(seeds[3], (CIN, FEAT), CIN ** -0.5, 0.125, ((0, 16),)),
        "w_proj": gaussian(seeds[4], (3 * FEAT, FEAT), (3 * FEAT) ** -0.5, 0.21875, ((0, 16),)),
        "cotangent": gaussian(seeds[5], (SAMPLES, HEIGHT, COLS, FEAT), 1.0, 6.0, ((0, 16), (1, 16))),
    }


EPSILON = 1e-05

def shifted_axis(values, offset, axis_dim):
    if offset == 0:
        return values
    length = values.shape[axis_dim]
    margin = abs(offset)
    pad_widths = [(0, 0)] * values.ndim
    pad_widths[axis_dim] = (margin, margin)
    padded = jnp.pad(values, pad_widths)
    return lax.slice_in_dim(padded, margin + offset, margin + offset + length, axis=axis_dim)

def contract_last(left, right):
    return lax.dot_general(left, right, (((left.ndim - 1,), (1,)), ((), ())), preferred_element_type=jnp.float32)

def tap_stack(gradient_list, row_stride):
    shifted_rows = shifted_axis(gradient_list, -DILATION_RATE * row_stride, 0)
    return jnp.concatenate([shifted_axis(shifted_rows, -DILATION_RATE * column_stride, 1) for column_stride in (-1, 0, 1)], -1)

def rounded(values):
    return lax.optimization_barrier(values.astype(jnp.bfloat16)).astype(jnp.float32)

def swish(values):
    return values * jax.nn.sigmoid(values)

def swish_slope(values):
    sigma = jax.nn.sigmoid(values)
    return sigma * (1.0 + values * (1.0 - sigma))

def normalize(values):
    centre = lax.optimization_barrier(jnp.mean(values, axis=(0, 1, 2)))
    spread = lax.optimization_barrier(jnp.mean(jnp.square(values - centre), axis=(0, 1, 2)))
    scale = lax.rsqrt(spread + EPSILON)
    return ((values - centre) * scale, scale)

def norm_back(upstream, normed, scale):
    first_mean = lax.optimization_barrier(jnp.mean(upstream, axis=(0, 1, 2)))
    second_mean = lax.optimization_barrier(jnp.mean(upstream * normed, axis=(0, 1, 2)))
    return (upstream - first_mean - normed * second_mean) * scale

def reference(images, w_point, w_atrous, w_image, w_proj, cotangent):
    chan_count, out_width = w_point.shape
    tap_band = 3 * out_width
    map_area = images.shape[1] * images.shape[2]
    factor = 1.0 / SAMPLES

    def forward_sample(sample_map):
        point_out = jnp.dot(sample_map, w_point, preferred_element_type=jnp.float32)
        dilated_branch_output = jnp.zeros(point_out.shape, jnp.float32)
        for row_stride in (-1, 0, 1):
            tap_product = jnp.dot(sample_map, w_atrous[:, (row_stride + 1) * tap_band:(row_stride + 2) * tap_band], preferred_element_type=jnp.float32)
            tap_product = shifted_axis(tap_product, DILATION_RATE * row_stride, 0)
            for column_stride in (-1, 0, 1):
                kernel_tap_slice = tap_product[..., (column_stride + 1) * out_width:(column_stride + 2) * out_width]
                dilated_branch_output = dilated_branch_output + shifted_axis(kernel_tap_slice, DILATION_RATE * column_stride, 1)
        pool_sums = lax.optimization_barrier(jnp.sum(sample_map, axis=(0, 1), dtype=jnp.float32))
        return (point_out, dilated_branch_output, pool_sums)
    point_out, dilated_branch_output, pool_sums = lax.map(forward_sample, images)
    norm_point, scale_point = normalize(point_out)
    norm_atrous, scale_atrous = normalize(dilated_branch_output)
    relu_point = swish(norm_point).astype(jnp.bfloat16)
    relu_atrous = swish(norm_atrous).astype(jnp.bfloat16)
    pooled = (pool_sums / map_area).astype(jnp.bfloat16)
    image_out = jnp.dot(pooled, w_image, preferred_element_type=jnp.float32)
    layer_mean = lax.optimization_barrier(jnp.mean(image_out, axis=-1, keepdims=True))
    layer_spread = lax.optimization_barrier(jnp.mean(jnp.square(image_out - layer_mean), axis=-1, keepdims=True))
    layer_scale = lax.rsqrt(layer_spread + EPSILON)
    layer_norm = (image_out - layer_mean) * layer_scale
    relu_image = swish(layer_norm).astype(jnp.bfloat16)
    relu_joined = jnp.concatenate([relu_point, relu_atrous], -1)
    mixed_out = jnp.dot(relu_joined, w_proj[:2 * out_width], preferred_element_type=jnp.float32)
    mixed_out = mixed_out + jnp.dot(relu_image, w_proj[2 * out_width:], preferred_element_type=jnp.float32)[:, None, None, :]
    norm_mix, scale_mix = normalize(mixed_out)
    result = swish(norm_mix).astype(jnp.bfloat16)
    upstream = cotangent.astype(jnp.float32) * swish_slope(norm_mix)
    grad_mix = norm_back(upstream, norm_mix, scale_mix)
    grad_mix_b = grad_mix.astype(jnp.bfloat16)
    column_b = lax.optimization_barrier(jnp.sum(grad_mix, axis=(1, 2))).astype(jnp.bfloat16)
    back_joined = contract_last(grad_mix_b, w_proj[:2 * out_width])
    back_image = contract_last(column_b, w_proj[2 * out_width:])
    up_image = back_image * swish_slope(layer_norm)
    grad_image_f = (up_image - lax.optimization_barrier(jnp.mean(up_image, axis=-1, keepdims=True)) - layer_norm * lax.optimization_barrier(jnp.mean(up_image * layer_norm, axis=-1, keepdims=True))) * layer_scale
    grad_image_b = grad_image_f.astype(jnp.bfloat16)
    grad_pool = contract_last(grad_image_b, w_image)
    up_point = back_joined[..., :out_width] * swish_slope(norm_point)
    up_atrous = back_joined[..., out_width:] * swish_slope(norm_atrous)
    grad_point_b = norm_back(up_point, norm_point, scale_point).astype(jnp.bfloat16)
    grad_atrous_b = norm_back(up_atrous, norm_atrous, scale_atrous).astype(jnp.bfloat16)

    def input_sample(parts_in):
        point_grad, atrous_grad, pool_grad = parts_in
        summed_terms = contract_last(point_grad, w_point) + pool_grad / map_area
        for row_stride in (-1, 0, 1):
            stacked = tap_stack(atrous_grad, row_stride)
            summed_terms = summed_terms + contract_last(stacked, w_atrous[:, (row_stride + 1) * tap_band:(row_stride + 2) * tap_band])
        return summed_terms.astype(jnp.bfloat16)
    input_grad = lax.map(input_sample, (grad_point_b, grad_atrous_b, grad_pool))

    def grad_sample(carried, parts_in):
        sample_map, point_grad, atrous_grad, joined_map, mix_grad = parts_in
        columns_all = jnp.concatenate([point_grad] + [tap_stack(atrous_grad, row_stride) for row_stride in (-1, 0, 1)], -1)
        strip_maps = sample_map.reshape(N_STRIP, -1, chan_count)
        strip_cols = columns_all.reshape(N_STRIP, -1, 10 * out_width)
        strip_joined = joined_map.reshape(N_STRIP, -1, 2 * out_width)
        strip_mix = mix_grad.reshape(N_STRIP, -1, out_width)

        def grad_strip(inner_sums, pieces):
            map_piece, col_piece, joined_piece, mix_piece = pieces
            weight_part = lax.dot_general(map_piece, col_piece, (((0,), (0,)), ((), ())), preferred_element_type=jnp.float32) * factor
            proj_part = lax.dot_general(joined_piece, mix_piece, (((0,), (0,)), ((), ())), preferred_element_type=jnp.float32) * factor
            return ((inner_sums[0] + rounded(weight_part), inner_sums[1] + rounded(proj_part)), None)
        carried, unused = lax.scan(grad_strip, carried, (strip_maps, strip_cols, strip_joined, strip_mix))
        return (carried, None)
    start_sums = (jnp.zeros((chan_count, 10 * out_width), jnp.float32), jnp.zeros((2 * out_width, out_width), jnp.float32))
    (weight_sums, proj_sums), unused = lax.scan(grad_sample, start_sums, (images, grad_point_b, grad_atrous_b, relu_joined, grad_mix_b))
    outer_terms = pooled.astype(jnp.float32)[:, :, None] * (grad_image_b.astype(jnp.float32) * factor)[:, None, :]
    grad_image = lax.optimization_barrier(jnp.sum(rounded(outer_terms), axis=0))
    proj_terms = relu_image.astype(jnp.float32)[:, :, None] * (column_b.astype(jnp.float32) * factor)[:, None, :]
    grad_proj = jnp.concatenate([proj_sums, lax.optimization_barrier(jnp.sum(rounded(proj_terms), axis=0))], 0)
    return (result, input_grad, weight_sums[:, :out_width], weight_sums[:, out_width:], grad_image, grad_proj)
```

```python
import jax
import jax.numpy as jnp
from jax import lax
from jax.experimental import pallas as pl
from jax.experimental.pallas import tpu as pltpu
from jax.sharding import Mesh
from jax.sharding import PartitionSpec as P

DILATION_RATE = 12
STRIP_SAMPLE = ("strip_0", "strip_1", "sample_0", "sample_1")
STRIP = ("strip_0", "strip_1")
SAMPLE = ("sample_0", "sample_1")


EPSILON = 1e-05


MESH_ID = pl.DeviceIdType.MESH


def total_kernel(x_ref, strip_ref, out_ref, slots_a, slots_b, send_a, recv_a, send_b, recv_b):
    strip = lax.axis_index("strip_0") * 2 + lax.axis_index("strip_1")
    sample = lax.axis_index("sample_0") * 4 + lax.axis_index("sample_1")

    def strip_peer(k):
        other = lax.rem(strip + k, 16)
        return {"strip_0": lax.div(other, 2), "strip_1": lax.rem(other, 2)}

    def sample_peer(k):
        other = lax.rem(sample + k, 16)
        return {"sample_0": lax.div(other, 4), "sample_1": lax.rem(other, 4)}

    barrier = pltpu.get_barrier_semaphore()
    for k in range(1, 16):
        pl.semaphore_signal(barrier, inc=1, device_id=strip_peer(k), device_id_type=MESH_ID)
        pl.semaphore_signal(barrier, inc=1, device_id=sample_peer(k), device_id_type=MESH_ID)
    pl.semaphore_wait(barrier, 30)

    def stage(source, slots, me, peer, send, recv):
        copies = []
        for k in range(1, 16):
            copy = pltpu.make_async_remote_copy(
                src_ref=source,
                dst_ref=slots.at[me],
                send_sem=send.at[k - 1],
                recv_sem=recv.at[k - 1],
                device_id=peer(k),
                device_id_type=MESH_ID,
            )
            copy.start()
            copies.append(copy)
        slots[me] = source[...]
        for copy in copies:
            copy.wait()
        return jnp.sum(slots[...], axis=0)

    strip_ref[...] = stage(x_ref, slots_a, strip, strip_peer, send_a, recv_a)
    out_ref[...] = stage(strip_ref, slots_b, sample, sample_peer, send_b, recv_b)


def mesh_total(array, call_id):
    shape = array.shape
    flat = array.reshape(-1, shape[-1])
    rows, width = flat.shape
    spec = pl.BlockSpec(memory_space=pltpu.VMEM)
    strip_sum, total = pl.pallas_call(
        total_kernel,
        out_shape=[jax.ShapeDtypeStruct((rows, width), jnp.float32)] * 2,
        in_specs=[spec],
        out_specs=[spec, spec],
        scratch_shapes=[
            pltpu.VMEM((16, rows, width), jnp.float32),
            pltpu.VMEM((16, rows, width), jnp.float32),
            pltpu.SemaphoreType.DMA((15,)),
            pltpu.SemaphoreType.DMA((15,)),
            pltpu.SemaphoreType.DMA((15,)),
            pltpu.SemaphoreType.DMA((15,)),
        ],
        compiler_params=pltpu.CompilerParams(collective_id=call_id, has_side_effects=True),
        name=f"mesh_total_{call_id}",
    )(flat)
    return total.reshape(shape)


def side_by_side(arrays, axis, dim, along):
    widths = [a.shape[along] for a in arrays]
    both = jnp.concatenate(arrays, axis=along)
    filled = lax.all_gather(both, axis, axis=dim, tiled=True)
    return tuple(jnp.split(filled, [sum(widths[:k]) for k in range(1, len(widths))], axis=along))


def from_everyone(array, axis):
    peers = lax.axis_size(axis)
    return lax.all_to_all(
        jnp.broadcast_to(array[None], (peers, *array.shape)), axis, 0, 0, tiled=True
    )


def taken_together(array, axis):
    return from_everyone(array, axis).sum(axis=0)


def passed_along(array, axis, by):
    peers = lax.axis_size(axis)
    pairs = [(i, i + by) for i in range(peers) if 0 <= i + by < peers]
    return lax.ppermute(array, axis, pairs)


def cut_along(array, dim, peers):
    before, after = (array.shape[:dim], array.shape[dim + 1 :])
    return jnp.moveaxis(array.reshape(*before, peers, -1, *after), dim, 0)


def sum_at_owner(array, axis, dim):
    tiles = cut_along(array, dim, lax.axis_size(axis))
    arrived = lax.all_to_all(tiles, axis, split_axis=0, concat_axis=0, tiled=True)
    return arrived.astype(jnp.float32).sum(axis=0)


def joined_along(tiles, dim):
    lengths = list(tiles.shape[1:])
    lengths[dim] *= tiles.shape[0]
    return jnp.moveaxis(tiles, 0, dim).reshape(lengths)


def gather_directly(array, axis, dim):
    tiles = from_everyone(array, axis)
    return joined_along(tiles, dim)


def total_of_pieces(array, axis):
    return lax.all_gather(array, axis).astype(jnp.float32).sum(0)


def shifted_axis(values, offset, axis_dim):
    if offset == 0:
        return values
    length = values.shape[axis_dim]
    margin = abs(offset)
    pad_widths = [(0, 0)] * values.ndim
    pad_widths[axis_dim] = (margin, margin)
    padded = jnp.pad(values, pad_widths)
    return lax.slice_in_dim(padded, margin + offset, margin + offset + length, axis=axis_dim)


def contract_last(left, right):
    return lax.dot_general(
        left, right, (((left.ndim - 1,), (1,)), ((), ())), preferred_element_type=jnp.float32
    )


def swish(values):
    return values * jax.nn.sigmoid(values)


def swish_slope(values):
    sigma = jax.nn.sigmoid(values)
    return sigma * (1.0 + values * (1.0 - sigma))


def row_part(source, tap_rows, out_width):
    tap_product = jnp.dot(source, tap_rows, preferred_element_type=jnp.float32)
    summed_terms = jnp.zeros(tap_product.shape[:-1] + (out_width,), jnp.float32)
    for column_stride in (-1, 0, 1):
        kernel_tap_slice = tap_product[
            ..., (column_stride + 1) * out_width : (column_stride + 2) * out_width
        ]
        summed_terms = summed_terms + shifted_axis(
            kernel_tap_slice, DILATION_RATE * column_stride, 1
        )
    return summed_terms


def column_stack(gradient_list):
    return jnp.concatenate(
        [
            shifted_axis(gradient_list, -DILATION_RATE * column_stride, 1)
            for column_stride in (-1, 0, 1)
        ],
        -1,
    )


def moments(values, position_count, call_id):
    branch_sums = jnp.stack([jnp.sum(tensor, axis=(0, 1)) for tensor in values])
    squares = jnp.stack([jnp.sum(jnp.square(tensor), axis=(0, 1)) for tensor in values])
    totals, powers = mesh_total(jnp.stack([branch_sums, squares]), call_id)
    centres = totals / position_count
    variances = powers / position_count - jnp.square(centres)
    return (centres, variances)


def on_device(images, w_point, w_atrous, w_image, w_proj, cotangent):
    sample_map = images[0]
    strip_row_count, col_count, chan_count = sample_map.shape
    out_width = w_point.shape[1]
    tap_band = 3 * out_width
    strips = lax.axis_size(STRIP)
    samples = lax.axis_size(SAMPLE)
    map_area = strips * strip_row_count * col_count
    position_count = samples * map_area
    strip_extent = DILATION_RATE // strip_row_count
    factor = 1.0 / samples
    point_full, atrous_full, image_full, proj_full = (
        *side_by_side((w_point, w_atrous, w_image), SAMPLE, 0, 1),
        lax.all_gather(w_proj, SAMPLE, axis=0, tiled=True),
    )
    pool_total = taken_together(jnp.sum(sample_map, axis=(0, 1), dtype=jnp.float32), STRIP)
    pooled = (pool_total / map_area).astype(jnp.bfloat16)

    def tap_rows(row_stride):
        return atrous_full[:, (row_stride + 1) * tap_band : (row_stride + 2) * tap_band]

    point_out = jnp.dot(sample_map, point_full, preferred_element_type=jnp.float32)
    dilated_branch_output = row_part(sample_map, tap_rows(0), out_width)
    for row_stride in (1, -1):
        dilated_branch_output = dilated_branch_output + passed_along(
            row_part(sample_map, tap_rows(row_stride), out_width).astype(jnp.bfloat16),
            STRIP,
            -row_stride * strip_extent,
        )
    centres, variances = moments([point_out, dilated_branch_output], position_count, 0)
    scales = lax.rsqrt(variances + EPSILON)
    norm_point = (point_out - centres[0]) * scales[0]
    norm_atrous = (dilated_branch_output - centres[1]) * scales[1]
    relu_joined = jnp.concatenate(
        [swish(norm_point).astype(jnp.bfloat16), swish(norm_atrous).astype(jnp.bfloat16)], -1
    )
    image_out = jnp.dot(pooled, image_full, preferred_element_type=jnp.float32)
    layer_mean = jnp.mean(image_out)
    layer_spread = jnp.mean(jnp.square(image_out - layer_mean))
    layer_scale = lax.rsqrt(layer_spread + EPSILON)
    layer_norm = (image_out - layer_mean) * layer_scale
    relu_image = swish(layer_norm).astype(jnp.bfloat16)
    mixed_out = jnp.dot(relu_joined, proj_full[: 2 * out_width], preferred_element_type=jnp.float32)
    mixed_out = mixed_out + jnp.dot(
        relu_image, proj_full[2 * out_width :], preferred_element_type=jnp.float32
    )
    mix_centre, mix_spread = moments([mixed_out], position_count, 1)
    mix_scale = lax.rsqrt(mix_spread[0] + EPSILON)
    norm_mix = (mixed_out - mix_centre[0]) * mix_scale
    result = swish(norm_mix).astype(jnp.bfloat16)
    upstream = cotangent[0].astype(jnp.float32) * swish_slope(norm_mix)
    first_sum, second_sum = mesh_total(
        jnp.stack([jnp.sum(upstream, axis=(0, 1)), jnp.sum(upstream * norm_mix, axis=(0, 1))]), 2
    )
    grad_mix = (
        upstream - first_sum / position_count - norm_mix * (second_sum / position_count)
    ) * mix_scale
    grad_mix_b = grad_mix.astype(jnp.bfloat16)
    column_total = taken_together(jnp.sum(grad_mix, axis=(0, 1)), STRIP)
    column_b = column_total.astype(jnp.bfloat16)
    back_joined = contract_last(grad_mix_b, proj_full[: 2 * out_width])
    back_image = contract_last(column_b, proj_full[2 * out_width :])
    up_image = back_image * swish_slope(layer_norm)
    grad_image_b = (
        (up_image - jnp.mean(up_image) - layer_norm * jnp.mean(up_image * layer_norm)) * layer_scale
    ).astype(jnp.bfloat16)
    grad_pool = contract_last(grad_image_b, image_full)
    up_point = back_joined[..., :out_width] * swish_slope(norm_point)
    up_atrous = back_joined[..., out_width:] * swish_slope(norm_atrous)
    local_sums = jnp.stack(
        [
            jnp.sum(up_point, axis=(0, 1)),
            jnp.sum(up_point * norm_point, axis=(0, 1)),
            jnp.sum(up_atrous, axis=(0, 1)),
            jnp.sum(up_atrous * norm_atrous, axis=(0, 1)),
        ]
    )
    branch_means = mesh_total(local_sums, 3) / position_count
    grad_point_b = ((up_point - branch_means[0] - norm_point * branch_means[1]) * scales[0]).astype(
        jnp.bfloat16
    )
    grad_atrous_b = (
        (up_atrous - branch_means[2] - norm_atrous * branch_means[3]) * scales[1]
    ).astype(jnp.bfloat16)
    input_grad = contract_last(grad_point_b, point_full) + grad_pool / map_area
    column_sets = []
    for row_stride in (-1, 0, 1):
        if row_stride == 0:
            source = grad_atrous_b
        else:
            source = passed_along(grad_atrous_b, STRIP, row_stride * strip_extent)
        stacked = column_stack(source)
        column_sets.append(stacked)
        input_grad = input_grad + contract_last(stacked, tap_rows(row_stride))
    image_gate = jnp.where(lax.axis_index(STRIP) == 0, 1.0, 0.0).astype(jnp.float32)
    columns_all = jnp.concatenate([grad_point_b] + column_sets, -1).reshape(
        strip_row_count * col_count, 10 * out_width
    )
    flat_map = sample_map.reshape(strip_row_count * col_count, chan_count)
    image_cols = grad_image_b.astype(jnp.float32) * (image_gate * factor)
    pooled_wide = pooled.astype(jnp.float32)
    proj_local = (
        lax.dot_general(
            relu_joined.reshape(-1, 2 * out_width),
            grad_mix_b.reshape(-1, out_width),
            (((0,), (0,)), ((), ())),
            preferred_element_type=jnp.float32,
        )
        * factor
    )
    proj_image = (
        relu_image.astype(jnp.float32)[:, None]
        * (column_b.astype(jnp.float32) * (image_gate * factor))[None, :]
    )
    proj_shard = sum_at_owner(
        jnp.concatenate([proj_local, proj_image], 0).astype(jnp.bfloat16), SAMPLE, 0
    )
    chan_piece = chan_count // (samples * strips)
    swapped_map = (
        flat_map.reshape(strip_row_count * col_count, samples, strips, chan_piece)
        .transpose(0, 2, 1, 3)
        .reshape(strip_row_count * col_count, chan_count)
    )
    swapped_pool = (
        pooled_wide.reshape(samples, strips, chan_piece).transpose(1, 0, 2).reshape(chan_count)
    )
    tap_terms = (
        lax.dot_general(
            swapped_map, columns_all, (((0,), (0,)), ((), ())), preferred_element_type=jnp.float32
        )
        * factor
    )
    strip_section = lax.psum_scatter(
        jnp.concatenate([tap_terms, swapped_pool[:, None] * image_cols[None, :]], 1).astype(
            jnp.bfloat16
        ),
        STRIP,
        scatter_dimension=0,
        tiled=True,
    )
    shard_part = sum_at_owner(strip_section, SAMPLE, 0)
    weight_total = gather_directly(shard_part.astype(jnp.bfloat16), STRIP, 0).astype(
        shard_part.dtype
    )
    proj_total = total_of_pieces(proj_shard.astype(jnp.bfloat16), STRIP).astype(jnp.float32)
    return (
        result[None],
        input_grad.astype(jnp.bfloat16)[None],
        weight_total[:, :out_width],
        weight_total[:, out_width : 10 * out_width],
        weight_total[:, 10 * out_width :],
        proj_total,
    )


def solution(mesh):
    finer = Mesh(mesh.devices.reshape(8, 2, 4, 4), ("strip_0", "strip_1", "sample_0", "sample_1"))
    placed = (
        P(SAMPLE, STRIP, None, None),
        P(SAMPLE, None),
        P(SAMPLE, None),
        P(SAMPLE, None),
        P(SAMPLE, None),
        P(SAMPLE, STRIP, None, None),
    )
    return jax.shard_map(
        on_device,
        mesh=finer,
        in_specs=placed,
        out_specs=(
            P(SAMPLE, STRIP, None, None),
            P(SAMPLE, STRIP, None, None),
            P(SAMPLE, None),
            P(SAMPLE, None),
            P(SAMPLE, None),
            P(SAMPLE, None),
        ),
        check_vma=False,
    )
```

```python
import functools

import jax
import jax.numpy as jnp
from jax import lax
from jax.experimental import pallas as pl
from jax.experimental.pallas import tpu as pltpu
from jax.sharding import Mesh
from jax.sharding import PartitionSpec as P

RATE = 12
STRIP = ("strip_0", "strip_1")
SAMPLE = ("sample_0", "sample_1")
EPSILON = 1e-05
MESH_ID = pl.DeviceIdType.MESH
F32 = jnp.float32
BF16 = jnp.bfloat16

CHANS = 2048
FEAT = 256
HALF = 128
ROWS = 3
COLS = 108
PITCH = 112
BLOCK = ROWS * PITCH
SPOTS = 2 * BLOCK
TAPS = 10
WIDE = TAPS * HALF
WIDER = WIDE + HALF
SHARD = 128
SAMPLE_AREA = 48.0 * 108.0
TOTAL_AREA = 16.0 * SAMPLE_AREA
FACTOR = 1.0 / 16.0


def places():
    return tuple(lax.axis_index(a) for a in STRIP + SAMPLE)


def z_peer(z, k):
    return {"strip_0": lax.rem(z + k + 8, 8)}


def other_core(c):
    return {"strip_1": 1 - c}


def along(axis, y, x, d):
    if axis == "x":
        return {"sample_1": lax.rem(x + d + 4, 4)}
    return {"sample_0": lax.rem(y + d + 4, 4)}


def sample_peer(me, k):
    other = lax.rem(me + k, 16)
    return {"sample_0": lax.div(other, 4), "sample_1": lax.rem(other, 4)}


def strip_peer(me, k):
    other = lax.rem(me + k, 16)
    return {"strip_0": lax.div(other, 2), "strip_1": lax.rem(other, 2)}


def greet(peers):
    barrier = pltpu.get_barrier_semaphore()
    for peer in peers:
        pl.semaphore_signal(barrier, inc=1, device_id=peer, device_id_type=MESH_ID)
    pl.semaphore_wait(barrier, len(peers))


def push(src, dst, send, recv, peer):
    copy = pltpu.make_async_remote_copy(
        src_ref=src,
        dst_ref=dst,
        send_sem=send,
        recv_sem=recv,
        device_id=peer,
        device_id_type=MESH_ID,
    )
    copy.start()
    return copy


def spot_column(shape):
    full = lax.broadcasted_iota(jnp.int32, (shape[0] // PITCH, PITCH, shape[1]), 1)
    return full.reshape(shape)


def moved(values, offset, column):
    if offset == 0:
        return values
    spots = values.shape[0]
    if offset > 0:
        return jnp.where(column < COLS - offset, pltpu.roll(values, spots - offset, 0), 0.0)
    inside = (column >= -offset) & (column < COLS)
    return jnp.where(inside, pltpu.roll(values, -offset, 0), 0.0)


def ring_gather(full, y, x, send, recv):
    count = [0]
    sent = []

    def put(kind, a, b, part, first, d):
        if kind == 0:
            row = lax.rem(y + b + 4, 4) * 4 + lax.rem(x + a + 4, 4)
            axis = "x" if first else "y"
        else:
            row = lax.rem(y + a + 4, 4) * 4 + lax.rem(x + b + 4, 4)
            axis = "y" if first else "x"
        start, size = ((0, 64), (0, 32), (32, 32))[part]
        rows = pl.ds(pl.multiple_of(row * SHARD + kind * 64 + start, 32), size)
        k = count[0]
        count[0] += 1
        copy = push(full.at[rows, :], full.at[rows, :], send.at[k], recv.at[k], along(axis, y, x, d))
        sent.append(copy)
        return copy

    kinds = (0, 1)
    right, left, up, down = {}, {}, {}, {}
    fr, fl, fu, fd = {}, {}, {}, {}

    def spread(kind, a):
        up[kind, a] = put(kind, a, 0, 0, False, 1)
        down[kind, a] = put(kind, a, 0, 0, False, -1)

    def relay(kind, a):
        up[kind, a].wait_recv()
        fu[kind, a] = put(kind, a, -1, 1, False, 1)
        down[kind, a].wait_recv()
        fd[kind, a] = put(kind, a, 1, 2, False, -1)

    for kind in kinds:
        right[kind] = put(kind, 0, 0, 0, True, 1)
        left[kind] = put(kind, 0, 0, 0, True, -1)
    for kind in kinds:
        spread(kind, 0)
    for kind in kinds:
        right[kind].wait_recv()
        fr[kind] = put(kind, -1, 0, 1, True, 1)
        left[kind].wait_recv()
        fl[kind] = put(kind, 1, 0, 2, True, -1)
    for kind in kinds:
        spread(kind, -1)
        spread(kind, 1)
    for kind in kinds:
        relay(kind, 0)
    for kind in kinds:
        fr[kind].wait_recv()
        fl[kind].wait_recv()
        spread(kind, 2)
    for a in (-1, 1, 2):
        for kind in kinds:
            relay(kind, a)
    for a in (0, -1, 1, 2):
        for kind in kinds:
            fu[kind, a].wait_recv()
            fd[kind, a].wait_recv()
    return sent


def forward_kernel(
    images, w_point, w_atrous, w_image, w_proj,
    spots_ref, full_ref, proj_ref, point_ref, centre_ref, outer_ref, pooled_ref, image_ref,
    taps, pool_src, pool_slots,
    local, core_send, core_recv, ring_send, ring_recv, proj_send, proj_recv, pool_send, pool_recv,
):
    z, c, y, x = places()
    sample = y * 4 + x
    mine = pl.multiple_of(c * BLOCK, 16)
    spots_ref[pl.ds(mine, BLOCK), :] = jnp.zeros((BLOCK, CHANS), BF16)

    lane = pl.multiple_of(c * HALF, HALF)
    shard = pl.ds(pl.multiple_of(sample * SHARD, SHARD), SHARD)
    loads = [pltpu.make_async_copy(w_point.at[:, pl.ds(lane, HALF)], full_ref.at[shard, pl.ds(0, HALF)], local.at[0])]
    for t in range(9):
        loads.append(
            pltpu.make_async_copy(
                w_atrous.at[:, pl.ds(pl.multiple_of(t * FEAT + lane, HALF), HALF)],
                full_ref.at[shard, pl.ds((t + 1) * HALF, HALF)],
                local.at[t + 1],
            )
        )
    loads.append(
        pltpu.make_async_copy(w_image.at[:, pl.ds(lane, HALF)], full_ref.at[shard, pl.ds(WIDE, HALF)], local.at[10])
    )
    loads.append(pltpu.make_async_copy(w_proj, proj_ref.at[sample], local.at[11]))
    for load in loads:
        load.start()
    for r in range(ROWS):
        spots_ref[pl.ds(pl.multiple_of(mine + r * PITCH, 16), COLS), :] = images[r]
    greet(
        [along("x", y, x, 1), along("x", y, x, -1), along("y", y, x, 1), along("y", y, x, -1), other_core(c)]
        + [z_peer(z, k) for k in range(1, 8)]
        + [sample_peer(sample, k) for k in range(1, 16) ]
    )
    for load in loads:
        load.wait()
    to_core = push(
        spots_ref.at[pl.ds(mine, BLOCK), :], spots_ref.at[pl.ds(mine, BLOCK), :],
        core_send.at[0], core_recv.at[0], other_core(c),
    )
    sent = [
        push(proj_ref.at[sample], proj_ref.at[sample], proj_send.at[k - 1], proj_recv.at[k - 1], sample_peer(sample, k))
        for k in range(1, 16)
    ]
    received = list(sent)
    sent += ring_gather(full_ref, y, x, ring_send, ring_recv)
    to_core.wait()

    def add_rows(i, total):
        return total + spots_ref[pl.ds(pl.multiple_of(i * 16, 16), 16), :].astype(F32)

    sums = lax.fori_loop(0, SPOTS // 16, add_rows, jnp.zeros((16, CHANS), F32))
    pool_src[...] = jnp.sum(sums, axis=0, keepdims=True)
    pools = [
        push(pool_src, pool_slots.at[z], pool_send.at[k - 1], pool_recv.at[k - 1], z_peer(z, k)) for k in range(1, 8)
    ]
    pool_slots[z] = pool_src[...]

    def multiply(n, carry):
        product = jnp.dot(
            spots_ref[...],
            full_ref[:, pl.ds(pl.multiple_of(n * FEAT, FEAT), FEAT)],
            preferred_element_type=F32,
        )
        taps[2 * n] = product[:, :HALF]
        taps[2 * n + 1] = product[:, HALF:]
        return carry

    lax.fori_loop(0, TAPS // 2, multiply, 0)
    column = spot_column((SPOTS, HALF))
    point_ref[...] = taps[0]

    def row_tap(r):
        first = 1 + 3 * (r + 1)
        return taps[first + 1] + moved(taps[first], -RATE, column) + moved(taps[first + 2], RATE, column)

    centre_ref[...] = row_tap(0)
    outer_ref[0] = row_tap(-1).astype(BF16)
    outer_ref[1] = row_tap(1).astype(BF16)
    for copy in pools:
        copy.wait()
    pooled = (jnp.sum(pool_slots[...], axis=0) / SAMPLE_AREA).astype(BF16)
    pooled_ref[...] = pooled.astype(F32)
    image = jnp.dot(
        jnp.broadcast_to(pooled, (16, CHANS)), full_ref[:, pl.ds(WIDE, HALF)], preferred_element_type=F32
    )
    image_ref[...] = image[0:8]
    for copy in received:
        copy.wait_recv()
    for copy in sent:
        copy.wait_send()


def silu(v):
    return v * lax.logistic(v)


def silu_slope(v):
    s = lax.logistic(v)
    return s * (1.0 + v * (1.0 - s))


def middle_kernel(
    point_ref, centre_ref, outer_ref, image_ref, proj_ref, cotangent,
    result_ref, grad_point_ref, grad_atrous_ref, proj_part_ref, image_grad_ref,
    halo, cot, relu, result_send, result_half, mix, images, columns,
    ar_src, ar_mid, ar_z, ar_xy, cot_send, norm_p, norm_a,
    core_send, core_recv, halo_send, halo_recv, z_send, z_recv, xy_send, xy_recv,
):
    z, c, y, x = places()
    sample = y * 4 + x
    mine = pl.multiple_of(c * BLOCK, 16)
    theirs = pl.multiple_of((1 - c) * BLOCK, 16)
    lane = pl.multiple_of(c * HALF, HALF)
    other_lane = pl.multiple_of((1 - c) * HALF, HALF)
    mate = other_core(c)
    cot[pl.ds(mine, BLOCK), :] = jnp.zeros((BLOCK, HALF), BF16)
    cot_send[...] = jnp.zeros_like(cot_send)
    greet([mate] + [z_peer(z, k) for k in range(1, 8)] + [sample_peer(sample, k) for k in range(1, 16)])

    below = push(outer_ref.at[0], halo.at[0], halo_send.at[0], halo_recv.at[0], z_peer(z, 2))
    above = push(outer_ref.at[1], halo.at[1], halo_send.at[1], halo_recv.at[1], z_peer(z, -2))
    images[c] = image_ref[...]
    swap_image = push(image_ref, images.at[c], core_send.at[0], core_recv.at[0], mate)
    for r in range(ROWS):
        rows = pl.ds(r * PITCH, COLS)
        cot_send[rows, :] = cotangent[r, :, pl.ds(other_lane, HALF)]
        cot[pl.ds(pl.multiple_of(mine + r * PITCH, 16), COLS), :] = cotangent[r, :, pl.ds(lane, HALF)]
    swap_cot = push(cot_send, cot.at[pl.ds(mine, BLOCK), :], core_send.at[1], core_recv.at[1], mate)

    column = spot_column((SPOTS, HALF))
    inside = column < COLS

    def totals(i, rows):
        for k, row in enumerate(rows):
            ar_src[i, pl.ds(k, 1), :] = row
        copies = [
            push(ar_src.at[i], ar_z.at[i, z], z_send.at[i, k - 1], z_recv.at[i, k - 1], z_peer(z, k))
            for k in range(1, 8)
        ]
        ar_z[i, z] = ar_src[i]
        for copy in copies:
            copy.wait()
        whole = jnp.sum(ar_z[i], axis=0)
        ar_mid[i] = whole
        copies = [
            push(ar_mid.at[i], ar_xy.at[i, sample], xy_send.at[i, k - 1], xy_recv.at[i, k - 1], sample_peer(sample, k))
            for k in range(1, 16)
        ]
        ar_xy[i, sample] = whole
        for copy in copies:
            copy.wait()
        total = jnp.sum(ar_xy[i], axis=0)
        return [whole[k : k + 1] for k in range(4)], [total[k : k + 1] for k in range(4)]

    def down(v):
        return jnp.sum(v, axis=0, keepdims=True)

    below.wait()
    above.wait()
    point = point_ref[...]
    zero = jnp.zeros((SPOTS, HALF), F32)
    atrous = (
        centre_ref[...]
        + jnp.where(z >= 2, halo[0].astype(F32), zero)
        + jnp.where(z < 6, halo[1].astype(F32), zero)
    )
    _, (s0, s1, s2, s3) = totals(0, [down(point), down(point * point), down(atrous), down(atrous * atrous)])

    def finish(total, power):
        centre = total / TOTAL_AREA
        return centre, lax.rsqrt(power / TOTAL_AREA - centre * centre + EPSILON)

    centre_p, scale_p = finish(s0, s1)
    centre_a, scale_a = finish(s2, s3)
    norm_p[...] = (point - centre_p) * scale_p
    norm_a[...] = (atrous - centre_a) * scale_a
    relu[c, :, pl.ds(0, HALF)] = jnp.where(inside, silu(norm_p[...]), 0.0).astype(BF16)
    relu[c, :, pl.ds(HALF, HALF)] = jnp.where(inside, silu(norm_a[...]), 0.0).astype(BF16)
    swap_relu = push(relu.at[c], relu.at[c], core_send.at[4], core_recv.at[4], mate)

    swap_image.wait()
    halves = [images[0][0:1], images[1][0:1]]

    def mean_of(pair):
        return (jnp.sum(pair[0]) + jnp.sum(pair[1])) * (1.0 / FEAT)

    image_mean = mean_of(halves)
    apart = [h - image_mean for h in halves]
    layer_scale = lax.rsqrt(jnp.full((1, HALF), mean_of([a * a for a in apart]) + EPSILON, F32))
    layer_norm = [a * layer_scale for a in apart]
    relu_image = jnp.concatenate([silu(v) for v in layer_norm], axis=1).astype(BF16)
    image_row = jnp.dot(
        jnp.broadcast_to(relu_image, (16, FEAT)),
        proj_ref[pl.ds(2 * FEAT, FEAT), pl.ds(lane, HALF)],
        preferred_element_type=F32,
    )[0:1]
    swap_relu.wait()

    mixed = jnp.zeros((SPOTS, HALF), F32) + image_row
    for k in range(2):
        for b in range(2):
            mixed = mixed + jnp.dot(
                relu[k, :, pl.ds(b * HALF, HALF)],
                proj_ref[pl.ds(b * FEAT + k * HALF, HALF), pl.ds(lane, HALF)],
                preferred_element_type=F32,
            )
    mixed = jnp.where(inside, mixed, 0.0)
    (mixed_sample, _, _, _), (s0, s1, _, _) = totals(1, [down(mixed), down(mixed * mixed), down(mixed[0:8]), down(mixed[0:8])])
    centre_m, scale_m = finish(s0, s1)
    norm_mix = (mixed - centre_m) * scale_m
    result = silu(norm_mix).astype(BF16)
    result_send[0] = result[:BLOCK]
    result_send[1] = result[BLOCK:]
    swap_result = push(result_send.at[1 - c], result_half, core_send.at[5], core_recv.at[5], mate)
    swap_cot.wait()
    upstream = jnp.where(inside, cot[...].astype(F32) * silu_slope(norm_mix), 0.0)
    (up_sample, _, _, _), (s0, s1, _, _) = totals(
        2, [down(upstream), down(upstream * norm_mix), down(mixed[0:8]), down(mixed[0:8])]
    )
    mean_u = s0 / TOTAL_AREA
    mean_un = s1 / TOTAL_AREA
    grad_mix = jnp.where(inside, (upstream - mean_u - norm_mix * mean_un) * scale_m, 0.0)
    mix[c] = grad_mix.astype(BF16)
    norm_sample = (mixed_sample - SAMPLE_AREA * centre_m) * scale_m
    column_total = (up_sample - SAMPLE_AREA * mean_u - mean_un * norm_sample) * scale_m
    columns[c] = jnp.broadcast_to(column_total, (8, HALF))
    swap_mix = push(mix.at[c], mix.at[c], core_send.at[6], core_recv.at[6], mate)
    swap_columns = push(columns.at[c], columns.at[c], core_send.at[7], core_recv.at[7], mate)
    swap_mix.wait()
    swap_columns.wait()

    def back(first):
        total = None
        for k in range(2):
            term = lax.dot_general(
                mix[k],
                proj_ref[pl.ds(pl.multiple_of(first + lane, HALF), HALF), pl.ds(k * HALF, HALF)],
                (((1,), (1,)), ((), ())),
                preferred_element_type=F32,
            )
            total = term if total is None else total + term
        return total

    norm_point = norm_p[...]
    norm_atrous = norm_a[...]
    up_point = back(0) * silu_slope(norm_point)
    up_atrous = back(FEAT) * silu_slope(norm_atrous)
    _, (s0, s1, s2, s3) = totals(
        3, [down(up_point), down(up_point * norm_point), down(up_atrous), down(up_atrous * norm_atrous)]
    )

    def back_norm(up, norm, first, second, scale):
        grad = (up - first / TOTAL_AREA - norm * (second / TOTAL_AREA)) * scale
        return jnp.where(inside, grad, 0.0).astype(BF16)

    grad_point_ref[...] = back_norm(up_point, norm_point, s0, s1, scale_p)
    grad_atrous_ref[...] = back_norm(up_atrous, norm_atrous, s2, s3, scale_a)

    column_b = jnp.concatenate([columns[0][0:1], columns[1][0:1]], axis=1).astype(BF16)
    back_image = lax.dot_general(
        jnp.broadcast_to(column_b, (16, FEAT)),
        proj_ref[pl.ds(2 * FEAT, FEAT), :],
        (((1,), (1,)), ((), ())),
        preferred_element_type=F32,
    )
    up_image = [back_image[0:1, k * HALF : (k + 1) * HALF] * silu_slope(layer_norm[k]) for k in range(2)]
    mean_up = mean_of(up_image)
    mean_up_norm = mean_of([up_image[k] * layer_norm[k] for k in range(2)])
    image_grad = jnp.concatenate(
        [(up_image[k] - mean_up - layer_norm[k] * mean_up_norm) * layer_scale for k in range(2)], axis=1
    )
    image_grad_ref[...] = jnp.broadcast_to(image_grad.astype(BF16).astype(F32), (8, FEAT))

    for k in range(2):
        part = lax.dot_general(
            relu[k], mix[c], (((0,), (0,)), ((), ())), preferred_element_type=F32
        ) * FACTOR
        proj_part_ref[pl.ds(k * HALF, HALF), :] = part[:HALF].astype(BF16)
        proj_part_ref[pl.ds(FEAT + k * HALF, HALF), :] = part[HALF:].astype(BF16)
    once = lax.broadcasted_iota(jnp.int32, (16, FEAT), 0) == 0
    gate = jnp.where(z == 0, FACTOR, 0.0).astype(F32)
    outer = lax.dot_general(
        jnp.where(once, jnp.broadcast_to(relu_image.astype(F32), (16, FEAT)), 0.0).astype(BF16),
        jnp.broadcast_to(columns[c][0:1], (16, HALF)).astype(BF16),
        (((0,), (0,)), ((), ())),
        preferred_element_type=F32,
    )
    proj_part_ref[pl.ds(2 * FEAT, FEAT), :] = (outer * gate).astype(BF16)

    swap_result.wait()
    own = result_send[c]
    came = result_half[...]
    for r in range(ROWS):
        rows = slice(r * PITCH, r * PITCH + COLS)
        result_ref[r, :, pl.ds(lane, HALF)] = own[rows]
        result_ref[r, :, pl.ds(other_lane, HALF)] = came[rows]


def backward_kernel(
    spots_ref, full_ref, pooled_ref, grad_point_ref, grad_atrous_ref, proj_part_ref, image_grad_ref,
    input_grad_ref, out_point_ref, out_atrous_ref, out_image_ref, out_proj_ref,
    halo, cols, partial, opposite, beside, pair, own, away, came,
    z_slots, z_sum, joined, proj_slots, proj_sum, proj_all, pool_rows, pool_all, image_all,
    halo_send, halo_recv, ring_send, ring_recv, core_send, core_recv,
    z_send, z_recv, all_send, all_recv, proj_send, proj_recv, spread_send, spread_recv,
    pool_send, pool_recv, image_send, image_recv,
):
    z, c, y, x = places()
    sample = y * 4 + x
    strip = z * 2 + c
    mate = other_core(c)
    greet([strip_peer(strip, k) for k in range(1, 16)] + [sample_peer(sample, k) for k in range(1, 16)])
    upper = push(grad_atrous_ref, halo.at[1], halo_send.at[1], halo_recv.at[1], z_peer(z, 2))
    lower = push(grad_atrous_ref, halo.at[0], halo_send.at[0], halo_recv.at[0], z_peer(z, -2))

    def to_samples(src_of, slots, send, recv):
        return [
            push(
                src_of(lax.rem(sample + k, 16)), slots.at[sample], send.at[k - 1], recv.at[k - 1],
                sample_peer(sample, k),
            )
            for k in range(1, 16)
        ]

    for k in range(16):
        pool_rows[k] = jnp.broadcast_to(pooled_ref[:, k * SHARD : (k + 1) * SHARD], (8, SHARD))
    sends = to_samples(lambda j: pool_rows.at[j], pool_all, pool_send, pool_recv)
    sends += to_samples(lambda j: image_grad_ref, image_all, image_send, image_recv)
    proj_copies = to_samples(lambda j: proj_part_ref.at[j], proj_slots, proj_send, proj_recv)
    pool_all[sample] = pool_rows[sample]
    image_all[sample] = image_grad_ref[...]
    proj_slots[sample] = proj_part_ref[sample]

    column = spot_column((SPOTS, HALF))
    cols[:, pl.ds(0, HALF)] = grad_point_ref[...]

    def fill(r, source):
        for s in (-1, 0, 1):
            t = 1 + 3 * (r + 1) + (s + 1)
            cols[:, pl.ds(t * HALF, HALF)] = moved(source, -RATE * s, column).astype(BF16)

    fill(0, grad_atrous_ref[...].astype(F32))
    zero = jnp.zeros((SPOTS, HALF), F32)
    upper.wait()
    lower.wait()
    fill(1, jnp.where(z >= 2, halo[1].astype(F32), zero))
    fill(-1, jnp.where(z < 6, halo[0].astype(F32), zero))

    def weight_part(k, carry):
        at = pl.ds(pl.multiple_of(k * FEAT, FEAT), FEAT)
        part = lax.dot_general(
            spots_ref[:, at], cols[...], (((0,), (0,)), ((), ())), preferred_element_type=F32
        )
        partial[at, :] = (part * FACTOR).astype(BF16)
        return carry

    lax.fori_loop(0, CHANS // FEAT, weight_part, 0)

    count = [0]
    done = []

    class Ring:
        def __init__(self, slot, axis, base, index):
            self.slot, self.axis, self.base, self.index = slot, axis, base, index

        def rows(self, o, start, size):
            return pl.ds(pl.multiple_of(self.index(o) * SHARD + self.base + start, 32), size)

        def put(self, src, dst, d):
            k = count[0]
            count[0] += 1
            copy = push(src, dst, ring_send.at[k], ring_recv.at[k], along(self.axis, y, x, d))
            done.append(copy)
            return copy

        def far(self):
            s = self.slot
            self.m0 = self.put(partial.at[self.rows(2, 0, 32), :], opposite.at[s, 0], 1)
            self.m1 = self.put(partial.at[self.rows(2, 32, 32), :], opposite.at[s, 1], -1)

        def near(self):
            s = self.slot
            self.m2 = self.put(partial.at[self.rows(1, 32, 32), :], beside.at[s, 0, pl.ds(32, 32), :], 1)
            self.m3 = self.put(partial.at[self.rows(-1, 0, 32), :], beside.at[s, 1, pl.ds(0, 32), :], -1)

        def relay(self):
            s = self.slot
            self.m0.wait_recv()
            at = self.rows(1, 0, 32)
            partial[at, :] = (partial[at, :].astype(F32) + opposite[s, 0].astype(F32)).astype(BF16)
            self.m4 = self.put(partial.at[at, :], beside.at[s, 0, pl.ds(0, 32), :], 1)
            self.m1.wait_recv()
            at = self.rows(-1, 32, 32)
            partial[at, :] = (partial[at, :].astype(F32) + opposite[s, 1].astype(F32)).astype(BF16)
            self.m5 = self.put(partial.at[at, :], beside.at[s, 1, pl.ds(32, 32), :], -1)

        def close(self):
            s = self.slot
            for m in (self.m2, self.m3, self.m4, self.m5):
                m.wait_recv()
            at = self.rows(0, 0, 64)
            partial[at, :] = (
                partial[at, :].astype(F32) + beside[s, 0].astype(F32) + beside[s, 1].astype(F32)
            ).astype(BF16)

    def block(dy, dx):
        return lax.rem(y + dy + 4, 4) * 4 + lax.rem(x + dx + 4, 4)

    order = (2, 1, -1, 0)
    rings = []
    for n, a in enumerate(order):
        rings.append(Ring(n, "y", 0, functools.partial(lambda a, o: block(o, a), a)))
        rings.append(Ring(4 + n, "x", 64, functools.partial(lambda a, o: block(a, o), a)))
    last = [
        Ring(8, "x", 0, lambda o: block(0, o)),
        Ring(9, "y", 64, lambda o: block(o, 0)),
    ]
    for ring in rings:
        ring.far()
    for ring in rings:
        ring.near()

    half_grad = image_grad_ref[:, pl.ds(pl.multiple_of(c * HALF, HALF), HALF)]
    grad_rows = jnp.concatenate([half_grad, half_grad], axis=0).astype(BF16)
    core_copies = []
    def input_part(k, carry):
        at = pl.ds(pl.multiple_of(k * FEAT, FEAT), FEAT)
        part = lax.dot_general(
            cols[...], full_ref[at, pl.ds(0, WIDE)], (((1,), (1,)), ((), ())), preferred_element_type=F32
        )
        pool = lax.dot_general(
            grad_rows, full_ref[at, pl.ds(WIDE, HALF)], (((1,), (1,)), ((), ())), preferred_element_type=F32
        )[0:1] / SAMPLE_AREA
        part = part + pool
        pair[0] = part[:BLOCK]
        pair[1] = part[BLOCK:]
        own[k] = pair[c]
        away[k] = pair[1 - c].astype(BF16)
        return carry

    lax.fori_loop(0, CHANS // FEAT, input_part, 0)
    swap = push(away, came, core_send.at[0], core_recv.at[0], mate)

    for ring in rings:
        ring.relay()
    for n in range(4):
        for ring in (rings[2 * n], rings[2 * n + 1]):
            ring.close()
        if n == 0:
            for ring in last:
                ring.far()
        if n == 2:
            for ring in last:
                ring.near()
    for ring in last:
        ring.relay()

    swap.wait()
    for k in range(CHANS // FEAT):
        total = (own[k] + came[k].astype(F32)).astype(BF16)
        for r in range(ROWS):
            input_grad_ref[r, :, pl.ds(k * FEAT, FEAT)] = total[r * PITCH : r * PITCH + COLS]

    for copy in sends:
        copy.wait()
    pools = pool_all[...][:, 0, :].astype(BF16)
    grads = image_all[...][:, 0, :].astype(BF16)
    out_image_ref[...] = (
        lax.dot_general(pools, grads, (((0,), (0,)), ((), ())), preferred_element_type=F32) * FACTOR
    )
    for copy in proj_copies:
        copy.wait()
    proj_sum[...] = jnp.sum(proj_slots[...].astype(F32), axis=0).astype(BF16)

    def to_strips(src, dst, send, recv):
        return [push(src, dst, send.at[k - 1], recv.at[k - 1], strip_peer(strip, k)) for k in range(1, 16)]

    spread = to_strips(proj_sum, proj_all.at[strip], spread_send, spread_recv)
    proj_all[strip] = proj_sum[...]

    for ring in last:
        ring.close()
    here = sample * SHARD
    z_copies = [
        push(
            partial.at[pl.ds(pl.multiple_of(here + lax.rem(z + k, 8) * 16, 16), 16), :],
            z_slots.at[z], z_send.at[k - 1], z_recv.at[k - 1], z_peer(z, k),
        )
        for k in range(1, 8)
    ]
    z_slots[z] = partial[pl.ds(pl.multiple_of(here + z * 16, 16), 16), :]
    for copy in z_copies:
        copy.wait()
    z_sum[...] = jnp.sum(z_slots[...].astype(F32), axis=0).astype(BF16)
    my_rows = pl.ds(pl.multiple_of(z * 16, 16), 16)
    all_copies = to_strips(z_sum, joined.at[c, my_rows, :], all_send, all_recv)
    joined[c, my_rows, :] = z_sum[...]
    for copy in spread:
        copy.wait()
    for k in range(2):
        total = proj_all[k].astype(F32)
        for level in range(1, 8):
            total = total + proj_all[2 * level + k].astype(F32)
        out_proj_ref[:, pl.ds(k * HALF, HALF)] = total
    for copy in all_copies:
        copy.wait()
    for k in range(2):
        out_point_ref[:, pl.ds(k * HALF, HALF)] = joined[k, :, pl.ds(0, HALF)].astype(F32)
        for t in range(9):
            out_atrous_ref[:, pl.ds(t * FEAT + k * HALF, HALF)] = joined[k, :, pl.ds((t + 1) * HALF, HALF)].astype(F32)
    for copy in done:
        copy.wait_send()


VMEM = pl.BlockSpec(memory_space=pltpu.VMEM)
ANY = pl.BlockSpec(memory_space=pl.ANY)


def dma(*shape):
    return pltpu.SemaphoreType.DMA(shape)


def sized(dtype, *shape):
    return jax.ShapeDtypeStruct(shape, dtype)


def params(call_id, mib):
    return pltpu.CompilerParams(collective_id=call_id, has_side_effects=True, vmem_limit_bytes=mib << 20)


def on_device(images, w_point, w_atrous, w_image, w_proj, cotangent):
    spots, full, proj, point, centre, outer, pooled, image = pl.pallas_call(
        forward_kernel,
        out_shape=[
            sized(BF16, SPOTS, CHANS),
            sized(BF16, CHANS, WIDER),
            sized(BF16, 16, 48, FEAT),
            sized(F32, SPOTS, HALF),
            sized(F32, SPOTS, HALF),
            sized(BF16, 2, SPOTS, HALF),
            sized(F32, 1, CHANS),
            sized(F32, 8, HALF),
        ],
        in_specs=[VMEM] + [ANY] * 4,
        out_specs=[VMEM] * 8,
        scratch_shapes=[
            pltpu.VMEM((TAPS, SPOTS, HALF), F32),
            pltpu.VMEM((1, CHANS), F32),
            pltpu.VMEM((8, 1, CHANS), F32),
            dma(15), dma(1), dma(1), dma(40), dma(40), dma(15), dma(15), dma(7), dma(7),
        ],
        compiler_params=params(0, 48),
        name="forward_gather",
    )(images[0], w_point, w_atrous, w_image, w_proj)

    result, grad_point, grad_atrous, proj_part, image_grad = pl.pallas_call(
        middle_kernel,
        out_shape=[
            sized(BF16, ROWS, COLS, FEAT),
            sized(BF16, SPOTS, HALF),
            sized(BF16, SPOTS, HALF),
            sized(BF16, 3 * FEAT, HALF),
            sized(F32, 8, FEAT),
        ],
        in_specs=[VMEM] * 6,
        out_specs=[VMEM] * 5,
        scratch_shapes=[
            pltpu.VMEM((2, SPOTS, HALF), BF16),
            pltpu.VMEM((SPOTS, HALF), BF16),
            pltpu.VMEM((2, SPOTS, FEAT), BF16),
            pltpu.VMEM((2, BLOCK, HALF), BF16),
            pltpu.VMEM((BLOCK, HALF), BF16),
            pltpu.VMEM((2, SPOTS, HALF), BF16),
            pltpu.VMEM((2, 8, HALF), F32),
            pltpu.VMEM((2, 8, HALF), F32),
            pltpu.VMEM((4, 4, HALF), F32),
            pltpu.VMEM((4, 4, HALF), F32),
            pltpu.VMEM((4, 8, 4, HALF), F32),
            pltpu.VMEM((4, 16, 4, HALF), F32),
            pltpu.VMEM((BLOCK, HALF), BF16),
            pltpu.VMEM((SPOTS, HALF), F32),
            pltpu.VMEM((SPOTS, HALF), F32),
            dma(8), dma(8), dma(2), dma(2), dma(4, 7), dma(4, 7), dma(4, 15), dma(4, 15),
        ],
        compiler_params=params(1, 32),
        name="middle",
    )(point, centre, outer, image, proj.reshape(3 * FEAT, FEAT), cotangent[0])

    input_grad, g_point, g_atrous, g_image, g_proj = pl.pallas_call(
        backward_kernel,
        out_shape=[
            sized(BF16, ROWS, COLS, CHANS),
            sized(F32, SHARD, FEAT),
            sized(F32, SHARD, 9 * FEAT),
            sized(F32, SHARD, FEAT),
            sized(F32, 48, FEAT),
        ],
        in_specs=[VMEM] * 7,
        out_specs=[VMEM] * 5,
        scratch_shapes=[
            pltpu.VMEM((2, SPOTS, HALF), BF16),
            pltpu.VMEM((SPOTS, WIDE), BF16),
            pltpu.VMEM((CHANS, WIDE), BF16),
            pltpu.VMEM((10, 2, 32, WIDE), BF16),
            pltpu.VMEM((10, 2, 64, WIDE), BF16),
            pltpu.VMEM((2, BLOCK, FEAT), F32),
            pltpu.VMEM((8, BLOCK, FEAT), F32),
            pltpu.VMEM((8, BLOCK, FEAT), BF16),
            pltpu.VMEM((8, BLOCK, FEAT), BF16),
            pltpu.VMEM((8, 16, WIDE), BF16),
            pltpu.VMEM((16, WIDE), BF16),
            pltpu.VMEM((2, SHARD, WIDE), BF16),
            pltpu.VMEM((16, 48, HALF), BF16),
            pltpu.VMEM((48, HALF), BF16),
            pltpu.VMEM((16, 48, HALF), BF16),
            pltpu.VMEM((16, 8, SHARD), F32),
            pltpu.VMEM((16, 8, SHARD), F32),
            pltpu.VMEM((16, 8, FEAT), F32),
            dma(2), dma(2), dma(60), dma(60), dma(1), dma(1), dma(7), dma(7), dma(15), dma(15),
            dma(15), dma(15), dma(15), dma(15), dma(15), dma(15), dma(15), dma(15),
        ],
        compiler_params=params(2, 56),
        name="backward_reduce",
    )(spots, full, pooled, grad_point, grad_atrous, proj_part.reshape(16, 48, HALF), image_grad)
    return (result[None], input_grad[None], g_point, g_atrous, g_image, g_proj)


def solution(mesh):
    finer = Mesh(mesh.devices.reshape(8, 2, 4, 4), STRIP + SAMPLE)
    placed = (
        P(SAMPLE, STRIP, None, None),
        P(SAMPLE, None),
        P(SAMPLE, None),
        P(SAMPLE, None),
        P(SAMPLE, None),
        P(SAMPLE, STRIP, None, None),
    )
    return jax.shard_map(
        on_device,
        mesh=finer,
        in_specs=placed,
        out_specs=(
            P(SAMPLE, STRIP, None, None),
            P(SAMPLE, STRIP, None, None),
            P(SAMPLE, None),
            P(SAMPLE, None),
            P(SAMPLE, None),
            P(SAMPLE, None),
        ),
        check_vma=False,
    )
```

```python
import functools
import types

import jax
import jax.numpy as jnp
from jax import lax
from jax.experimental import pallas as pl
from jax.experimental.pallas import tpu as pltpu
from jax.sharding import Mesh
from jax.sharding import PartitionSpec as P

RATE = 12
STRIP = ("strip_0", "strip_1")
SAMPLE = ("sample_0", "sample_1")
EPSILON = 1e-05
MESH_ID = pl.DeviceIdType.MESH
F32 = jnp.float32
BF16 = jnp.bfloat16

CHANS = 2048
FEAT = 256
HALF = 128
ROWS = 3
COLS = 108
PITCH = 112
BLOCK = ROWS * PITCH
SPOTS = 2 * BLOCK
TAPS = 10
WIDE = TAPS * HALF
WIDER = WIDE + HALF
SHARD = 128
SAMPLE_AREA = 48.0 * 108.0
TOTAL_AREA = 16.0 * SAMPLE_AREA
FACTOR = 1.0 / 16.0


def places():
    return tuple(lax.axis_index(a) for a in STRIP + SAMPLE)


def z_peer(z, k):
    return {"strip_0": lax.rem(z + k + 8, 8)}


def other_core(c):
    return {"strip_1": 1 - c}


def along(axis, y, x, d):
    if axis == "x":
        return {"sample_1": lax.rem(x + d + 4, 4)}
    return {"sample_0": lax.rem(y + d + 4, 4)}


def sample_peer(me, k):
    other = lax.rem(me + k, 16)
    return {"sample_0": lax.div(other, 4), "sample_1": lax.rem(other, 4)}


def strip_peer(me, k):
    other = lax.rem(me + k, 16)
    return {"strip_0": lax.div(other, 2), "strip_1": lax.rem(other, 2)}


def greet(peers):
    barrier = pltpu.get_barrier_semaphore()
    for peer in peers:
        pl.semaphore_signal(barrier, inc=1, device_id=peer, device_id_type=MESH_ID)
    pl.semaphore_wait(barrier, len(peers))


def push(src, dst, send, recv, peer):
    copy = pltpu.make_async_remote_copy(
        src_ref=src,
        dst_ref=dst,
        send_sem=send,
        recv_sem=recv,
        device_id=peer,
        device_id_type=MESH_ID,
    )
    copy.start()
    return copy


def spot_column(shape):
    full = lax.broadcasted_iota(jnp.int32, (shape[0] // PITCH, PITCH, shape[1]), 1)
    return full.reshape(shape)


def moved(values, offset, column):
    if offset == 0:
        return values
    spots = values.shape[0]
    if offset > 0:
        return jnp.where(column < COLS - offset, pltpu.roll(values, spots - offset, 0), 0.0)
    inside = (column >= -offset) & (column < COLS)
    return jnp.where(inside, pltpu.roll(values, -offset, 0), 0.0)


def ring_gather(full, y, x, send, recv, early, late):
    count = [0]
    sent = []

    def put(kind, a, b, part, first, d):
        if kind == 0:
            row = lax.rem(y + b + 4, 4) * 4 + lax.rem(x + a + 4, 4)
            axis = "x" if first else "y"
        else:
            row = lax.rem(y + a + 4, 4) * 4 + lax.rem(x + b + 4, 4)
            axis = "y" if first else "x"
        start, size = ((0, 64), (0, 32), (32, 32))[part]
        rows = pl.ds(pl.multiple_of(row * SHARD + kind * 64 + start, 32), size)
        k = count[0]
        count[0] += 1
        copy = push(full.at[rows, :], full.at[rows, :], send.at[k], recv.at[k], along(axis, y, x, d))
        sent.append(copy)
        return copy

    kinds = (0, 1)
    right, left, up, down = {}, {}, {}, {}
    fr, fl, fu, fd = {}, {}, {}, {}

    def spread(kind, a):
        up[kind, a] = put(kind, a, 0, 0, False, 1)
        down[kind, a] = put(kind, a, 0, 0, False, -1)

    def relay(kind, a):
        up[kind, a].wait_recv()
        fu[kind, a] = put(kind, a, -1, 1, False, 1)
        down[kind, a].wait_recv()
        fd[kind, a] = put(kind, a, 1, 2, False, -1)

    for kind in kinds:
        right[kind] = put(kind, 0, 0, 0, True, 1)
        left[kind] = put(kind, 0, 0, 0, True, -1)
    for kind in kinds:
        spread(kind, 0)
    early()
    for kind in kinds:
        right[kind].wait_recv()
        fr[kind] = put(kind, -1, 0, 1, True, 1)
        left[kind].wait_recv()
        fl[kind] = put(kind, 1, 0, 2, True, -1)
    for kind in kinds:
        spread(kind, -1)
        spread(kind, 1)
    for kind in kinds:
        relay(kind, 0)
    late()
    for kind in kinds:
        fr[kind].wait_recv()
        fl[kind].wait_recv()
        spread(kind, 2)
    for a in (-1, 1, 2):
        for kind in kinds:
            relay(kind, a)
    for a in (0, -1, 1, 2):
        for kind in kinds:
            fu[kind, a].wait_recv()
            fd[kind, a].wait_recv()
    return sent


def silu(v):
    return v * lax.logistic(v)


def silu_slope(v):
    s = lax.logistic(v)
    return s * (1.0 + v * (1.0 - s))


def whole_kernel(names, *refs):
    v = types.SimpleNamespace(**dict(zip(names, refs)))
    z, c, y, x = places()
    sample = y * 4 + x
    strip = z * 2 + c
    mate = other_core(c)
    mine = pl.multiple_of(c * BLOCK, 16)
    lane = pl.multiple_of(c * HALF, HALF)
    other_lane = pl.multiple_of((1 - c) * HALF, HALF)
    column = spot_column((SPOTS, HALF))
    inside = column < COLS
    zero = jnp.zeros((SPOTS, HALF), F32)

    def swap(src, dst, k):
        return push(src, dst, v.core_send.at[k], v.core_recv.at[k], mate)

    full, spots, proj = v.full, v.spots, v.proj
    shard = pl.ds(pl.multiple_of(sample * SHARD, SHARD), SHARD)
    loads = [pltpu.make_async_copy(v.w_point.at[:, pl.ds(lane, HALF)], full.at[shard, pl.ds(0, HALF)], v.local.at[0])]
    for t in range(9):
        loads.append(
            pltpu.make_async_copy(
                v.w_atrous.at[:, pl.ds(pl.multiple_of(t * FEAT + lane, HALF), HALF)],
                full.at[shard, pl.ds((t + 1) * HALF, HALF)],
                v.local.at[t + 1],
            )
        )
    loads.append(
        pltpu.make_async_copy(v.w_image.at[:, pl.ds(lane, HALF)], full.at[shard, pl.ds(WIDE, HALF)], v.local.at[10])
    )
    own_rows = pl.ds(pl.multiple_of(sample * 48, 16), 48)
    loads.append(pltpu.make_async_copy(v.w_proj, proj.at[own_rows, :], v.local.at[11]))
    inputs = [
        pltpu.make_async_copy(v.images, v.stage, v.local.at[12]),
        pltpu.make_async_copy(v.cotangent, v.cot_stage, v.local.at[13]),
    ]
    for load in loads + inputs:
        load.start()
    spots[pl.ds(mine, BLOCK), :] = jnp.zeros((BLOCK, CHANS), BF16)
    v.cot[pl.ds(mine, BLOCK), :] = jnp.zeros((BLOCK, HALF), BF16)
    v.cot_send[...] = jnp.zeros_like(v.cot_send)
    greet([strip_peer(strip, k) for k in range(1, 16)] + [sample_peer(sample, k) for k in range(1, 16)])
    for load in loads:
        load.wait()

    later = []

    def early():
        for load in inputs:
            load.wait()
        for r in range(ROWS):
            spots[pl.ds(pl.multiple_of(mine + r * PITCH, 16), COLS), :] = v.stage[r]
        later.append(swap(spots.at[pl.ds(mine, BLOCK), :], spots.at[pl.ds(mine, BLOCK), :], 0))
        for r in range(ROWS):
            v.cot_send[pl.ds(r * PITCH, COLS), :] = v.cot_stage[r, :, pl.ds(other_lane, HALF)]
            v.cot[pl.ds(pl.multiple_of(mine + r * PITCH, 16), COLS), :] = v.cot_stage[r, :, pl.ds(lane, HALF)]
        later.append(swap(v.cot_send, v.cot.at[pl.ds(mine, BLOCK), :], 1))
        later.extend(
            push(
                proj.at[own_rows, :], proj.at[own_rows, :], v.proj_send.at[k - 1], v.proj_recv.at[k - 1],
                sample_peer(sample, k),
            )
            for k in range(1, 16)
        )

    pools = []

    def late():
        later[0].wait_recv()

        def add_rows(i, total):
            return total + spots[pl.ds(pl.multiple_of(i * 16, 16), 16), :].astype(F32)

        sums = lax.fori_loop(0, SPOTS // 16, add_rows, jnp.zeros((16, CHANS), F32))
        v.pool_src[...] = jnp.sum(sums, axis=0, keepdims=True)
        pools.extend(
            push(v.pool_src, v.pool_slots.at[z], v.pool_send.at[k - 1], v.pool_recv.at[k - 1], z_peer(z, k))
            for k in range(1, 8)
        )
        v.pool_slots[z] = v.pool_src[...]

    ring_sent = ring_gather(full, y, x, v.gather_send, v.gather_recv, early, late)

    def multiply(n, carry):
        product = jnp.dot(
            spots[...], full[:, pl.ds(pl.multiple_of(n * FEAT, FEAT), FEAT)], preferred_element_type=F32
        )
        v.taps[2 * n] = product[:, :HALF]
        v.taps[2 * n + 1] = product[:, HALF:]
        return carry

    lax.fori_loop(0, TAPS // 2, multiply, 0)

    def row_tap(r):
        first = 1 + 3 * (r + 1)
        return v.taps[first + 1] + moved(v.taps[first], -RATE, column) + moved(v.taps[first + 2], RATE, column)

    v.outer[0] = row_tap(-1).astype(BF16)
    below = push(v.outer.at[0], v.halo.at[0], v.halo_send.at[0], v.halo_recv.at[0], z_peer(z, 2))
    v.outer[1] = row_tap(1).astype(BF16)
    above = push(v.outer.at[1], v.halo.at[1], v.halo_send.at[1], v.halo_recv.at[1], z_peer(z, -2))
    v.centre[...] = row_tap(0)
    for copy in pools:
        copy.wait()
    pooled = (jnp.sum(v.pool_slots[...], axis=0) / SAMPLE_AREA).astype(BF16)
    image = jnp.dot(
        jnp.broadcast_to(pooled, (16, CHANS)), full[:, pl.ds(WIDE, HALF)], preferred_element_type=F32
    )
    v.images_half[c] = image[0:8]
    later.append(swap(v.images_half.at[c], v.images_half.at[c], 2))

    def to_samples(src_of, slots, send, recv):
        return [
            push(
                src_of(lax.rem(sample + k, 16)), slots.at[sample], send.at[k - 1], recv.at[k - 1],
                sample_peer(sample, k),
            )
            for k in range(1, 16)
        ]

    for k in range(16):
        v.pool_rows[k] = jnp.broadcast_to(pooled[:, k * SHARD : (k + 1) * SHARD].astype(F32), (8, SHARD))

    def totals(i, rows, meanwhile):
        for k, row in enumerate(rows):
            v.ar_src[i, pl.ds(k, 1), :] = row
        copies = [
            push(v.ar_src.at[i], v.ar_z.at[i, z], v.z_send.at[i, k - 1], v.z_recv.at[i, k - 1], z_peer(z, k))
            for k in range(1, 8)
        ]
        v.ar_z[i, z] = v.ar_src[i]
        meanwhile[0]()
        for copy in copies:
            copy.wait()
        whole = jnp.sum(v.ar_z[i], axis=0)
        v.ar_mid[i] = whole
        copies = [
            push(
                v.ar_mid.at[i], v.ar_xy.at[i, sample], v.xy_send.at[i, k - 1], v.xy_recv.at[i, k - 1],
                sample_peer(sample, k),
            )
            for k in range(1, 16)
        ]
        v.ar_xy[i, sample] = whole
        meanwhile[1]()
        for copy in copies:
            copy.wait()
        total = jnp.sum(v.ar_xy[i], axis=0)
        return [whole[k : k + 1] for k in range(4)], [total[k : k + 1] for k in range(4)]

    def down(a):
        return jnp.sum(a, axis=0, keepdims=True)

    def finish(total, power):
        centre = total / TOTAL_AREA
        return centre, lax.rsqrt(power / TOTAL_AREA - centre * centre + EPSILON)

    def mean_of(both):
        return (jnp.sum(both[0]) + jnp.sum(both[1])) * (1.0 / FEAT)

    nothing = lambda: None
    below.wait()
    above.wait()
    point = v.taps[0]
    atrous = (
        v.centre[...]
        + jnp.where(z >= 2, v.halo[0].astype(F32), zero)
        + jnp.where(z < 6, v.halo[1].astype(F32), zero)
    )
    v.centre[...] = atrous
    keep = types.SimpleNamespace()

    def send_pools():
        keep.pools = to_samples(lambda j: v.pool_rows.at[j], v.pool_all, v.pall_send, v.pall_recv)
        v.pool_all[sample] = v.pool_rows[sample]

    def image_forward():
        later[-1].wait_recv()
        halves = [v.images_half[0][0:1], v.images_half[1][0:1]]
        image_mean = mean_of(halves)
        apart = [h - image_mean for h in halves]
        keep.layer_scale = lax.rsqrt(jnp.full((1, HALF), mean_of([a * a for a in apart]) + EPSILON, F32))
        keep.layer_norm = [a * keep.layer_scale for a in apart]
        keep.relu_image = jnp.concatenate([silu(a) for a in keep.layer_norm], axis=1).astype(BF16)
        for copy in later[2:17]:
            copy.wait_recv()
        keep.image_row = jnp.dot(
            jnp.broadcast_to(keep.relu_image, (16, FEAT)),
            proj[pl.ds(2 * FEAT, FEAT), pl.ds(lane, HALF)],
            preferred_element_type=F32,
        )[0:1]

    _, (s0, s1, s2, s3) = totals(
        0, [down(point), down(point * point), down(atrous), down(atrous * atrous)], (send_pools, image_forward)
    )
    centre_p, scale_p = finish(s0, s1)
    centre_a, scale_a = finish(s2, s3)
    v.norm_p[...] = (point - centre_p) * scale_p
    v.norm_a[...] = (v.centre[...] - centre_a) * scale_a
    relu = v.relu
    relu[c, :, pl.ds(0, HALF)] = jnp.where(inside, silu(v.norm_p[...]), 0.0).astype(BF16)
    relu[c, :, pl.ds(HALF, HALF)] = jnp.where(inside, silu(v.norm_a[...]), 0.0).astype(BF16)
    swap_relu = swap(relu.at[c], relu.at[c], 3)

    def mix_term(k):
        total = None
        for b in range(2):
            first = pl.multiple_of(k * HALF + b * FEAT, HALF)
            term = jnp.dot(
                relu[k, :, pl.ds(b * HALF, HALF)],
                proj[pl.ds(first, HALF), pl.ds(lane, HALF)],
                preferred_element_type=F32,
            )
            total = term if total is None else total + term
        return total

    mixed = mix_term(c) + keep.image_row
    swap_relu.wait()
    mixed = jnp.where(inside, mixed + mix_term(1 - c), 0.0)
    v.mixed[...] = mixed

    def slope_point():
        v.slope_p[...] = silu_slope(v.norm_p[...])

    def slope_atrous():
        v.slope_a[...] = silu_slope(v.norm_a[...])

    blank = jnp.zeros((1, HALF), F32)
    (mixed_sample, _, _, _), (s0, s1, _, _) = totals(
        1, [down(mixed), down(mixed * mixed), blank, blank], (slope_point, slope_atrous)
    )
    centre_m, scale_m = finish(s0, s1)
    norm_mix = (v.mixed[...] - centre_m) * scale_m
    v.mixed[...] = norm_mix
    later[1].wait_recv()
    sigma = lax.logistic(norm_mix)
    upstream = jnp.where(inside, v.cot[...].astype(F32) * (sigma * (1.0 + norm_mix * (1.0 - sigma))), 0.0)
    v.upstream[...] = upstream

    def make_result():
        result = silu(v.mixed[...]).astype(BF16)
        v.result_send[0] = result[:BLOCK]
        v.result_send[1] = result[BLOCK:]
        keep.result = swap(v.result_send.at[1 - c], v.result_half, 4)

    def store_result():
        keep.result.wait_recv()
        for r in range(ROWS):
            rows = pl.ds(r * PITCH, COLS)
            v.out_result[r, :, pl.ds(lane, HALF)] = v.result_send[c, rows, :]
            v.out_result[r, :, pl.ds(other_lane, HALF)] = v.result_half[rows, :]

    (up_sample, _, _, _), (s0, s1, _, _) = totals(
        2, [down(upstream), down(upstream * norm_mix), blank, blank], (make_result, store_result)
    )
    mean_u = s0 / TOTAL_AREA
    mean_un = s1 / TOTAL_AREA
    grad_mix = jnp.where(inside, (v.upstream[...] - mean_u - v.mixed[...] * mean_un) * scale_m, 0.0)
    mix, columns = v.mix, v.columns
    mix[c] = grad_mix.astype(BF16)
    swap_mix = swap(mix.at[c], mix.at[c], 5)
    norm_sample = (mixed_sample - SAMPLE_AREA * centre_m) * scale_m
    column_total = (up_sample - SAMPLE_AREA * mean_u - mean_un * norm_sample) * scale_m
    columns[c] = jnp.broadcast_to(column_total, (8, HALF))
    swap_columns = swap(columns.at[c], columns.at[c], 6)

    def back_term(first, k):
        return lax.dot_general(
            mix[k],
            proj[pl.ds(pl.multiple_of(first + lane, HALF), HALF), pl.ds(pl.multiple_of(k * HALF, HALF), HALF)],
            (((1,), (1,)), ((), ())),
            preferred_element_type=F32,
        )

    back_p = back_term(0, c)
    back_a = back_term(FEAT, c)
    swap_mix.wait()
    up_point = (back_p + back_term(0, 1 - c)) * v.slope_p[...]
    up_atrous = (back_a + back_term(FEAT, 1 - c)) * v.slope_a[...]
    v.slope_p[...] = up_point
    v.slope_a[...] = up_atrous

    def image_backward():
        swap_columns.wait()
        column_b = jnp.concatenate([columns[0][0:1], columns[1][0:1]], axis=1).astype(BF16)
        back_image = lax.dot_general(
            jnp.broadcast_to(column_b, (16, FEAT)),
            proj[pl.ds(2 * FEAT, FEAT), :],
            (((1,), (1,)), ((), ())),
            preferred_element_type=F32,
        )
        layer_norm = keep.layer_norm
        up_image = [back_image[0:1, k * HALF : (k + 1) * HALF] * silu_slope(layer_norm[k]) for k in range(2)]
        mean_up = mean_of(up_image)
        mean_up_norm = mean_of([up_image[k] * layer_norm[k] for k in range(2)])
        image_grad = jnp.concatenate(
            [(up_image[k] - mean_up - layer_norm[k] * mean_up_norm) * keep.layer_scale for k in range(2)], axis=1
        )
        v.image_grad[...] = jnp.broadcast_to(image_grad.astype(BF16).astype(F32), (8, FEAT))
        keep.images = to_samples(lambda j: v.image_grad, v.image_all, v.image_send, v.image_recv)
        v.image_all[sample] = v.image_grad[...]

    def proj_gradient():
        for k in range(2):
            part = lax.dot_general(
                relu[k], mix[c], (((0,), (0,)), ((), ())), preferred_element_type=F32
            ) * FACTOR
            v.proj_part[pl.ds(k * HALF, HALF), :] = part[:HALF].astype(BF16)
            v.proj_part[pl.ds(FEAT + k * HALF, HALF), :] = part[HALF:].astype(BF16)
        once = lax.broadcasted_iota(jnp.int32, (16, FEAT), 0) == 0
        gate = jnp.where(z == 0, FACTOR, 0.0).astype(F32)
        outer = lax.dot_general(
            jnp.where(once, jnp.broadcast_to(keep.relu_image.astype(F32), (16, FEAT)), 0.0).astype(BF16),
            jnp.broadcast_to(columns[c][0:1], (16, HALF)).astype(BF16),
            (((0,), (0,)), ((), ())),
            preferred_element_type=F32,
        )
        v.proj_part[pl.ds(2 * FEAT, FEAT), :] = (outer * gate).astype(BF16)

    _, (s0, s1, s2, s3) = totals(
        3,
        [down(up_point), down(up_point * v.norm_p[...]), down(up_atrous), down(up_atrous * v.norm_a[...])],
        (image_backward, proj_gradient),
    )

    def back_norm(up, norm, first, second, scale):
        grad = (up - first / TOTAL_AREA - norm * (second / TOTAL_AREA)) * scale
        return jnp.where(inside, grad, 0.0)

    grad_atrous = back_norm(v.slope_a[...], v.norm_a[...], s2, s3, scale_a)
    v.grad_atrous[...] = grad_atrous.astype(BF16)
    upper = push(v.grad_atrous, v.back_halo.at[1], v.halo_send.at[2], v.halo_recv.at[2], z_peer(z, 2))
    lower = push(v.grad_atrous, v.back_halo.at[0], v.halo_send.at[3], v.halo_recv.at[3], z_peer(z, -2))
    proj_copies = [
        push(
            v.proj_part.at[pl.ds(pl.multiple_of(lax.rem(sample + k, 16) * 48, 16), 48), :], v.proj_slots.at[sample],
            v.pgrad_send.at[k - 1], v.pgrad_recv.at[k - 1], sample_peer(sample, k),
        )
        for k in range(1, 16)
    ]
    v.proj_slots[sample] = v.proj_part[own_rows, :]
    cols = v.cols
    cols[:, pl.ds(0, HALF)] = back_norm(v.slope_p[...], v.norm_p[...], s0, s1, scale_p).astype(BF16)

    def fill(r, source):
        for s in (-1, 0, 1):
            t = 1 + 3 * (r + 1) + (s + 1)
            cols[:, pl.ds(t * HALF, HALF)] = moved(source, -RATE * s, column).astype(BF16)

    fill(0, v.grad_atrous[...].astype(F32))
    upper.wait()
    fill(1, jnp.where(z >= 2, v.back_halo[1].astype(F32), zero))
    lower.wait()
    fill(-1, jnp.where(z < 6, v.back_halo[0].astype(F32), zero))

    partial, opposite, beside = v.partial, v.opposite, v.beside

    def weight_block(dy):
        base = lax.rem(y + dy + 4, 4) * 512

        def weight_part(k, carry):
            at = pl.ds(pl.multiple_of(base + k * FEAT, FEAT), FEAT)
            part = lax.dot_general(
                spots[:, at], cols[...], (((0,), (0,)), ((), ())), preferred_element_type=F32
            )
            partial[at, :] = (part * FACTOR).astype(BF16)
            return carry

        lax.fori_loop(0, 2, weight_part, 0)

    count = [0]
    done = []

    class Ring:
        def __init__(self, slot, axis, base, index):
            self.slot, self.axis, self.base, self.index = slot, axis, base, index

        def rows(self, o, start, size):
            return pl.ds(pl.multiple_of(self.index(o) * SHARD + self.base + start, 32), size)

        def put(self, src, dst, d):
            k = count[0]
            count[0] += 1
            copy = push(src, dst, v.ring_send.at[k], v.ring_recv.at[k], along(self.axis, y, x, d))
            done.append(copy)
            return copy

        def far(self):
            s = self.slot
            self.m0 = self.put(partial.at[self.rows(2, 0, 32), :], opposite.at[s, 0], 1)
            self.m1 = self.put(partial.at[self.rows(2, 32, 32), :], opposite.at[s, 1], -1)

        def near_up(self):
            self.m2 = self.put(partial.at[self.rows(1, 32, 32), :], beside.at[self.slot, 0, pl.ds(32, 32), :], 1)

        def near_down(self):
            self.m3 = self.put(partial.at[self.rows(-1, 0, 32), :], beside.at[self.slot, 1, pl.ds(0, 32), :], -1)

        def relay(self):
            s = self.slot
            self.m0.wait_recv()
            at = self.rows(1, 0, 32)
            partial[at, :] = (partial[at, :].astype(F32) + opposite[s, 0].astype(F32)).astype(BF16)
            self.m4 = self.put(partial.at[at, :], beside.at[s, 0, pl.ds(0, 32), :], 1)
            self.m1.wait_recv()
            at = self.rows(-1, 32, 32)
            partial[at, :] = (partial[at, :].astype(F32) + opposite[s, 1].astype(F32)).astype(BF16)
            self.m5 = self.put(partial.at[at, :], beside.at[s, 1, pl.ds(32, 32), :], -1)

        def close(self):
            s = self.slot
            for m in (self.m2, self.m3, self.m4, self.m5):
                m.wait_recv()
            at = self.rows(0, 0, 64)
            partial[at, :] = (
                partial[at, :].astype(F32) + beside[s, 0].astype(F32) + beside[s, 1].astype(F32)
            ).astype(BF16)

    def block(dy, dx):
        return lax.rem(y + dy + 4, 4) * 4 + lax.rem(x + dx + 4, 4)

    order = (2, 1, -1, 0)
    by_y = [Ring(n, "y", 0, functools.partial(lambda a, o: block(o, a), a)) for n, a in enumerate(order)]
    by_x = [Ring(4 + n, "x", 64, functools.partial(lambda a, o: block(a, o), a)) for n, a in enumerate(order)]
    last = [
        Ring(8, "x", 0, lambda o: block(0, o)),
        Ring(9, "y", 64, lambda o: block(o, 0)),
    ]
    for n, dy in enumerate(order):
        weight_block(dy)
        by_x[n].far()
        if dy == 2:
            for ring in by_y:
                ring.far()
        if dy == 1:
            for ring in by_y:
                ring.near_up()
        if dy == -1:
            for ring in by_y:
                ring.near_down()
        by_x[n].near_up()
        by_x[n].near_down()

    half_grad = v.image_grad[:, pl.ds(lane, HALF)]
    grad_rows = jnp.concatenate([half_grad, half_grad], axis=0).astype(BF16)

    def input_part(k, carry):
        at = pl.ds(pl.multiple_of(k * FEAT, FEAT), FEAT)
        part = lax.dot_general(
            cols[...], full[at, pl.ds(0, WIDE)], (((1,), (1,)), ((), ())), preferred_element_type=F32
        )
        pool = lax.dot_general(
            grad_rows, full[at, pl.ds(WIDE, HALF)], (((1,), (1,)), ((), ())), preferred_element_type=F32
        )[0:1] / SAMPLE_AREA
        part = part + pool
        v.pair[0] = part[:BLOCK]
        v.pair[1] = part[BLOCK:]
        v.own[k] = v.pair[c]
        v.away[k] = v.pair[1 - c].astype(BF16)
        return carry

    lax.fori_loop(0, 4, input_part, 0)
    for n in range(4):
        by_x[n].relay()
        by_y[n].relay()
    lax.fori_loop(4, 8, input_part, 0)
    swap_input = swap(v.away, v.came, 7)
    for n in range(4):
        by_y[n].close()
        by_x[n].close()
        if n == 0:
            for ring in last:
                ring.far()
        if n == 1:
            for ring in last:
                ring.near_up()
        if n == 2:
            for ring in last:
                ring.near_down()
    for ring in last:
        ring.relay()

    for copy in proj_copies:
        copy.wait()
    v.proj_sum[...] = jnp.sum(v.proj_slots[...].astype(F32), axis=0).astype(BF16)

    def to_strips(src, dst, send, recv):
        return [push(src, dst, send.at[k - 1], recv.at[k - 1], strip_peer(strip, k)) for k in range(1, 16)]

    spread = to_strips(v.proj_sum, v.proj_all.at[strip], v.spread_send, v.spread_recv)
    v.proj_all[strip] = v.proj_sum[...]

    for ring in last:
        ring.close()
    here = sample * SHARD
    z_copies = [
        push(
            partial.at[pl.ds(pl.multiple_of(here + lax.rem(z + k, 8) * 16, 16), 16), :],
            v.z_slots.at[z], v.zsum_send.at[k - 1], v.zsum_recv.at[k - 1], z_peer(z, k),
        )
        for k in range(1, 8)
    ]
    v.z_slots[z] = partial[pl.ds(pl.multiple_of(here + z * 16, 16), 16), :]

    swap_input.wait()
    for k in range(CHANS // FEAT):
        total = (v.own[k] + v.came[k].astype(F32)).astype(BF16)
        for r in range(ROWS):
            v.out_input[r, :, pl.ds(k * FEAT, FEAT)] = total[r * PITCH : r * PITCH + COLS]

    for copy in z_copies:
        copy.wait()
    v.z_sum[...] = jnp.sum(v.z_slots[...].astype(F32), axis=0).astype(BF16)
    my_rows = pl.ds(pl.multiple_of(z * 16, 16), 16)
    joined = v.joined
    all_copies = to_strips(v.z_sum, joined.at[c, my_rows, :], v.all_send, v.all_recv)
    joined[c, my_rows, :] = v.z_sum[...]

    for copy in keep.pools + keep.images:
        copy.wait()
    v.out_image[...] = (
        lax.dot_general(
            v.pool_all[...][:, 0, :].astype(BF16), v.image_all[...][:, 0, :].astype(BF16),
            (((0,), (0,)), ((), ())), preferred_element_type=F32,
        )
        * FACTOR
    )
    for copy in spread:
        copy.wait()
    for k in range(2):
        total = v.proj_all[k].astype(F32)
        for level in range(1, 8):
            total = total + v.proj_all[2 * level + k].astype(F32)
        v.out_proj[:, pl.ds(k * HALF, HALF)] = total
    for copy in ring_sent + later + done:
        copy.wait_send()
    keep.result.wait_send()
    for copy in all_copies:
        copy.wait()
    for k in range(2):
        v.out_point[:, pl.ds(k * HALF, HALF)] = joined[k, :, pl.ds(0, HALF)].astype(F32)
        for t in range(9):
            v.out_atrous[:, pl.ds(t * FEAT + k * HALF, HALF)] = joined[k, :, pl.ds((t + 1) * HALF, HALF)].astype(F32)


VMEM = pl.BlockSpec(memory_space=pltpu.VMEM)
ANY = pl.BlockSpec(memory_space=pl.ANY)


def dma(*shape):
    return pltpu.SemaphoreType.DMA(shape)


def sized(dtype, *shape):
    return jax.ShapeDtypeStruct(shape, dtype)


ARGS = ("images", "w_point", "w_atrous", "w_image", "w_proj", "cotangent")
OUTS = (
    ("out_result", sized(BF16, ROWS, COLS, FEAT)),
    ("out_input", sized(BF16, ROWS, COLS, CHANS)),
    ("out_point", sized(F32, SHARD, FEAT)),
    ("out_atrous", sized(F32, SHARD, 9 * FEAT)),
    ("out_image", sized(F32, SHARD, FEAT)),
    ("out_proj", sized(F32, 48, FEAT)),
)
SCRATCH = (
    ("stage", (ROWS, COLS, CHANS), BF16),
    ("cot_stage", (ROWS, COLS, FEAT), BF16),
    ("spots", (SPOTS, CHANS), BF16),
    ("full", (CHANS, WIDER), BF16),
    ("proj", (3 * FEAT, FEAT), BF16),
    ("taps", (TAPS, SPOTS, HALF), F32),
    ("pool_src", (1, CHANS), F32),
    ("pool_slots", (8, 1, CHANS), F32),
    ("pool_rows", (16, 8, SHARD), F32),
    ("pool_all", (16, 8, SHARD), F32),
    ("image_grad", (8, FEAT), F32),
    ("image_all", (16, 8, FEAT), F32),
    ("images_half", (2, 8, HALF), F32),
    ("outer", (2, SPOTS, HALF), BF16),
    ("halo", (2, SPOTS, HALF), BF16),
    ("centre", (SPOTS, HALF), F32),
    ("norm_p", (SPOTS, HALF), F32),
    ("norm_a", (SPOTS, HALF), F32),
    ("slope_p", (SPOTS, HALF), F32),
    ("slope_a", (SPOTS, HALF), F32),
    ("mixed", (SPOTS, HALF), F32),
    ("upstream", (SPOTS, HALF), F32),
    ("relu", (2, SPOTS, FEAT), BF16),
    ("mix", (2, SPOTS, HALF), BF16),
    ("columns", (2, 8, HALF), F32),
    ("cot", (SPOTS, HALF), BF16),
    ("cot_send", (BLOCK, HALF), BF16),
    ("result_send", (2, BLOCK, HALF), BF16),
    ("result_half", (BLOCK, HALF), BF16),
    ("ar_src", (4, 4, HALF), F32),
    ("ar_mid", (4, 4, HALF), F32),
    ("ar_z", (4, 8, 4, HALF), F32),
    ("ar_xy", (4, 16, 4, HALF), F32),
    ("proj_part", (3 * FEAT, HALF), BF16),
    ("proj_slots", (16, 48, HALF), BF16),
    ("proj_sum", (48, HALF), BF16),
    ("proj_all", (16, 48, HALF), BF16),
    ("grad_atrous", (SPOTS, HALF), BF16),
    ("back_halo", (2, SPOTS, HALF), BF16),
    ("cols", (SPOTS, WIDE), BF16),
    ("partial", (CHANS, WIDE), BF16),
    ("opposite", (10, 2, 32, WIDE), BF16),
    ("beside", (10, 2, 64, WIDE), BF16),
    ("pair", (2, BLOCK, FEAT), F32),
    ("own", (8, BLOCK, FEAT), F32),
    ("away", (8, BLOCK, FEAT), BF16),
    ("came", (8, BLOCK, FEAT), BF16),
    ("z_slots", (8, 16, WIDE), BF16),
    ("z_sum", (16, WIDE), BF16),
    ("joined", (2, SHARD, WIDE), BF16),
)
SEMAPHORES = (
    ("local", (14,)),
    ("core", (8,)),
    ("gather", (40,)),
    ("proj", (15,)),
    ("pool", (7,)),
    ("pall", (15,)),
    ("image", (15,)),
    ("halo", (4,)),
    ("z", (4, 7)),
    ("xy", (4, 15)),
    ("pgrad", (15,)),
    ("ring", (60,)),
    ("zsum", (7,)),
    ("spread", (15,)),
    ("all", (15,)),
)


def on_device(images, w_point, w_atrous, w_image, w_proj, cotangent):
    names = list(ARGS) + [n for n, _ in OUTS] + [n for n, _, _ in SCRATCH]
    scratch = [pltpu.VMEM(shape, dtype) for _, shape, dtype in SCRATCH]
    for name, shape in SEMAPHORES:
        kinds = ("local",) if name == "local" else (name + "_send", name + "_recv")
        for kind in kinds:
            names.append(kind)
            scratch.append(dma(*shape))
    outs = pl.pallas_call(
        functools.partial(whole_kernel, tuple(names)),
        out_shape=[shape for _, shape in OUTS],
        in_specs=[ANY] * 6,
        out_specs=[VMEM] * 6,
        scratch_shapes=scratch,
        compiler_params=pltpu.CompilerParams(
            collective_id=0, has_side_effects=True, vmem_limit_bytes=60 << 20
        ),
        name="whole",
    )(images[0], w_point, w_atrous, w_image, w_proj, cotangent[0])
    return (outs[0][None], outs[1][None], *outs[2:])


def solution(mesh):
    finer = Mesh(mesh.devices.reshape(8, 2, 4, 4), STRIP + SAMPLE)
    placed = (
        P(SAMPLE, STRIP, None, None),
        P(SAMPLE, None),
        P(SAMPLE, None),
        P(SAMPLE, None),
        P(SAMPLE, None),
        P(SAMPLE, STRIP, None, None),
    )
    return jax.shard_map(
        on_device,
        mesh=finer,
        in_specs=placed,
        out_specs=(
            P(SAMPLE, STRIP, None, None),
            P(SAMPLE, STRIP, None, None),
            P(SAMPLE, None),
            P(SAMPLE, None),
            P(SAMPLE, None),
            P(SAMPLE, None),
        ),
        check_vma=False,
    )
```

```python
import functools
import types

import jax
import jax.numpy as jnp
from jax import lax
from jax.experimental import pallas as pl
from jax.experimental.pallas import tpu as pltpu
from jax.sharding import Mesh
from jax.sharding import PartitionSpec as P

RATE = 12
STRIP = ("strip_0", "strip_1")
SAMPLE = ("sample_0", "sample_1")
EPSILON = 1e-05
MESH_ID = pl.DeviceIdType.MESH
F32 = jnp.float32
BF16 = jnp.bfloat16

CHANS = 2048
FEAT = 256
HALF = 128
ROWS = 3
COLS = 108
PITCH = 112
BLOCK = ROWS * PITCH
SPOTS = 2 * BLOCK
DEPTH = 768
TAPS = 10
WIDE = TAPS * HALF
WIDER = WIDE + HALF
SHARD = 128
SAMPLE_AREA = 48.0 * 108.0
TOTAL_AREA = 16.0 * SAMPLE_AREA
FACTOR = 1.0 / 16.0


def places():
    return tuple(lax.axis_index(a) for a in STRIP + SAMPLE)


def z_peer(z, k):
    return {"strip_0": lax.rem(z + k + 8, 8)}


def other_core(c):
    return {"strip_1": 1 - c}


def along(axis, y, x, d):
    if axis == "x":
        return {"sample_1": lax.rem(x + d + 4, 4)}
    return {"sample_0": lax.rem(y + d + 4, 4)}


def sample_peer(me, k):
    other = lax.rem(me + k, 16)
    return {"sample_0": lax.div(other, 4), "sample_1": lax.rem(other, 4)}


def greet(peers, meanwhile):
    barrier = pltpu.get_barrier_semaphore()
    for peer in peers:
        pl.semaphore_signal(barrier, inc=1, device_id=peer, device_id_type=MESH_ID)
    meanwhile()
    pl.semaphore_wait(barrier, len(peers))


def push(src, dst, send, recv, peer):
    copy = pltpu.make_async_remote_copy(
        src_ref=src,
        dst_ref=dst,
        send_sem=send,
        recv_sem=recv,
        device_id=peer,
        device_id_type=MESH_ID,
    )
    copy.start()
    return copy


def spot_column(shape):
    full = lax.broadcasted_iota(jnp.int32, (shape[0] // PITCH, PITCH, shape[1]), 1)
    return full.reshape(shape)


def moved(values, offset, column):
    if offset == 0:
        return values
    spots = values.shape[0]
    if offset > 0:
        return jnp.where(column < COLS - offset, pltpu.roll(values, spots - offset, 0), 0.0)
    inside = (column >= -offset) & (column < COLS)
    return jnp.where(inside, pltpu.roll(values, -offset, 0), 0.0)


def ring_gather(full, y, x, send, recv, early, late):
    count = [0]
    sent = []

    def put(kind, a, b, part, first, d):
        if kind == 0:
            row = lax.rem(y + b + 4, 4) * 4 + lax.rem(x + a + 4, 4)
            axis = "x" if first else "y"
        else:
            row = lax.rem(y + a + 4, 4) * 4 + lax.rem(x + b + 4, 4)
            axis = "y" if first else "x"
        start, size = ((0, 64), (0, 32), (32, 32))[part]
        rows = pl.ds(pl.multiple_of(row * SHARD + kind * 64 + start, 32), size)
        k = count[0]
        count[0] += 1
        copy = push(full.at[rows, :], full.at[rows, :], send.at[k], recv.at[k], along(axis, y, x, d))
        sent.append(copy)
        return copy

    kinds = (0, 1)
    right, left, up, down = {}, {}, {}, {}
    fr, fl, fu, fd = {}, {}, {}, {}

    def spread(kind, a):
        up[kind, a] = put(kind, a, 0, 0, False, 1)
        down[kind, a] = put(kind, a, 0, 0, False, -1)

    def relay(kind, a):
        up[kind, a].wait_recv()
        fu[kind, a] = put(kind, a, -1, 1, False, 1)
        down[kind, a].wait_recv()
        fd[kind, a] = put(kind, a, 1, 2, False, -1)

    for kind in kinds:
        right[kind] = put(kind, 0, 0, 0, True, 1)
        left[kind] = put(kind, 0, 0, 0, True, -1)
    for kind in kinds:
        spread(kind, 0)
    early()
    for kind in kinds:
        right[kind].wait_recv()
        fr[kind] = put(kind, -1, 0, 1, True, 1)
        left[kind].wait_recv()
        fl[kind] = put(kind, 1, 0, 2, True, -1)
    for kind in kinds:
        spread(kind, -1)
        spread(kind, 1)
    for kind in kinds:
        relay(kind, 0)
    late()
    for kind in kinds:
        fr[kind].wait_recv()
        fl[kind].wait_recv()
        spread(kind, 2)
    for a in (-1, 1, 2):
        for kind in kinds:
            relay(kind, a)
    for a in (0, -1, 1, 2):
        for kind in kinds:
            fu[kind, a].wait_recv()
            fd[kind, a].wait_recv()
    return sent


def silu(v):
    return v * lax.logistic(v)


def silu_slope(v):
    s = lax.logistic(v)
    return s * (1.0 + v * (1.0 - s))


def whole_kernel(names, *refs):
    v = types.SimpleNamespace(**dict(zip(names, refs)))
    z, c, y, x = places()
    sample = y * 4 + x
    mate = other_core(c)
    mine = pl.multiple_of(c * BLOCK, 16)
    lane = pl.multiple_of(c * HALF, HALF)
    other_lane = pl.multiple_of((1 - c) * HALF, HALF)
    column = spot_column((SPOTS, HALF))
    inside = column < COLS
    zero = jnp.zeros((SPOTS, HALF), F32)

    def swap(src, dst, k):
        return push(src, dst, v.core_send.at[k], v.core_recv.at[k], mate)

    full, spots, proj = v.full, v.spots, v.proj
    shard = pl.ds(pl.multiple_of(sample * SHARD, SHARD), SHARD)
    loads = [pltpu.make_async_copy(v.w_point.at[:, pl.ds(lane, HALF)], full.at[shard, pl.ds(0, HALF)], v.local.at[0])]
    for t in range(9):
        loads.append(
            pltpu.make_async_copy(
                v.w_atrous.at[:, pl.ds(pl.multiple_of(t * FEAT + lane, HALF), HALF)],
                full.at[shard, pl.ds((t + 1) * HALF, HALF)],
                v.local.at[t + 1],
            )
        )
    loads.append(
        pltpu.make_async_copy(v.w_image.at[:, pl.ds(lane, HALF)], full.at[shard, pl.ds(WIDE, HALF)], v.local.at[10])
    )
    own_rows = pl.ds(pl.multiple_of(sample * 48, 16), 48)
    half_lanes = pl.ds(lane, HALF)
    loads.append(
        pltpu.make_async_copy(v.w_proj.at[:, half_lanes], proj.at[own_rows, half_lanes], v.local.at[11])
    )
    inputs = [
        pltpu.make_async_copy(v.images, v.stage, v.local.at[12]),
        pltpu.make_async_copy(v.cotangent, v.cot_stage, v.local.at[13]),
    ]
    for load in loads + inputs:
        load.start()

    def clear():
        spots[pl.ds(mine, BLOCK), :] = jnp.zeros((BLOCK, CHANS), BF16)
        spots[pl.ds(SPOTS, DEPTH - SPOTS), :] = jnp.zeros((DEPTH - SPOTS, CHANS), BF16)
        v.cols[pl.ds(SPOTS, DEPTH - SPOTS), :] = jnp.zeros((DEPTH - SPOTS, WIDE), BF16)
        v.cot[pl.ds(mine, BLOCK), :] = jnp.zeros((BLOCK, HALF), BF16)
        v.cot_send[...] = jnp.zeros_like(v.cot_send)

    greet([mate] + [z_peer(z, k) for k in range(1, 8)] + [sample_peer(sample, k) for k in range(1, 16)], clear)
    for load in loads:
        load.wait()

    later = []

    def early():
        for load in inputs:
            load.wait()
        for r in range(ROWS):
            spots[pl.ds(pl.multiple_of(mine + r * PITCH, 16), COLS), :] = v.stage[r]
        later.append(swap(spots.at[pl.ds(mine, BLOCK), :], spots.at[pl.ds(mine, BLOCK), :], 0))
        for r in range(ROWS):
            v.cot_send[pl.ds(r * PITCH, COLS), :] = v.cot_stage[r, :, pl.ds(other_lane, HALF)]
            v.cot[pl.ds(pl.multiple_of(mine + r * PITCH, 16), COLS), :] = v.cot_stage[r, :, pl.ds(lane, HALF)]
        later.append(swap(v.cot_send, v.cot.at[pl.ds(mine, BLOCK), :], 1))

    pools = []

    def late():
        later[0].wait_recv()

        def add_rows(i, total):
            return total + spots[pl.ds(pl.multiple_of(i * 16, 16), 16), :].astype(F32)

        sums = lax.fori_loop(0, SPOTS // 16, add_rows, jnp.zeros((16, CHANS), F32))
        v.pool_src[...] = jnp.sum(sums, axis=0, keepdims=True)
        pools.extend(
            push(v.pool_src, v.pool_slots.at[z], v.pool_send.at[k - 1], v.pool_recv.at[k - 1], z_peer(z, k))
            for k in range(1, 8)
        )
        v.pool_slots[z] = v.pool_src[...]

        def flip(k, carry):
            at = pl.ds(pl.multiple_of(k * SHARD, SHARD), SHARD)
            v.flipped[at, :] = spots[:, at].T
            return carry

        lax.fori_loop(0, CHANS // SHARD, flip, 0)

    ring_sent = ring_gather(full, y, x, v.gather_send, v.gather_recv, early, late)

    proj_copies = [
        push(
            proj.at[own_rows, half_lanes], proj.at[own_rows, half_lanes],
            v.proj_send.at[k - 1], v.proj_recv.at[k - 1], sample_peer(sample, k),
        )
        for k in range(1, 16)
    ]

    def multiply(n, carry):
        product = jnp.dot(
            spots[pl.ds(0, SPOTS), :], full[:, pl.ds(pl.multiple_of(n * FEAT, FEAT), FEAT)], preferred_element_type=F32
        )
        v.taps[2 * n] = product[:, :HALF]
        v.taps[2 * n + 1] = product[:, HALF:]
        return carry

    lax.fori_loop(0, TAPS // 2, multiply, 0)

    def row_tap(r):
        first = 1 + 3 * (r + 1)
        return v.taps[first + 1] + moved(v.taps[first], -RATE, column) + moved(v.taps[first + 2], RATE, column)

    v.outer[0] = row_tap(-1).astype(BF16)
    below = push(v.outer.at[0], v.halo.at[0], v.halo_send.at[0], v.halo_recv.at[0], z_peer(z, 2))
    v.outer[1] = row_tap(1).astype(BF16)
    above = push(v.outer.at[1], v.halo.at[1], v.halo_send.at[1], v.halo_recv.at[1], z_peer(z, -2))
    v.centre[...] = row_tap(0)
    keep = types.SimpleNamespace()

    def to_samples(src_of, slots, send, recv):
        return [
            push(
                src_of(lax.rem(sample + k, 16)), slots.at[sample], send.at[k - 1], recv.at[k - 1],
                sample_peer(sample, k),
            )
            for k in range(1, 16)
        ]


    def totals(i, rows, meanwhile):
        for k, row in enumerate(rows):
            v.ar_src[i, pl.ds(k, 1), :] = row
        copies = [
            push(v.ar_src.at[i], v.ar_z.at[i, z], v.z_send.at[i, k - 1], v.z_recv.at[i, k - 1], z_peer(z, k))
            for k in range(1, 8)
        ]
        v.ar_z[i, z] = v.ar_src[i]
        meanwhile[0]()
        for copy in copies:
            copy.wait()
        whole = jnp.sum(v.ar_z[i], axis=0)
        v.ar_mid[i] = whole
        copies = [
            push(
                v.ar_mid.at[i], v.ar_xy.at[i, sample], v.xy_send.at[i, k - 1], v.xy_recv.at[i, k - 1],
                sample_peer(sample, k),
            )
            for k in range(1, 16)
        ]
        v.ar_xy[i, sample] = whole
        meanwhile[1]()
        for copy in copies:
            copy.wait()
        total = jnp.sum(v.ar_xy[i], axis=0)
        return [whole[k : k + 1] for k in range(4)], [total[k : k + 1] for k in range(4)]

    def down(a):
        return jnp.sum(a, axis=0, keepdims=True)

    def finish(total, power):
        centre = total / TOTAL_AREA
        return centre, lax.rsqrt(power / TOTAL_AREA - centre * centre + EPSILON)

    def mean_of(both):
        return (jnp.sum(both[0]) + jnp.sum(both[1])) * (1.0 / FEAT)

    nothing = lambda: None
    below.wait()
    above.wait()
    point = v.taps[0]
    atrous = (
        v.centre[...]
        + jnp.where(z >= 2, v.halo[0].astype(F32), zero)
        + jnp.where(z < 6, v.halo[1].astype(F32), zero)
    )
    v.centre[...] = atrous

    def send_pools():
        for k in range(16):
            rows = keep.pooled[:, k * SHARD : (k + 1) * SHARD].astype(F32)
            v.pool_rows[k] = jnp.broadcast_to(rows, (8, SHARD))
        keep.pools = to_samples(lambda j: v.pool_rows.at[j], v.pool_all, v.pall_send, v.pall_recv)
        v.pool_all[sample] = v.pool_rows[sample]

    def image_product():
        for copy in pools:
            copy.wait()
        keep.pooled = (jnp.sum(v.pool_slots[...], axis=0) / SAMPLE_AREA).astype(BF16)
        image = jnp.dot(
            jnp.broadcast_to(keep.pooled, (16, CHANS)), full[:, pl.ds(WIDE, HALF)], preferred_element_type=F32
        )
        v.images_half[c] = image[0:8]
        later.append(swap(v.images_half.at[c], v.images_half.at[c], 2))
        for copy in proj_copies:
            copy.wait()
        later.append(swap(proj.at[:, half_lanes], proj.at[:, half_lanes], 8))

    def image_forward():
        later[-2].wait_recv()
        halves = [v.images_half[0][0:1], v.images_half[1][0:1]]
        image_mean = mean_of(halves)
        apart = [h - image_mean for h in halves]
        keep.layer_scale = lax.rsqrt(jnp.full((1, HALF), mean_of([a * a for a in apart]) + EPSILON, F32))
        keep.layer_norm = [a * keep.layer_scale for a in apart]
        keep.relu_image = jnp.concatenate([silu(a) for a in keep.layer_norm], axis=1).astype(BF16)
        later[-1].wait_recv()
        keep.image_row = jnp.dot(
            jnp.broadcast_to(keep.relu_image, (16, FEAT)),
            proj[pl.ds(2 * FEAT, FEAT), pl.ds(lane, HALF)],
            preferred_element_type=F32,
        )[0:1]

    _, (s0, s1, s2, s3) = totals(
        0, [down(point), down(point * point), down(atrous), down(atrous * atrous)], (image_product, image_forward)
    )
    centre_p, scale_p = finish(s0, s1)
    centre_a, scale_a = finish(s2, s3)
    v.norm_p[...] = (point - centre_p) * scale_p
    v.norm_a[...] = (v.centre[...] - centre_a) * scale_a
    relu = v.relu
    relu[c, :, pl.ds(0, HALF)] = jnp.where(inside, silu(v.norm_p[...]), 0.0).astype(BF16)
    relu[c, :, pl.ds(HALF, HALF)] = jnp.where(inside, silu(v.norm_a[...]), 0.0).astype(BF16)
    swap_relu = swap(relu.at[c], relu.at[c], 3)

    def mix_term(k):
        total = None
        for b in range(2):
            first = pl.multiple_of(k * HALF + b * FEAT, HALF)
            term = jnp.dot(
                relu[k, :, pl.ds(b * HALF, HALF)],
                proj[pl.ds(first, HALF), pl.ds(lane, HALF)],
                preferred_element_type=F32,
            )
            total = term if total is None else total + term
        return total

    mixed = mix_term(c) + keep.image_row
    swap_relu.wait()
    mixed = jnp.where(inside, mixed + mix_term(1 - c), 0.0)
    v.mixed[...] = mixed

    def slope_point():
        send_pools()
        v.slope_p[...] = silu_slope(v.norm_p[...])

    def slope_atrous():
        v.slope_a[...] = silu_slope(v.norm_a[...])

    blank = jnp.zeros((1, HALF), F32)
    (mixed_sample, _, _, _), (s0, s1, _, _) = totals(
        1, [down(mixed), down(mixed * mixed), blank, blank], (slope_point, slope_atrous)
    )
    centre_m, scale_m = finish(s0, s1)
    norm_mix = (v.mixed[...] - centre_m) * scale_m
    v.mixed[...] = norm_mix
    later[1].wait_recv()
    sigma = lax.logistic(norm_mix)
    upstream = jnp.where(inside, v.cot[...].astype(F32) * (sigma * (1.0 + norm_mix * (1.0 - sigma))), 0.0)
    v.upstream[...] = upstream

    def make_result():
        result = silu(v.mixed[...]).astype(BF16)
        v.result_send[0] = result[:BLOCK]
        v.result_send[1] = result[BLOCK:]
        keep.result = swap(v.result_send.at[1 - c], v.result_half, 4)

    def store_result():
        keep.result.wait_recv()
        for r in range(ROWS):
            rows = pl.ds(r * PITCH, COLS)
            v.out_result[r, :, pl.ds(lane, HALF)] = v.result_send[c, rows, :]
            v.out_result[r, :, pl.ds(other_lane, HALF)] = v.result_half[rows, :]

    (up_sample, _, _, _), (s0, s1, _, _) = totals(
        2, [down(upstream), down(upstream * norm_mix), blank, blank], (make_result, store_result)
    )
    mean_u = s0 / TOTAL_AREA
    mean_un = s1 / TOTAL_AREA
    grad_mix = jnp.where(inside, (v.upstream[...] - mean_u - v.mixed[...] * mean_un) * scale_m, 0.0)
    mix, columns = v.mix, v.columns
    mix[c] = grad_mix.astype(BF16)
    swap_mix = swap(mix.at[c], mix.at[c], 5)
    norm_sample = (mixed_sample - SAMPLE_AREA * centre_m) * scale_m
    column_total = (up_sample - SAMPLE_AREA * mean_u - mean_un * norm_sample) * scale_m
    columns[c] = jnp.broadcast_to(column_total, (8, HALF))
    swap_columns = swap(columns.at[c], columns.at[c], 6)

    def back_term(first, k):
        return lax.dot_general(
            mix[k],
            proj[pl.ds(pl.multiple_of(first + lane, HALF), HALF), pl.ds(pl.multiple_of(k * HALF, HALF), HALF)],
            (((1,), (1,)), ((), ())),
            preferred_element_type=F32,
        )

    back_p = back_term(0, c)
    back_a = back_term(FEAT, c)
    swap_mix.wait()
    up_point = (back_p + back_term(0, 1 - c)) * v.slope_p[...]
    up_atrous = (back_a + back_term(FEAT, 1 - c)) * v.slope_a[...]
    v.slope_p[...] = up_point
    v.slope_a[...] = up_atrous

    def image_backward():
        swap_columns.wait()
        column_b = jnp.concatenate([columns[0][0:1], columns[1][0:1]], axis=1).astype(BF16)
        back_image = lax.dot_general(
            jnp.broadcast_to(column_b, (16, FEAT)),
            proj[pl.ds(2 * FEAT, FEAT), :],
            (((1,), (1,)), ((), ())),
            preferred_element_type=F32,
        )
        layer_norm = keep.layer_norm
        up_image = [back_image[0:1, k * HALF : (k + 1) * HALF] * silu_slope(layer_norm[k]) for k in range(2)]
        mean_up = mean_of(up_image)
        mean_up_norm = mean_of([up_image[k] * layer_norm[k] for k in range(2)])
        image_grad = jnp.concatenate(
            [(up_image[k] - mean_up - layer_norm[k] * mean_up_norm) * keep.layer_scale for k in range(2)], axis=1
        )
        v.image_grad[...] = jnp.broadcast_to(image_grad.astype(BF16).astype(F32), (8, FEAT))
        keep.images = to_samples(lambda j: v.image_grad, v.image_all, v.image_send, v.image_recv)
        v.image_all[sample] = v.image_grad[...]

    def proj_gradient():
        for k in range(2):
            part = lax.dot_general(
                relu[k], mix[c], (((0,), (0,)), ((), ())), preferred_element_type=F32
            ) * FACTOR
            v.proj_part[pl.ds(k * HALF, HALF), :] = part[:HALF].astype(BF16)
            v.proj_part[pl.ds(FEAT + k * HALF, HALF), :] = part[HALF:].astype(BF16)
        once = lax.broadcasted_iota(jnp.int32, (16, FEAT), 0) == 0
        gate = jnp.where(z == 0, FACTOR, 0.0).astype(F32)
        outer = lax.dot_general(
            jnp.where(once, jnp.broadcast_to(keep.relu_image.astype(F32), (16, FEAT)), 0.0).astype(BF16),
            jnp.broadcast_to(columns[c][0:1], (16, HALF)).astype(BF16),
            (((0,), (0,)), ((), ())),
            preferred_element_type=F32,
        )
        v.proj_part[pl.ds(2 * FEAT, FEAT), :] = (outer * gate).astype(BF16)

    _, (s0, s1, s2, s3) = totals(
        3,
        [down(up_point), down(up_point * v.norm_p[...]), down(up_atrous), down(up_atrous * v.norm_a[...])],
        (image_backward, proj_gradient),
    )

    def back_norm(up, norm, first, second, scale):
        grad = (up - first / TOTAL_AREA - norm * (second / TOTAL_AREA)) * scale
        return jnp.where(inside, grad, 0.0)

    grad_atrous = back_norm(v.slope_a[...], v.norm_a[...], s2, s3, scale_a)
    v.grad_atrous[...] = grad_atrous.astype(BF16)
    upper = push(v.grad_atrous, v.back_halo.at[1], v.halo_send.at[2], v.halo_recv.at[2], z_peer(z, 2))
    lower = push(v.grad_atrous, v.back_halo.at[0], v.halo_send.at[3], v.halo_recv.at[3], z_peer(z, -2))
    grad_copies = [
        push(
            v.proj_part.at[pl.ds(pl.multiple_of(lax.rem(sample + k, 16) * 48, 16), 48), :], v.proj_slots.at[sample],
            v.pgrad_send.at[k - 1], v.pgrad_recv.at[k - 1], sample_peer(sample, k),
        )
        for k in range(1, 16)
    ]
    v.proj_slots[sample] = v.proj_part[own_rows, :]
    cols = v.cols
    cols[pl.ds(0, SPOTS), pl.ds(0, HALF)] = back_norm(v.slope_p[...], v.norm_p[...], s0, s1, scale_p).astype(BF16)

    def fill(r, source):
        for s in (-1, 0, 1):
            t = 1 + 3 * (r + 1) + (s + 1)
            cols[pl.ds(0, SPOTS), pl.ds(t * HALF, HALF)] = moved(source, -RATE * s, column).astype(BF16)

    fill(0, v.grad_atrous[...].astype(F32))
    upper.wait()
    fill(1, jnp.where(z >= 2, v.back_halo[1].astype(F32), zero))
    lower.wait()
    fill(-1, jnp.where(z < 6, v.back_halo[0].astype(F32), zero))

    partial, opposite, beside = v.partial, v.opposite, v.beside

    def weight_block(dy):
        base = lax.rem(y + dy + 4, 4) * 512

        def weight_part(k, carry):
            at = pl.ds(pl.multiple_of(base + k * FEAT, FEAT), FEAT)
            part = jnp.dot(v.flipped[at, :], cols[...], preferred_element_type=F32)
            partial[at, :] = (part * FACTOR).astype(BF16)
            return carry

        lax.fori_loop(0, 2, weight_part, 0)

    count = [0]
    done = []

    class Ring:
        def __init__(self, slot, axis, base, index):
            self.slot, self.axis, self.base, self.index = slot, axis, base, index

        def rows(self, o, start, size):
            return pl.ds(pl.multiple_of(self.index(o) * SHARD + self.base + start, 32), size)

        def put(self, src, dst, d):
            k = count[0]
            count[0] += 1
            copy = push(src, dst, v.ring_send.at[k], v.ring_recv.at[k], along(self.axis, y, x, d))
            done.append(copy)
            return copy

        def far(self):
            s = self.slot
            self.m0 = self.put(partial.at[self.rows(2, 0, 32), :], opposite.at[s, 0], 1)
            self.m1 = self.put(partial.at[self.rows(2, 32, 32), :], opposite.at[s, 1], -1)

        def near_up(self):
            self.m2 = self.put(partial.at[self.rows(1, 32, 32), :], beside.at[self.slot, 0, pl.ds(32, 32), :], 1)

        def near_down(self):
            self.m3 = self.put(partial.at[self.rows(-1, 0, 32), :], beside.at[self.slot, 1, pl.ds(0, 32), :], -1)

        def relay(self):
            s = self.slot
            self.m0.wait_recv()
            at = self.rows(1, 0, 32)
            partial[at, :] = (partial[at, :].astype(F32) + opposite[s, 0].astype(F32)).astype(BF16)
            self.m4 = self.put(partial.at[at, :], beside.at[s, 0, pl.ds(0, 32), :], 1)
            self.m1.wait_recv()
            at = self.rows(-1, 32, 32)
            partial[at, :] = (partial[at, :].astype(F32) + opposite[s, 1].astype(F32)).astype(BF16)
            self.m5 = self.put(partial.at[at, :], beside.at[s, 1, pl.ds(32, 32), :], -1)

        def close(self):
            s = self.slot
            for m in (self.m2, self.m3, self.m4, self.m5):
                m.wait_recv()
            at = self.rows(0, 0, 64)
            partial[at, :] = (
                partial[at, :].astype(F32) + beside[s, 0].astype(F32) + beside[s, 1].astype(F32)
            ).astype(BF16)

    def block(dy, dx):
        return lax.rem(y + dy + 4, 4) * 4 + lax.rem(x + dx + 4, 4)

    order = (2, 1, -1, 0)
    by_y = [Ring(n, "y", 0, functools.partial(lambda a, o: block(o, a), a)) for n, a in enumerate(order)]
    by_x = [Ring(4 + n, "x", 64, functools.partial(lambda a, o: block(a, o), a)) for n, a in enumerate(order)]
    last = [
        Ring(8, "x", 0, lambda o: block(0, o)),
        Ring(9, "y", 64, lambda o: block(o, 0)),
    ]
    for n, dy in enumerate(order):
        weight_block(dy)
        by_x[n].far()
        if dy == 2:
            for ring in by_y:
                ring.far()
        if dy == 1:
            for ring in by_y:
                ring.near_up()
        if dy == -1:
            for ring in by_y:
                ring.near_down()
        by_x[n].near_up()
        by_x[n].near_down()

    half_grad = v.image_grad[:, pl.ds(lane, HALF)]
    grad_rows = jnp.concatenate([half_grad, half_grad], axis=0).astype(BF16)

    def input_part(k, carry):
        at = pl.ds(pl.multiple_of(k * FEAT, FEAT), FEAT)
        part = lax.dot_general(
            cols[pl.ds(0, SPOTS), :], full[at, pl.ds(0, WIDE)], (((1,), (1,)), ((), ())), preferred_element_type=F32
        )
        pool = lax.dot_general(
            grad_rows, full[at, pl.ds(WIDE, HALF)], (((1,), (1,)), ((), ())), preferred_element_type=F32
        )[0:1] / SAMPLE_AREA
        part = part + pool
        v.pair[0] = part[:BLOCK]
        v.pair[1] = part[BLOCK:]
        v.own[k] = v.pair[c]
        v.away[k] = v.pair[1 - c].astype(BF16)
        return carry

    lax.fori_loop(0, 4, input_part, 0)
    for n in range(4):
        by_x[n].relay()
        by_y[n].relay()
    lax.fori_loop(4, 8, input_part, 0)
    swap_input = swap(v.away, v.came, 7)
    for n in range(4):
        by_y[n].close()
        by_x[n].close()
        if n == 0:
            for ring in last:
                ring.far()
        if n == 1:
            for ring in last:
                ring.near_up()
        if n == 2:
            for ring in last:
                ring.near_down()
    for ring in last:
        ring.relay()

    for copy in grad_copies:
        copy.wait()
    v.proj_sum[...] = jnp.sum(v.proj_slots[...].astype(F32), axis=0).astype(BF16)

    def to_levels(src, dst, send, recv):
        return [push(src, dst, send.at[k - 1], recv.at[k - 1], z_peer(z, k)) for k in range(1, 8)]

    spread = to_levels(v.proj_sum, v.proj_all.at[z], v.spread_send, v.spread_recv)
    v.proj_all[z] = v.proj_sum[...]

    for ring in last:
        ring.close()
    here = sample * SHARD
    z_copies = [
        push(
            partial.at[pl.ds(pl.multiple_of(here + lax.rem(z + k, 8) * 16, 16), 16), :],
            v.z_slots.at[z], v.zsum_send.at[k - 1], v.zsum_recv.at[k - 1], z_peer(z, k),
        )
        for k in range(1, 8)
    ]
    v.z_slots[z] = partial[pl.ds(pl.multiple_of(here + z * 16, 16), 16), :]

    swap_input.wait()
    for k in range(CHANS // FEAT):
        total = (v.own[k] + v.came[k].astype(F32)).astype(BF16)
        for r in range(ROWS):
            v.out_input[r, :, pl.ds(k * FEAT, FEAT)] = total[r * PITCH : r * PITCH + COLS]

    for copy in z_copies:
        copy.wait()
    v.z_sum[...] = jnp.sum(v.z_slots[...].astype(F32), axis=0).astype(BF16)
    my_rows = pl.ds(pl.multiple_of(z * 16, 16), 16)
    joined = v.joined
    all_copies = to_levels(v.z_sum, joined.at[c, my_rows, :], v.all_send, v.all_recv)
    joined[c, my_rows, :] = v.z_sum[...]

    for copy in keep.pools + keep.images:
        copy.wait()
    v.out_image[...] = (
        lax.dot_general(
            v.pool_all[...][:, 0, :].astype(BF16), v.image_all[...][:, 0, :].astype(BF16),
            (((0,), (0,)), ((), ())), preferred_element_type=F32,
        )
        * FACTOR
    )
    for copy in spread:
        copy.wait()
    v.proj_half[c] = jnp.sum(v.proj_all[...].astype(F32), axis=0)
    swap_proj = swap(v.proj_half.at[c], v.proj_half.at[c], 9)
    for copy in ring_sent + later + done:
        copy.wait_send()
    keep.result.wait_send()
    for copy in all_copies:
        copy.wait()
    swap_joined = swap(joined.at[c], joined.at[c], 10)

    def store(k):
        out = pl.ds(pl.multiple_of(k * HALF, HALF), HALF)
        v.out_point[:, out] = joined[k, :, pl.ds(0, HALF)].astype(F32)
        for t in range(9):
            out = pl.ds(pl.multiple_of(t * FEAT + k * HALF, HALF), HALF)
            v.out_atrous[:, out] = joined[k, :, pl.ds((t + 1) * HALF, HALF)].astype(F32)

    store(c)
    swap_proj.wait()
    for k in range(2):
        v.out_proj[:, pl.ds(k * HALF, HALF)] = v.proj_half[k]
    swap_joined.wait()
    store(1 - c)


def finish_kernel(*refs):
    ins, outs, rooms, (sems_in, sems_out) = refs[:6], refs[6:12], refs[12:18], refs[18:]
    arriving = [pltpu.make_async_copy(ins[k], rooms[k], sems_in.at[k]) for k in range(6)]
    leaving = [pltpu.make_async_copy(rooms[k], outs[k], sems_out.at[k]) for k in range(6)]
    for copy in arriving:
        copy.start()
    for k in range(6):
        arriving[k].wait()
        leaving[k].start()
    for copy in leaving:
        copy.wait()


VMEM = pl.BlockSpec(memory_space=pltpu.VMEM)
ANY = pl.BlockSpec(memory_space=pl.ANY)


def dma(*shape):
    return pltpu.SemaphoreType.DMA(shape)


def sized(dtype, *shape):
    return jax.ShapeDtypeStruct(shape, dtype)


ARGS = ("images", "w_point", "w_atrous", "w_image", "w_proj", "cotangent")
OUTS = (
    ("out_result", sized(BF16, ROWS, COLS, FEAT)),
    ("out_input", sized(BF16, ROWS, COLS, CHANS)),
    ("out_point", sized(F32, SHARD, FEAT)),
    ("out_atrous", sized(F32, SHARD, 9 * FEAT)),
    ("out_image", sized(F32, SHARD, FEAT)),
    ("out_proj", sized(F32, 48, FEAT)),
)
SCRATCH = (
    ("stage", (ROWS, COLS, CHANS), BF16),
    ("cot_stage", (ROWS, COLS, FEAT), BF16),
    ("spots", (DEPTH, CHANS), BF16),
    ("flipped", (CHANS, DEPTH), BF16),
    ("full", (CHANS, WIDER), BF16),
    ("proj", (3 * FEAT, FEAT), BF16),
    ("taps", (TAPS, SPOTS, HALF), F32),
    ("pool_src", (1, CHANS), F32),
    ("pool_slots", (8, 1, CHANS), F32),
    ("pool_rows", (16, 8, SHARD), F32),
    ("pool_all", (16, 8, SHARD), F32),
    ("image_grad", (8, FEAT), F32),
    ("image_all", (16, 8, FEAT), F32),
    ("images_half", (2, 8, HALF), F32),
    ("outer", (2, SPOTS, HALF), BF16),
    ("halo", (2, SPOTS, HALF), BF16),
    ("centre", (SPOTS, HALF), F32),
    ("norm_p", (SPOTS, HALF), F32),
    ("norm_a", (SPOTS, HALF), F32),
    ("slope_p", (SPOTS, HALF), F32),
    ("slope_a", (SPOTS, HALF), F32),
    ("mixed", (SPOTS, HALF), F32),
    ("upstream", (SPOTS, HALF), F32),
    ("relu", (2, SPOTS, FEAT), BF16),
    ("mix", (2, SPOTS, HALF), BF16),
    ("columns", (2, 8, HALF), F32),
    ("cot", (SPOTS, HALF), BF16),
    ("cot_send", (BLOCK, HALF), BF16),
    ("result_send", (2, BLOCK, HALF), BF16),
    ("result_half", (BLOCK, HALF), BF16),
    ("ar_src", (4, 4, HALF), F32),
    ("ar_mid", (4, 4, HALF), F32),
    ("ar_z", (4, 8, 4, HALF), F32),
    ("ar_xy", (4, 16, 4, HALF), F32),
    ("proj_part", (3 * FEAT, HALF), BF16),
    ("proj_slots", (16, 48, HALF), BF16),
    ("proj_sum", (48, HALF), BF16),
    ("proj_all", (8, 48, HALF), BF16),
    ("proj_half", (2, 48, HALF), F32),
    ("grad_atrous", (SPOTS, HALF), BF16),
    ("back_halo", (2, SPOTS, HALF), BF16),
    ("cols", (DEPTH, WIDE), BF16),
    ("partial", (CHANS, WIDE), BF16),
    ("opposite", (10, 2, 32, WIDE), BF16),
    ("beside", (10, 2, 64, WIDE), BF16),
    ("pair", (2, BLOCK, FEAT), F32),
    ("own", (8, BLOCK, FEAT), F32),
    ("away", (8, BLOCK, FEAT), BF16),
    ("came", (8, BLOCK, FEAT), BF16),
    ("z_slots", (8, 16, WIDE), BF16),
    ("z_sum", (16, WIDE), BF16),
    ("joined", (2, SHARD, WIDE), BF16),
)
SEMAPHORES = (
    ("local", (14,)),
    ("core", (11,)),
    ("gather", (40,)),
    ("proj", (15,)),
    ("pool", (7,)),
    ("pall", (15,)),
    ("image", (15,)),
    ("halo", (4,)),
    ("z", (4, 7)),
    ("xy", (4, 15)),
    ("pgrad", (15,)),
    ("ring", (60,)),
    ("zsum", (7,)),
    ("spread", (7,)),
    ("all", (7,)),
)


def on_device(images, w_point, w_atrous, w_image, w_proj, cotangent):
    names = list(ARGS) + [n for n, _ in OUTS] + [n for n, _, _ in SCRATCH]
    scratch = [pltpu.VMEM(shape, dtype) for _, shape, dtype in SCRATCH]
    for name, shape in SEMAPHORES:
        kinds = ("local",) if name == "local" else (name + "_send", name + "_recv")
        for kind in kinds:
            names.append(kind)
            scratch.append(dma(*shape))
    outs = pl.pallas_call(
        functools.partial(whole_kernel, tuple(names)),
        out_shape=[shape for _, shape in OUTS],
        in_specs=[ANY] * 6,
        out_specs=[VMEM] * 6,
        scratch_shapes=scratch,
        compiler_params=pltpu.CompilerParams(
            collective_id=0, has_side_effects=True, vmem_limit_bytes=60 << 20
        ),
        name="whole",
    )(images[0], w_point, w_atrous, w_image, w_proj, cotangent[0])
    outs = pl.pallas_call(
        finish_kernel,
        out_shape=[shape for _, shape in OUTS],
        in_specs=[ANY] * 6,
        out_specs=[ANY] * 6,
        scratch_shapes=[pltpu.VMEM(shape.shape, shape.dtype) for _, shape in OUTS] + [dma(6), dma(6)],
        compiler_params=pltpu.CompilerParams(vmem_limit_bytes=60 << 20),
        name="finish",
    )(*outs)
    return (outs[0][None], outs[1][None], *outs[2:])


def solution(mesh):
    finer = Mesh(mesh.devices.reshape(8, 2, 4, 4), STRIP + SAMPLE)
    placed = (
        P(SAMPLE, STRIP, None, None),
        P(SAMPLE, None),
        P(SAMPLE, None),
        P(SAMPLE, None),
        P(SAMPLE, None),
        P(SAMPLE, STRIP, None, None),
    )
    return jax.shard_map(
        on_device,
        mesh=finer,
        in_specs=placed,
        out_specs=(
            P(SAMPLE, STRIP, None, None),
            P(SAMPLE, STRIP, None, None),
            P(SAMPLE, None),
            P(SAMPLE, None),
            P(SAMPLE, None),
            P(SAMPLE, None),
        ),
        check_vma=False,
    )
```

```python
import functools
import types

import jax
import jax.numpy as jnp
from jax import lax
from jax.experimental import pallas as pl
from jax.experimental.pallas import tpu as pltpu
from jax.sharding import Mesh
from jax.sharding import PartitionSpec as P

RATE = 12
STRIP = ("strip_0", "strip_1")
SAMPLE = ("sample_0", "sample_1")
EPSILON = 1e-05
MESH_ID = pl.DeviceIdType.MESH
F32 = jnp.float32
BF16 = jnp.bfloat16

CHANS = 2048
FEAT = 256
HALF = 128
ROWS = 3
COLS = 108
PITCH = 112
BLOCK = ROWS * PITCH
SPOTS = 2 * BLOCK
DEPTH = 768
TAPS = 10
WIDE = TAPS * HALF
WIDER = WIDE + HALF
SHARD = 128
SAMPLE_AREA = 48.0 * 108.0
TOTAL_AREA = 16.0 * SAMPLE_AREA
FACTOR = 1.0 / 16.0


def places():
    return tuple(lax.axis_index(a) for a in STRIP + SAMPLE)


def z_peer(z, k):
    return {"strip_0": lax.rem(z + k + 8, 8)}


def other_core(c):
    return {"strip_1": 1 - c}


def along(axis, y, x, d):
    if axis == "x":
        return {"sample_1": lax.rem(x + d + 4, 4)}
    return {"sample_0": lax.rem(y + d + 4, 4)}


def sample_peer(me, k):
    other = lax.rem(me + k, 16)
    return {"sample_0": lax.div(other, 4), "sample_1": lax.rem(other, 4)}


def greet(peers, meanwhile):
    barrier = pltpu.get_barrier_semaphore()
    for peer in peers:
        pl.semaphore_signal(barrier, inc=1, device_id=peer, device_id_type=MESH_ID)
    meanwhile()
    pl.semaphore_wait(barrier, len(peers))


def push(src, dst, send, recv, peer):
    copy = pltpu.make_async_remote_copy(
        src_ref=src,
        dst_ref=dst,
        send_sem=send,
        recv_sem=recv,
        device_id=peer,
        device_id_type=MESH_ID,
    )
    copy.start()
    return copy


def spot_column(shape):
    full = lax.broadcasted_iota(jnp.int32, (shape[0] // PITCH, PITCH, shape[1]), 1)
    return full.reshape(shape)


def moved(values, offset, column):
    if offset == 0:
        return values
    spots = values.shape[0]
    if offset > 0:
        return jnp.where(column < COLS - offset, pltpu.roll(values, spots - offset, 0), 0.0)
    inside = (column >= -offset) & (column < COLS)
    return jnp.where(inside, pltpu.roll(values, -offset, 0), 0.0)


def ring_gather(full, y, x, send, recv, early, late, filler):
    count = [0]
    sent = []

    def put(kind, a, b, part, first, d):
        if kind == 0:
            row = lax.rem(y + b + 4, 4) * 4 + lax.rem(x + a + 4, 4)
            axis = "x" if first else "y"
        else:
            row = lax.rem(y + a + 4, 4) * 4 + lax.rem(x + b + 4, 4)
            axis = "y" if first else "x"
        start, size = ((0, 64), (0, 32), (32, 32))[part]
        rows = pl.ds(pl.multiple_of(row * SHARD + kind * 64 + start, 32), size)
        k = count[0]
        count[0] += 1
        copy = push(full.at[rows, :], full.at[rows, :], send.at[k], recv.at[k], along(axis, y, x, d))
        sent.append(copy)
        return copy

    kinds = (0, 1)
    right, left, up, down = {}, {}, {}, {}
    fr, fl, fu, fd = {}, {}, {}, {}

    def spread(kind, a):
        up[kind, a] = put(kind, a, 0, 0, False, 1)
        down[kind, a] = put(kind, a, 0, 0, False, -1)

    def relay(kind, a):
        up[kind, a].wait_recv()
        fu[kind, a] = put(kind, a, -1, 1, False, 1)
        down[kind, a].wait_recv()
        fd[kind, a] = put(kind, a, 1, 2, False, -1)

    for kind in kinds:
        right[kind] = put(kind, 0, 0, 0, True, 1)
        left[kind] = put(kind, 0, 0, 0, True, -1)
    for kind in kinds:
        spread(kind, 0)
    early()
    for kind in kinds:
        right[kind].wait_recv()
        fr[kind] = put(kind, -1, 0, 1, True, 1)
        left[kind].wait_recv()
        fl[kind] = put(kind, 1, 0, 2, True, -1)
    for kind in kinds:
        spread(kind, -1)
        spread(kind, 1)
    for kind in kinds:
        relay(kind, 0)
    late()
    for kind in kinds:
        fr[kind].wait_recv()
        fl[kind].wait_recv()
        spread(kind, 2)
        filler(kind)
    for n, a in enumerate((-1, 1, 2)):
        for kind in kinds:
            relay(kind, a)
            filler(2 + 2 * n + kind)
    for a in (0, -1, 1, 2):
        for kind in kinds:
            fu[kind, a].wait_recv()
            fd[kind, a].wait_recv()
    return sent


def silu(v):
    return v * lax.logistic(v)


def silu_slope(v):
    s = lax.logistic(v)
    return s * (1.0 + v * (1.0 - s))


def whole_kernel(names, *refs):
    v = types.SimpleNamespace(**dict(zip(names, refs)))
    z, c, y, x = places()
    sample = y * 4 + x
    mate = other_core(c)
    mine = pl.multiple_of(c * BLOCK, 16)
    lane = pl.multiple_of(c * HALF, HALF)
    other_lane = pl.multiple_of((1 - c) * HALF, HALF)
    column = spot_column((SPOTS, HALF))
    inside = column < COLS
    zero = jnp.zeros((SPOTS, HALF), F32)

    def swap(src, dst, k):
        return push(src, dst, v.core_send.at[k], v.core_recv.at[k], mate)

    full, spots, proj = v.full, v.spots, v.proj
    shard = pl.ds(pl.multiple_of(sample * SHARD, SHARD), SHARD)
    loads = [pltpu.make_async_copy(v.w_point.at[:, pl.ds(lane, HALF)], full.at[shard, pl.ds(0, HALF)], v.local.at[0])]
    for t in range(9):
        loads.append(
            pltpu.make_async_copy(
                v.w_atrous.at[:, pl.ds(pl.multiple_of(t * FEAT + lane, HALF), HALF)],
                full.at[shard, pl.ds((t + 1) * HALF, HALF)],
                v.local.at[t + 1],
            )
        )
    loads.append(
        pltpu.make_async_copy(v.w_image.at[:, pl.ds(lane, HALF)], full.at[shard, pl.ds(WIDE, HALF)], v.local.at[10])
    )
    own_rows = pl.ds(pl.multiple_of(sample * 48, 16), 48)
    half_lanes = pl.ds(lane, HALF)
    loads.append(
        pltpu.make_async_copy(v.w_proj.at[:, half_lanes], proj.at[own_rows, half_lanes], v.local.at[11])
    )
    inputs = [
        pltpu.make_async_copy(v.images, v.stage, v.local.at[12]),
        pltpu.make_async_copy(v.cotangent, v.cot_stage, v.local.at[13]),
    ]
    for load in loads + inputs:
        load.start()

    def clear():
        spots[pl.ds(mine, BLOCK), :] = jnp.zeros((BLOCK, CHANS), BF16)
        spots[pl.ds(SPOTS, DEPTH - SPOTS), :] = jnp.zeros((DEPTH - SPOTS, CHANS), BF16)
        v.cols[pl.ds(SPOTS, DEPTH - SPOTS), :] = jnp.zeros((DEPTH - SPOTS, WIDE), BF16)
        v.cot[pl.ds(mine, BLOCK), :] = jnp.zeros((BLOCK, HALF), BF16)
        v.cot_send[...] = jnp.zeros_like(v.cot_send)

    greet([mate] + [z_peer(z, k) for k in range(1, 8)] + [sample_peer(sample, k) for k in range(1, 16)], clear)
    for load in loads:
        load.wait()

    later = []

    def early():
        for load in inputs:
            load.wait()
        for r in range(ROWS):
            spots[pl.ds(pl.multiple_of(mine + r * PITCH, 16), COLS), :] = v.stage[r]
        later.append(swap(spots.at[pl.ds(mine, BLOCK), :], spots.at[pl.ds(mine, BLOCK), :], 0))
        for r in range(ROWS):
            v.cot_send[pl.ds(r * PITCH, COLS), :] = v.cot_stage[r, :, pl.ds(other_lane, HALF)]
            v.cot[pl.ds(pl.multiple_of(mine + r * PITCH, 16), COLS), :] = v.cot_stage[r, :, pl.ds(lane, HALF)]
        later.append(swap(v.cot_send, v.cot.at[pl.ds(mine, BLOCK), :], 1))

    pools = []

    def late():
        later[0].wait_recv()

        def add_rows(i, total):
            return total + spots[pl.ds(pl.multiple_of(i * 16, 16), 16), :].astype(F32)

        sums = lax.fori_loop(0, SPOTS // 16, add_rows, jnp.zeros((16, CHANS), F32))
        v.pool_src[...] = jnp.sum(sums, axis=0, keepdims=True)
        pools.extend(
            push(v.pool_src, v.pool_slots.at[z], v.pool_send.at[k - 1], v.pool_recv.at[k - 1], z_peer(z, k))
            for k in range(1, 8)
        )
        v.pool_slots[z] = v.pool_src[...]

    def filler(n):
        def flip(k, carry):
            at = pl.ds(pl.multiple_of(k * SHARD, SHARD), SHARD)
            v.flipped[at, :] = spots[:, at].T
            return carry

        lax.fori_loop(2 * n, 2 * n + 2, flip, 0)

    ring_sent = ring_gather(full, y, x, v.gather_send, v.gather_recv, early, late, filler)

    proj_copies = [
        push(
            proj.at[own_rows, half_lanes], proj.at[own_rows, half_lanes],
            v.proj_send.at[k - 1], v.proj_recv.at[k - 1], sample_peer(sample, k),
        )
        for k in range(1, 16)
    ]

    def multiply(n, carry):
        product = jnp.dot(
            spots[pl.ds(0, SPOTS), :], full[:, pl.ds(n * FEAT if isinstance(n, int) else pl.multiple_of(n * FEAT, FEAT), FEAT)],
            preferred_element_type=F32,
        )
        v.taps[2 * n] = product[:, :HALF]
        v.taps[2 * n + 1] = product[:, HALF:]
        return carry

    def row_tap(r):
        first = 1 + 3 * (r + 1)
        return v.taps[first + 1] + moved(v.taps[first], -RATE, column) + moved(v.taps[first + 2], RATE, column)

    lax.fori_loop(0, 2, multiply, 0)
    v.outer[0] = row_tap(-1).astype(BF16)
    below = push(v.outer.at[0], v.halo.at[0], v.halo_send.at[0], v.halo_recv.at[0], z_peer(z, 2))
    lax.fori_loop(3, 5, multiply, 0)
    v.outer[1] = row_tap(1).astype(BF16)
    above = push(v.outer.at[1], v.halo.at[1], v.halo_send.at[1], v.halo_recv.at[1], z_peer(z, -2))
    multiply(2, 0)
    v.centre[...] = row_tap(0)
    keep = types.SimpleNamespace()

    def to_samples(src_of, slots, send, recv):
        return [
            push(
                src_of(lax.rem(sample + k, 16)), slots.at[sample], send.at[k - 1], recv.at[k - 1],
                sample_peer(sample, k),
            )
            for k in range(1, 16)
        ]


    def totals(i, rows, meanwhile):
        for k, row in enumerate(rows):
            v.ar_src[i, pl.ds(k, 1), :] = row
        copies = [
            push(v.ar_src.at[i], v.ar_z.at[i, z], v.z_send.at[i, k - 1], v.z_recv.at[i, k - 1], z_peer(z, k))
            for k in range(1, 8)
        ]
        v.ar_z[i, z] = v.ar_src[i]
        meanwhile[0]()
        for copy in copies:
            copy.wait()
        whole = jnp.sum(v.ar_z[i], axis=0)
        v.ar_mid[i] = whole
        copies = [
            push(
                v.ar_mid.at[i], v.ar_xy.at[i, sample], v.xy_send.at[i, k - 1], v.xy_recv.at[i, k - 1],
                sample_peer(sample, k),
            )
            for k in range(1, 16)
        ]
        v.ar_xy[i, sample] = whole
        meanwhile[1]()
        for copy in copies:
            copy.wait()
        total = jnp.sum(v.ar_xy[i], axis=0)
        return [whole[k : k + 1] for k in range(4)], [total[k : k + 1] for k in range(4)]

    def down(a):
        return jnp.sum(a, axis=0, keepdims=True)

    def finish(total, power):
        centre = total / TOTAL_AREA
        return centre, lax.rsqrt(power / TOTAL_AREA - centre * centre + EPSILON)

    def mean_of(both):
        return (jnp.sum(both[0]) + jnp.sum(both[1])) * (1.0 / FEAT)

    nothing = lambda: None
    below.wait()
    above.wait()
    point = v.taps[0]
    atrous = (
        v.centre[...]
        + jnp.where(z >= 2, v.halo[0].astype(F32), zero)
        + jnp.where(z < 6, v.halo[1].astype(F32), zero)
    )
    v.centre[...] = atrous

    def send_pools():
        for k in range(16):
            rows = keep.pooled[:, k * SHARD : (k + 1) * SHARD].astype(F32)
            v.pool_rows[k] = jnp.broadcast_to(rows, (8, SHARD))
        keep.pools = to_samples(lambda j: v.pool_rows.at[j], v.pool_all, v.pall_send, v.pall_recv)
        v.pool_all[sample] = v.pool_rows[sample]

    def image_product():
        for copy in pools:
            copy.wait()
        keep.pooled = (jnp.sum(v.pool_slots[...], axis=0) / SAMPLE_AREA).astype(BF16)
        image = jnp.dot(
            jnp.broadcast_to(keep.pooled, (16, CHANS)), full[:, pl.ds(WIDE, HALF)], preferred_element_type=F32
        )
        v.images_half[c] = image[0:8]
        later.append(swap(v.images_half.at[c], v.images_half.at[c], 2))
        for copy in proj_copies:
            copy.wait()
        later.append(swap(proj.at[:, half_lanes], proj.at[:, half_lanes], 8))

    def image_forward():
        later[-2].wait_recv()
        halves = [v.images_half[0][0:1], v.images_half[1][0:1]]
        image_mean = mean_of(halves)
        apart = [h - image_mean for h in halves]
        keep.layer_scale = lax.rsqrt(jnp.full((1, HALF), mean_of([a * a for a in apart]) + EPSILON, F32))
        keep.layer_norm = [a * keep.layer_scale for a in apart]
        keep.relu_image = jnp.concatenate([silu(a) for a in keep.layer_norm], axis=1).astype(BF16)
        later[-1].wait_recv()
        keep.image_row = jnp.dot(
            jnp.broadcast_to(keep.relu_image, (16, FEAT)),
            proj[pl.ds(2 * FEAT, FEAT), pl.ds(lane, HALF)],
            preferred_element_type=F32,
        )[0:1]

    _, (s0, s1, s2, s3) = totals(
        0, [down(point), down(point * point), down(atrous), down(atrous * atrous)], (image_product, image_forward)
    )
    centre_p, scale_p = finish(s0, s1)
    centre_a, scale_a = finish(s2, s3)
    v.norm_p[...] = (point - centre_p) * scale_p
    v.norm_a[...] = (v.centre[...] - centre_a) * scale_a
    relu = v.relu
    relu[c, :, pl.ds(0, HALF)] = jnp.where(inside, silu(v.norm_p[...]), 0.0).astype(BF16)
    relu[c, :, pl.ds(HALF, HALF)] = jnp.where(inside, silu(v.norm_a[...]), 0.0).astype(BF16)
    swap_relu = swap(relu.at[c], relu.at[c], 3)

    def mix_term(k):
        total = None
        for b in range(2):
            first = pl.multiple_of(k * HALF + b * FEAT, HALF)
            term = jnp.dot(
                relu[k, :, pl.ds(b * HALF, HALF)],
                proj[pl.ds(first, HALF), pl.ds(lane, HALF)],
                preferred_element_type=F32,
            )
            total = term if total is None else total + term
        return total

    mixed = mix_term(c) + keep.image_row
    swap_relu.wait()
    mixed = jnp.where(inside, mixed + mix_term(1 - c), 0.0)
    v.mixed[...] = mixed

    def to_rows(source, slots, k):
        return [
            push(source, slots.at[1], v.halo_send.at[k], v.halo_recv.at[k], z_peer(z, 2)),
            push(source, slots.at[0], v.halo_send.at[k + 1], v.halo_recv.at[k + 1], z_peer(z, -2)),
        ]

    def slope_point():
        v.norm_send[...] = v.norm_a[...].astype(BF16)
        keep.norms = to_rows(v.norm_send, v.norm_halo, 2)
        send_pools()
        v.slope_p[...] = silu_slope(v.norm_p[...])

    def slope_atrous():
        v.slope_a[...] = silu_slope(v.norm_a[...])

    blank = jnp.zeros((1, HALF), F32)
    (mixed_sample, _, _, _), (s0, s1, _, _) = totals(
        1, [down(mixed), down(mixed * mixed), blank, blank], (slope_point, slope_atrous)
    )
    centre_m, scale_m = finish(s0, s1)
    norm_mix = (v.mixed[...] - centre_m) * scale_m
    v.mixed[...] = norm_mix
    later[1].wait_recv()
    sigma = lax.logistic(norm_mix)
    upstream = jnp.where(inside, v.cot[...].astype(F32) * (sigma * (1.0 + norm_mix * (1.0 - sigma))), 0.0)
    v.upstream[...] = upstream

    def make_result():
        result = silu(v.mixed[...]).astype(BF16)
        v.result_send[0] = result[:BLOCK]
        v.result_send[1] = result[BLOCK:]
        keep.result = swap(v.result_send.at[1 - c], v.result_half, 4)

    def store_result():
        keep.result.wait_recv()
        for r in range(ROWS):
            rows = pl.ds(r * PITCH, COLS)
            v.out_result[r, :, pl.ds(lane, HALF)] = v.result_send[c, rows, :]
            v.out_result[r, :, pl.ds(other_lane, HALF)] = v.result_half[rows, :]

    (up_sample, _, _, _), (s0, s1, _, _) = totals(
        2, [down(upstream), down(upstream * norm_mix), blank, blank], (make_result, store_result)
    )
    mean_u = s0 / TOTAL_AREA
    mean_un = s1 / TOTAL_AREA
    grad_mix = jnp.where(inside, (v.upstream[...] - mean_u - v.mixed[...] * mean_un) * scale_m, 0.0)
    mix, columns = v.mix, v.columns
    mix[c] = grad_mix.astype(BF16)
    swap_mix = swap(mix.at[c], mix.at[c], 5)
    norm_sample = (mixed_sample - SAMPLE_AREA * centre_m) * scale_m
    column_total = (up_sample - SAMPLE_AREA * mean_u - mean_un * norm_sample) * scale_m
    columns[c] = jnp.broadcast_to(column_total, (8, HALF))
    swap_columns = swap(columns.at[c], columns.at[c], 6)

    def back_term(first, k):
        return lax.dot_general(
            mix[k],
            proj[pl.ds(pl.multiple_of(first + lane, HALF), HALF), pl.ds(pl.multiple_of(k * HALF, HALF), HALF)],
            (((1,), (1,)), ((), ())),
            preferred_element_type=F32,
        )

    back_p = back_term(0, c)
    back_a = back_term(FEAT, c)
    swap_mix.wait()
    up_point = (back_p + back_term(0, 1 - c)) * v.slope_p[...]
    up_atrous = (back_a + back_term(FEAT, 1 - c)) * v.slope_a[...]
    v.slope_p[...] = up_point
    v.slope_a[...] = up_atrous

    def image_backward():
        v.up_send[...] = v.slope_a[...].astype(BF16)
        keep.ups = to_rows(v.up_send, v.up_halo, 4)
        swap_columns.wait()
        column_b = jnp.concatenate([columns[0][0:1], columns[1][0:1]], axis=1).astype(BF16)
        back_image = lax.dot_general(
            jnp.broadcast_to(column_b, (16, FEAT)),
            proj[pl.ds(2 * FEAT, FEAT), :],
            (((1,), (1,)), ((), ())),
            preferred_element_type=F32,
        )
        layer_norm = keep.layer_norm
        up_image = [back_image[0:1, k * HALF : (k + 1) * HALF] * silu_slope(layer_norm[k]) for k in range(2)]
        mean_up = mean_of(up_image)
        mean_up_norm = mean_of([up_image[k] * layer_norm[k] for k in range(2)])
        image_grad = jnp.concatenate(
            [(up_image[k] - mean_up - layer_norm[k] * mean_up_norm) * keep.layer_scale for k in range(2)], axis=1
        )
        v.image_grad[...] = jnp.broadcast_to(image_grad.astype(BF16).astype(F32), (8, FEAT))
        keep.images = to_samples(lambda j: v.image_grad, v.image_all, v.image_send, v.image_recv)
        v.image_all[sample] = v.image_grad[...]

    def proj_gradient():
        for k in range(2):
            part = lax.dot_general(
                relu[k], mix[c], (((0,), (0,)), ((), ())), preferred_element_type=F32
            ) * FACTOR
            v.proj_part[pl.ds(k * HALF, HALF), :] = part[:HALF].astype(BF16)
            v.proj_part[pl.ds(FEAT + k * HALF, HALF), :] = part[HALF:].astype(BF16)
        once = lax.broadcasted_iota(jnp.int32, (16, FEAT), 0) == 0
        gate = jnp.where(z == 0, FACTOR, 0.0).astype(F32)
        outer = lax.dot_general(
            jnp.where(once, jnp.broadcast_to(keep.relu_image.astype(F32), (16, FEAT)), 0.0).astype(BF16),
            jnp.broadcast_to(columns[c][0:1], (16, HALF)).astype(BF16),
            (((0,), (0,)), ((), ())),
            preferred_element_type=F32,
        )
        v.proj_part[pl.ds(2 * FEAT, FEAT), :] = (outer * gate).astype(BF16)

    _, (s0, s1, s2, s3) = totals(
        3,
        [down(up_point), down(up_point * v.norm_p[...]), down(up_atrous), down(up_atrous * v.norm_a[...])],
        (image_backward, proj_gradient),
    )

    def back_norm(up, norm, first, second, scale):
        grad = (up - first / TOTAL_AREA - norm * (second / TOTAL_AREA)) * scale
        return jnp.where(inside, grad, 0.0)

    grad_atrous = back_norm(v.slope_a[...], v.norm_a[...], s2, s3, scale_a)
    grad_copies = [
        push(
            v.proj_part.at[pl.ds(pl.multiple_of(lax.rem(sample + k, 16) * 48, 16), 48), :], v.proj_slots.at[sample],
            v.pgrad_send.at[k - 1], v.pgrad_recv.at[k - 1], sample_peer(sample, k),
        )
        for k in range(1, 16)
    ]
    v.proj_slots[sample] = v.proj_part[own_rows, :]
    cols = v.cols
    cols[pl.ds(0, SPOTS), pl.ds(0, HALF)] = back_norm(v.slope_p[...], v.norm_p[...], s0, s1, scale_p).astype(BF16)

    def fill(r, source):
        for s in (-1, 0, 1):
            t = 1 + 3 * (r + 1) + (s + 1)
            cols[pl.ds(0, SPOTS), pl.ds(t * HALF, HALF)] = moved(source, -RATE * s, column).astype(BF16)

    fill(0, grad_atrous)
    for copy in keep.norms + keep.ups:
        copy.wait()

    def came_rows(k):
        return back_norm(v.up_halo[k].astype(F32), v.norm_halo[k].astype(F32), s2, s3, scale_a)

    fill(1, jnp.where(z >= 2, came_rows(1), zero))
    fill(-1, jnp.where(z < 6, came_rows(0), zero))

    partial, opposite, beside = v.partial, v.opposite, v.beside

    def weight_block(dy):
        base = lax.rem(y + dy + 4, 4) * 512

        def weight_part(k, carry):
            at = pl.ds(pl.multiple_of(base + k * FEAT, FEAT), FEAT)
            part = jnp.dot(v.flipped[at, :], cols[...], preferred_element_type=F32)
            partial[at, :] = (part * FACTOR).astype(BF16)
            return carry

        lax.fori_loop(0, 2, weight_part, 0)

    count = [0]
    done = []

    class Ring:
        def __init__(self, slot, axis, base, index):
            self.slot, self.axis, self.base, self.index = slot, axis, base, index

        def rows(self, o, start, size):
            return pl.ds(pl.multiple_of(self.index(o) * SHARD + self.base + start, 32), size)

        def put(self, src, dst, d):
            k = count[0]
            count[0] += 1
            copy = push(src, dst, v.ring_send.at[k], v.ring_recv.at[k], along(self.axis, y, x, d))
            done.append(copy)
            return copy

        def far(self):
            s = self.slot
            self.m0 = self.put(partial.at[self.rows(2, 0, 32), :], opposite.at[s, 0], 1)
            self.m1 = self.put(partial.at[self.rows(2, 32, 32), :], opposite.at[s, 1], -1)

        def near_up(self):
            self.m2 = self.put(partial.at[self.rows(1, 32, 32), :], beside.at[self.slot, 0, pl.ds(32, 32), :], 1)

        def near_down(self):
            self.m3 = self.put(partial.at[self.rows(-1, 0, 32), :], beside.at[self.slot, 1, pl.ds(0, 32), :], -1)

        def relay(self):
            s = self.slot
            self.m0.wait_recv()
            at = self.rows(1, 0, 32)
            partial[at, :] = (partial[at, :].astype(F32) + opposite[s, 0].astype(F32)).astype(BF16)
            self.m4 = self.put(partial.at[at, :], beside.at[s, 0, pl.ds(0, 32), :], 1)
            self.m1.wait_recv()
            at = self.rows(-1, 32, 32)
            partial[at, :] = (partial[at, :].astype(F32) + opposite[s, 1].astype(F32)).astype(BF16)
            self.m5 = self.put(partial.at[at, :], beside.at[s, 1, pl.ds(32, 32), :], -1)

        def close(self):
            s = self.slot
            for m in (self.m2, self.m3, self.m4, self.m5):
                m.wait_recv()
            at = self.rows(0, 0, 64)
            partial[at, :] = (
                partial[at, :].astype(F32) + beside[s, 0].astype(F32) + beside[s, 1].astype(F32)
            ).astype(BF16)

    def block(dy, dx):
        return lax.rem(y + dy + 4, 4) * 4 + lax.rem(x + dx + 4, 4)

    order = (2, 1, -1, 0)
    by_y = [Ring(n, "y", 0, functools.partial(lambda a, o: block(o, a), a)) for n, a in enumerate(order)]
    by_x = [Ring(4 + n, "x", 64, functools.partial(lambda a, o: block(a, o), a)) for n, a in enumerate(order)]
    last = [
        Ring(8, "x", 0, lambda o: block(0, o)),
        Ring(9, "y", 64, lambda o: block(o, 0)),
    ]
    for n, dy in enumerate(order):
        weight_block(dy)
        by_x[n].far()
        if dy == 2:
            for ring in by_y:
                ring.far()
        if dy == 1:
            for ring in by_y:
                ring.near_up()
        if dy == -1:
            for ring in by_y:
                ring.near_down()
        by_x[n].near_up()
        by_x[n].near_down()

    half_grad = v.image_grad[:, pl.ds(lane, HALF)]
    grad_rows = jnp.concatenate([half_grad, half_grad], axis=0).astype(BF16)

    def input_part(k, carry):
        at = pl.ds(pl.multiple_of(k * FEAT, FEAT), FEAT)
        part = lax.dot_general(
            cols[pl.ds(0, SPOTS), :], full[at, pl.ds(0, WIDE)], (((1,), (1,)), ((), ())), preferred_element_type=F32
        )
        pool = lax.dot_general(
            grad_rows, full[at, pl.ds(WIDE, HALF)], (((1,), (1,)), ((), ())), preferred_element_type=F32
        )[0:1] / SAMPLE_AREA
        part = part + pool
        v.pair[0] = part[:BLOCK]
        v.pair[1] = part[BLOCK:]
        v.own[k] = v.pair[c]
        v.away[k] = v.pair[1 - c].astype(BF16)
        return carry

    lax.fori_loop(0, 4, input_part, 0)
    for n in range(4):
        by_x[n].relay()
        by_y[n].relay()
    lax.fori_loop(4, 8, input_part, 0)
    swap_input = swap(v.away, v.came, 7)
    for n in range(4):
        by_y[n].close()
        by_x[n].close()
        if n == 0:
            for ring in last:
                ring.far()
        if n == 1:
            for ring in last:
                ring.near_up()
        if n == 2:
            for ring in last:
                ring.near_down()
    for ring in last:
        ring.relay()

    for copy in grad_copies:
        copy.wait()
    v.proj_sum[...] = jnp.sum(v.proj_slots[...].astype(F32), axis=0).astype(BF16)

    def to_levels(src, dst, send, recv):
        return [push(src, dst, send.at[k - 1], recv.at[k - 1], z_peer(z, k)) for k in range(1, 8)]

    spread = to_levels(v.proj_sum, v.proj_all.at[z], v.spread_send, v.spread_recv)
    v.proj_all[z] = v.proj_sum[...]

    for ring in last:
        ring.close()
    here = sample * SHARD
    z_copies = [
        push(
            partial.at[pl.ds(pl.multiple_of(here + lax.rem(z + k, 8) * 16, 16), 16), :],
            v.z_slots.at[z], v.zsum_send.at[k - 1], v.zsum_recv.at[k - 1], z_peer(z, k),
        )
        for k in range(1, 8)
    ]
    v.z_slots[z] = partial[pl.ds(pl.multiple_of(here + z * 16, 16), 16), :]

    swap_input.wait()
    for k in range(CHANS // FEAT):
        total = (v.own[k] + v.came[k].astype(F32)).astype(BF16)
        for r in range(ROWS):
            v.out_input[r, :, pl.ds(k * FEAT, FEAT)] = total[r * PITCH : r * PITCH + COLS]

    for copy in z_copies:
        copy.wait()
    v.z_sum[...] = jnp.sum(v.z_slots[...].astype(F32), axis=0).astype(BF16)
    my_rows = pl.ds(pl.multiple_of(z * 16, 16), 16)
    joined = v.joined
    all_copies = to_levels(v.z_sum, joined.at[c, my_rows, :], v.all_send, v.all_recv)
    joined[c, my_rows, :] = v.z_sum[...]

    for copy in keep.pools + keep.images:
        copy.wait()
    v.out_image[...] = (
        lax.dot_general(
            v.pool_all[...][:, 0, :].astype(BF16), v.image_all[...][:, 0, :].astype(BF16),
            (((0,), (0,)), ((), ())), preferred_element_type=F32,
        )
        * FACTOR
    )
    for copy in spread:
        copy.wait()
    v.proj_half[c] = jnp.sum(v.proj_all[...].astype(F32), axis=0)
    swap_proj = swap(v.proj_half.at[c], v.proj_half.at[c], 9)
    for copy in ring_sent + later + done:
        copy.wait_send()
    keep.result.wait_send()
    for copy in all_copies:
        copy.wait()
    swap_joined = swap(joined.at[c], joined.at[c], 10)

    def store(k):
        out = pl.ds(pl.multiple_of(k * HALF, HALF), HALF)
        v.out_point[:, out] = joined[k, :, pl.ds(0, HALF)].astype(F32)
        for t in range(9):
            out = pl.ds(pl.multiple_of(t * FEAT + k * HALF, HALF), HALF)
            v.out_atrous[:, out] = joined[k, :, pl.ds((t + 1) * HALF, HALF)].astype(F32)

    store(c)
    swap_proj.wait()
    for k in range(2):
        v.out_proj[:, pl.ds(k * HALF, HALF)] = v.proj_half[k]
    swap_joined.wait()
    store(1 - c)


def finish_kernel(*refs):
    ins, outs, rooms, (sems_in, sems_out) = refs[:6], refs[6:12], refs[12:18], refs[18:]
    arriving = [pltpu.make_async_copy(ins[k], rooms[k], sems_in.at[k]) for k in range(6)]
    leaving = [pltpu.make_async_copy(rooms[k], outs[k], sems_out.at[k]) for k in range(6)]
    for copy in arriving:
        copy.start()
    for k in range(6):
        arriving[k].wait()
        leaving[k].start()
    for copy in leaving:
        copy.wait()


VMEM = pl.BlockSpec(memory_space=pltpu.VMEM)
ANY = pl.BlockSpec(memory_space=pl.ANY)


def dma(*shape):
    return pltpu.SemaphoreType.DMA(shape)


def sized(dtype, *shape):
    return jax.ShapeDtypeStruct(shape, dtype)


ARGS = ("images", "w_point", "w_atrous", "w_image", "w_proj", "cotangent")
OUTS = (
    ("out_result", sized(BF16, ROWS, COLS, FEAT)),
    ("out_input", sized(BF16, ROWS, COLS, CHANS)),
    ("out_point", sized(F32, SHARD, FEAT)),
    ("out_atrous", sized(F32, SHARD, 9 * FEAT)),
    ("out_image", sized(F32, SHARD, FEAT)),
    ("out_proj", sized(F32, 48, FEAT)),
)
SCRATCH = (
    ("stage", (ROWS, COLS, CHANS), BF16),
    ("cot_stage", (ROWS, COLS, FEAT), BF16),
    ("spots", (DEPTH, CHANS), BF16),
    ("flipped", (CHANS, DEPTH), BF16),
    ("full", (CHANS, WIDER), BF16),
    ("proj", (3 * FEAT, FEAT), BF16),
    ("taps", (TAPS, SPOTS, HALF), F32),
    ("pool_src", (1, CHANS), F32),
    ("pool_slots", (8, 1, CHANS), F32),
    ("pool_rows", (16, 8, SHARD), F32),
    ("pool_all", (16, 8, SHARD), F32),
    ("image_grad", (8, FEAT), F32),
    ("image_all", (16, 8, FEAT), F32),
    ("images_half", (2, 8, HALF), F32),
    ("outer", (2, SPOTS, HALF), BF16),
    ("halo", (2, SPOTS, HALF), BF16),
    ("centre", (SPOTS, HALF), F32),
    ("norm_p", (SPOTS, HALF), F32),
    ("norm_a", (SPOTS, HALF), F32),
    ("slope_p", (SPOTS, HALF), F32),
    ("slope_a", (SPOTS, HALF), F32),
    ("mixed", (SPOTS, HALF), F32),
    ("upstream", (SPOTS, HALF), F32),
    ("relu", (2, SPOTS, FEAT), BF16),
    ("mix", (2, SPOTS, HALF), BF16),
    ("columns", (2, 8, HALF), F32),
    ("cot", (SPOTS, HALF), BF16),
    ("cot_send", (BLOCK, HALF), BF16),
    ("result_send", (2, BLOCK, HALF), BF16),
    ("result_half", (BLOCK, HALF), BF16),
    ("ar_src", (4, 4, HALF), F32),
    ("ar_mid", (4, 4, HALF), F32),
    ("ar_z", (4, 8, 4, HALF), F32),
    ("ar_xy", (4, 16, 4, HALF), F32),
    ("proj_part", (3 * FEAT, HALF), BF16),
    ("proj_slots", (16, 48, HALF), BF16),
    ("proj_sum", (48, HALF), BF16),
    ("proj_all", (8, 48, HALF), BF16),
    ("proj_half", (2, 48, HALF), F32),
    ("norm_send", (SPOTS, HALF), BF16),
    ("norm_halo", (2, SPOTS, HALF), BF16),
    ("up_send", (SPOTS, HALF), BF16),
    ("up_halo", (2, SPOTS, HALF), BF16),
    ("cols", (DEPTH, WIDE), BF16),
    ("partial", (CHANS, WIDE), BF16),
    ("opposite", (10, 2, 32, WIDE), BF16),
    ("beside", (10, 2, 64, WIDE), BF16),
    ("pair", (2, BLOCK, FEAT), F32),
    ("own", (8, BLOCK, FEAT), F32),
    ("away", (8, BLOCK, FEAT), BF16),
    ("came", (8, BLOCK, FEAT), BF16),
    ("z_slots", (8, 16, WIDE), BF16),
    ("z_sum", (16, WIDE), BF16),
    ("joined", (2, SHARD, WIDE), BF16),
)
SEMAPHORES = (
    ("local", (14,)),
    ("core", (11,)),
    ("gather", (40,)),
    ("proj", (15,)),
    ("pool", (7,)),
    ("pall", (15,)),
    ("image", (15,)),
    ("halo", (6,)),
    ("z", (4, 7)),
    ("xy", (4, 15)),
    ("pgrad", (15,)),
    ("ring", (60,)),
    ("zsum", (7,)),
    ("spread", (7,)),
    ("all", (7,)),
)


def on_device(images, w_point, w_atrous, w_image, w_proj, cotangent):
    names = list(ARGS) + [n for n, _ in OUTS] + [n for n, _, _ in SCRATCH]
    scratch = [pltpu.VMEM(shape, dtype) for _, shape, dtype in SCRATCH]
    for name, shape in SEMAPHORES:
        kinds = ("local",) if name == "local" else (name + "_send", name + "_recv")
        for kind in kinds:
            names.append(kind)
            scratch.append(dma(*shape))
    outs = pl.pallas_call(
        functools.partial(whole_kernel, tuple(names)),
        out_shape=[shape for _, shape in OUTS],
        in_specs=[ANY] * 6,
        out_specs=[VMEM] * 6,
        scratch_shapes=scratch,
        compiler_params=pltpu.CompilerParams(
            collective_id=0, has_side_effects=True, vmem_limit_bytes=60 << 20
        ),
        name="whole",
    )(images[0], w_point, w_atrous, w_image, w_proj, cotangent[0])
    outs = pl.pallas_call(
        finish_kernel,
        out_shape=[shape for _, shape in OUTS],
        in_specs=[ANY] * 6,
        out_specs=[ANY] * 6,
        scratch_shapes=[pltpu.VMEM(shape.shape, shape.dtype) for _, shape in OUTS] + [dma(6), dma(6)],
        compiler_params=pltpu.CompilerParams(vmem_limit_bytes=60 << 20),
        name="finish",
    )(*outs)
    return (outs[0][None], outs[1][None], *outs[2:])


def solution(mesh):
    finer = Mesh(mesh.devices.reshape(8, 2, 4, 4), STRIP + SAMPLE)
    placed = (
        P(SAMPLE, STRIP, None, None),
        P(SAMPLE, None),
        P(SAMPLE, None),
        P(SAMPLE, None),
        P(SAMPLE, None),
        P(SAMPLE, STRIP, None, None),
    )
    return jax.shard_map(
        on_device,
        mesh=finer,
        in_specs=placed,
        out_specs=(
            P(SAMPLE, STRIP, None, None),
            P(SAMPLE, STRIP, None, None),
            P(SAMPLE, None),
            P(SAMPLE, None),
            P(SAMPLE, None),
            P(SAMPLE, None),
        ),
        check_vma=False,
    )
```

```python
import functools
import types

import jax
import jax.numpy as jnp
from jax import lax
from jax.experimental import pallas as pl
from jax.experimental.pallas import tpu as pltpu
from jax.sharding import Mesh
from jax.sharding import PartitionSpec as P

RATE = 12
STRIP = ("strip_0", "strip_1")
SAMPLE = ("sample_0", "sample_1")
EPSILON = 1e-05
MESH_ID = pl.DeviceIdType.MESH
F32 = jnp.float32
BF16 = jnp.bfloat16

CHANS = 2048
FEAT = 256
HALF = 128
ROWS = 3
COLS = 108
PITCH = 112
BLOCK = ROWS * PITCH
SPOTS = 2 * BLOCK
DEPTH = 768
TAPS = 10
WIDE = TAPS * HALF
WIDER = WIDE + HALF
SHARD = 128
SAMPLE_AREA = 48.0 * 108.0
TOTAL_AREA = 16.0 * SAMPLE_AREA
FACTOR = 1.0 / 16.0


def places():
    return tuple(lax.axis_index(a) for a in STRIP + SAMPLE)


def z_peer(z, k):
    return {"strip_0": lax.rem(z + k + 8, 8)}


def other_core(c):
    return {"strip_1": 1 - c}


def along(axis, y, x, d):
    if axis == "x":
        return {"sample_1": lax.rem(x + d + 4, 4)}
    return {"sample_0": lax.rem(y + d + 4, 4)}


def sample_peer(me, k):
    other = lax.rem(me + k, 16)
    return {"sample_0": lax.div(other, 4), "sample_1": lax.rem(other, 4)}


def greet(peers, meanwhile):
    barrier = pltpu.get_barrier_semaphore()
    for peer in peers:
        pl.semaphore_signal(barrier, inc=1, device_id=peer, device_id_type=MESH_ID)
    meanwhile()
    pl.semaphore_wait(barrier, len(peers))


def push(src, dst, send, recv, peer):
    copy = pltpu.make_async_remote_copy(
        src_ref=src,
        dst_ref=dst,
        send_sem=send,
        recv_sem=recv,
        device_id=peer,
        device_id_type=MESH_ID,
    )
    copy.start()
    return copy


def spot_column(shape):
    full = lax.broadcasted_iota(jnp.int32, (shape[0] // PITCH, PITCH, shape[1]), 1)
    return full.reshape(shape)


def moved(values, offset, column):
    if offset == 0:
        return values
    spots = values.shape[0]
    if offset > 0:
        return jnp.where(column < COLS - offset, pltpu.roll(values, spots - offset, 0), 0.0)
    inside = (column >= -offset) & (column < COLS)
    return jnp.where(inside, pltpu.roll(values, -offset, 0), 0.0)


def ring_gather(full, z, y, x, sems, early, late, filler):
    send, recv, level_send, level_recv = sems
    count = [0, 0]
    sent, levels = [], []
    odd = lax.rem(z, 2)
    lanes = pl.ds(pl.multiple_of(odd * FEAT, FEAT), 4 * FEAT)
    lent = pl.ds(pl.multiple_of(odd * 4 * FEAT, FEAT), FEAT)
    partner = {"strip_0": z + 1 - 2 * odd}

    def row_of(kind, a, b):
        if kind == 0:
            return lax.rem(y + b + 4, 4) * 4 + lax.rem(x + a + 4, 4)
        return lax.rem(y + a + 4, 4) * 4 + lax.rem(x + b + 4, 4)

    def put(kind, a, b, part, first, d):
        axis = "x" if first == (kind == 0) else "y"
        start, size = ((0, 64), (0, 32), (32, 32))[part]
        rows = pl.ds(pl.multiple_of(row_of(kind, a, b) * SHARD + kind * 64 + start, 32), size)
        k = count[0]
        count[0] += 1
        copy = push(full.at[rows, lanes], full.at[rows, lanes], send.at[k], recv.at[k], along(axis, y, x, d))
        sent.append(copy)
        return copy

    def lend(kind, a, b):
        rows = pl.ds(pl.multiple_of(row_of(kind, a, b) * SHARD + kind * 64, 64), 64)
        k = count[1]
        count[1] += 1
        levels.append(push(full.at[rows, lent], full.at[rows, lent], level_send.at[k], level_recv.at[k], partner))

    kinds = (0, 1)
    right, left, up, down = {}, {}, {}, {}
    fr, fl, fu, fd = {}, {}, {}, {}

    def spread(kind, a):
        up[kind, a] = put(kind, a, 0, 0, False, 1)
        down[kind, a] = put(kind, a, 0, 0, False, -1)

    def relay(kind, a):
        up[kind, a].wait_recv()
        fu[kind, a] = put(kind, a, -1, 1, False, 1)
        down[kind, a].wait_recv()
        fd[kind, a] = put(kind, a, 1, 2, False, -1)
        lend(kind, a, -1)
        lend(kind, a, 1)

    def close(a):
        for kind in kinds:
            fu[kind, a].wait_recv()
            fd[kind, a].wait_recv()
            lend(kind, a, 2)

    for kind in kinds:
        right[kind] = put(kind, 0, 0, 0, True, 1)
        left[kind] = put(kind, 0, 0, 0, True, -1)
    for kind in kinds:
        spread(kind, 0)
    early()
    for kind in kinds:
        right[kind].wait_recv()
        fr[kind] = put(kind, -1, 0, 1, True, 1)
        left[kind].wait_recv()
        fl[kind] = put(kind, 1, 0, 2, True, -1)
    for kind in kinds:
        spread(kind, -1)
        spread(kind, 1)
        lend(kind, -1, 0)
        lend(kind, 1, 0)
    for kind in kinds:
        relay(kind, 0)
    late()
    for kind in kinds:
        fr[kind].wait_recv()
        fl[kind].wait_recv()
        spread(kind, 2)
        lend(kind, 2, 0)
        filler(kind)
    for n, a in enumerate((-1, 1, 2)):
        for kind in kinds:
            relay(kind, a)
            filler(2 + 2 * n + kind)
        close((0, -1, 1)[n])
    close(2)
    for copy in levels:
        copy.wait_recv()
    return sent + levels


def silu(v):
    return v * lax.logistic(v)


def silu_slope(v):
    s = lax.logistic(v)
    return s * (1.0 + v * (1.0 - s))


def whole_kernel(names, *refs):
    v = types.SimpleNamespace(**dict(zip(names, refs)))
    z, c, y, x = places()
    sample = y * 4 + x
    mate = other_core(c)
    mine = pl.multiple_of(c * BLOCK, 16)
    lane = pl.multiple_of(c * HALF, HALF)
    other_lane = pl.multiple_of((1 - c) * HALF, HALF)
    column = spot_column((SPOTS, HALF))
    inside = column < COLS
    zero = jnp.zeros((SPOTS, HALF), F32)

    def swap(src, dst, k):
        return push(src, dst, v.core_send.at[k], v.core_recv.at[k], mate)

    full, spots, proj = v.full, v.spots, v.proj
    shard = pl.ds(pl.multiple_of(sample * SHARD, SHARD), SHARD)
    loads = [pltpu.make_async_copy(v.w_point.at[:, pl.ds(lane, HALF)], full.at[shard, pl.ds(0, HALF)], v.local.at[0])]
    for t in range(9):
        loads.append(
            pltpu.make_async_copy(
                v.w_atrous.at[:, pl.ds(pl.multiple_of(t * FEAT + lane, HALF), HALF)],
                full.at[shard, pl.ds((t + 1) * HALF, HALF)],
                v.local.at[t + 1],
            )
        )
    loads.append(
        pltpu.make_async_copy(v.w_image.at[:, pl.ds(lane, HALF)], full.at[shard, pl.ds(WIDE, HALF)], v.local.at[10])
    )
    own_rows = pl.ds(pl.multiple_of(sample * 48, 16), 48)
    half_lanes = pl.ds(lane, HALF)
    loads.append(
        pltpu.make_async_copy(v.w_proj.at[:, half_lanes], proj.at[own_rows, half_lanes], v.local.at[11])
    )
    inputs = [
        pltpu.make_async_copy(v.images, v.stage, v.local.at[12]),
        pltpu.make_async_copy(v.cotangent, v.cot_stage, v.local.at[13]),
    ]
    for load in loads + inputs:
        load.start()

    def clear():
        spots[pl.ds(mine, BLOCK), :] = jnp.zeros((BLOCK, CHANS), BF16)
        spots[pl.ds(SPOTS, DEPTH - SPOTS), :] = jnp.zeros((DEPTH - SPOTS, CHANS), BF16)
        v.cols[pl.ds(SPOTS, DEPTH - SPOTS), :] = jnp.zeros((DEPTH - SPOTS, WIDE), BF16)
        v.cot[pl.ds(mine, BLOCK), :] = jnp.zeros((BLOCK, HALF), BF16)
        v.cot_send[...] = jnp.zeros_like(v.cot_send)

    greet([mate] + [z_peer(z, k) for k in range(1, 8)] + [sample_peer(sample, k) for k in range(1, 16)], clear)
    for load in loads:
        load.wait()

    later = []

    def early():
        for load in inputs:
            load.wait()
        for r in range(ROWS):
            spots[pl.ds(pl.multiple_of(mine + r * PITCH, 16), COLS), :] = v.stage[r]
        later.append(swap(spots.at[pl.ds(mine, BLOCK), :], spots.at[pl.ds(mine, BLOCK), :], 0))
        for r in range(ROWS):
            v.cot_send[pl.ds(r * PITCH, COLS), :] = v.cot_stage[r, :, pl.ds(other_lane, HALF)]
            v.cot[pl.ds(pl.multiple_of(mine + r * PITCH, 16), COLS), :] = v.cot_stage[r, :, pl.ds(lane, HALF)]
        later.append(swap(v.cot_send, v.cot.at[pl.ds(mine, BLOCK), :], 1))

    pools = []

    def late():
        later[0].wait_recv()

        def add_rows(i, total):
            return total + spots[pl.ds(pl.multiple_of(i * 16, 16), 16), :].astype(F32)

        sums = lax.fori_loop(0, SPOTS // 16, add_rows, jnp.zeros((16, CHANS), F32))
        v.pool_src[...] = jnp.sum(sums, axis=0, keepdims=True)
        pools.extend(
            push(v.pool_src, v.pool_slots.at[z], v.pool_send.at[k - 1], v.pool_recv.at[k - 1], z_peer(z, k))
            for k in range(1, 8)
        )
        v.pool_slots[z] = v.pool_src[...]

    def filler(n):
        def flip(k, carry):
            at = pl.ds(pl.multiple_of(k * SHARD, SHARD), SHARD)
            v.flipped[at, :] = spots[:, at].T
            return carry

        lax.fori_loop(2 * n, 2 * n + 2, flip, 0)

    ring_sems = (v.gather_send, v.gather_recv, v.level_send, v.level_recv)
    ring_sent = ring_gather(full, z, y, x, ring_sems, early, late, filler)
    image_part = full.at[shard, pl.ds(WIDE, HALF)]
    image_copies = [
        push(image_part, image_part, v.wimage_send.at[k - 1], v.wimage_recv.at[k - 1], sample_peer(sample, k))
        for k in range(1, 16)
    ]

    proj_copies = [
        push(
            proj.at[own_rows, half_lanes], proj.at[own_rows, half_lanes],
            v.proj_send.at[k - 1], v.proj_recv.at[k - 1], sample_peer(sample, k),
        )
        for k in range(1, 16)
    ]

    def multiply(n, carry):
        product = jnp.dot(
            spots[pl.ds(0, SPOTS), :], full[:, pl.ds(n * FEAT if isinstance(n, int) else pl.multiple_of(n * FEAT, FEAT), FEAT)],
            preferred_element_type=F32,
        )
        v.taps[2 * n] = product[:, :HALF]
        v.taps[2 * n + 1] = product[:, HALF:]
        return carry

    def row_tap(r):
        first = 1 + 3 * (r + 1)
        return v.taps[first + 1] + moved(v.taps[first], -RATE, column) + moved(v.taps[first + 2], RATE, column)

    lax.fori_loop(0, 2, multiply, 0)
    v.outer[0] = row_tap(-1).astype(BF16)
    below = push(v.outer.at[0], v.halo.at[0], v.halo_send.at[0], v.halo_recv.at[0], z_peer(z, 2))
    lax.fori_loop(3, 5, multiply, 0)
    v.outer[1] = row_tap(1).astype(BF16)
    above = push(v.outer.at[1], v.halo.at[1], v.halo_send.at[1], v.halo_recv.at[1], z_peer(z, -2))
    multiply(2, 0)
    v.centre[...] = row_tap(0)
    keep = types.SimpleNamespace()

    def to_samples(src_of, slots, send, recv):
        return [
            push(
                src_of(lax.rem(sample + k, 16)), slots.at[sample], send.at[k - 1], recv.at[k - 1],
                sample_peer(sample, k),
            )
            for k in range(1, 16)
        ]


    def totals(i, rows, meanwhile):
        for k, row in enumerate(rows):
            v.ar_src[i, pl.ds(k, 1), :] = row
        copies = [
            push(v.ar_src.at[i], v.ar_z.at[i, z], v.z_send.at[i, k - 1], v.z_recv.at[i, k - 1], z_peer(z, k))
            for k in range(1, 8)
        ]
        v.ar_z[i, z] = v.ar_src[i]
        meanwhile[0]()
        for copy in copies:
            copy.wait()
        whole = jnp.sum(v.ar_z[i], axis=0)
        v.ar_mid[i] = whole
        copies = [
            push(
                v.ar_mid.at[i], v.ar_xy.at[i, sample], v.xy_send.at[i, k - 1], v.xy_recv.at[i, k - 1],
                sample_peer(sample, k),
            )
            for k in range(1, 16)
        ]
        v.ar_xy[i, sample] = whole
        meanwhile[1]()
        for copy in copies:
            copy.wait()
        total = jnp.sum(v.ar_xy[i], axis=0)
        return [whole[k : k + 1] for k in range(4)], [total[k : k + 1] for k in range(4)]

    def down(a):
        return jnp.sum(a, axis=0, keepdims=True)

    def finish(total, power):
        centre = total / TOTAL_AREA
        return centre, lax.rsqrt(power / TOTAL_AREA - centre * centre + EPSILON)

    def mean_of(both):
        return (jnp.sum(both[0]) + jnp.sum(both[1])) * (1.0 / FEAT)

    nothing = lambda: None
    below.wait()
    above.wait()
    point = v.taps[0]
    atrous = (
        v.centre[...]
        + jnp.where(z >= 2, v.halo[0].astype(F32), zero)
        + jnp.where(z < 6, v.halo[1].astype(F32), zero)
    )
    v.centre[...] = atrous

    def send_pools():
        for k in range(16):
            rows = keep.pooled[:, k * SHARD : (k + 1) * SHARD].astype(F32)
            v.pool_rows[k] = jnp.broadcast_to(rows, (8, SHARD))
        keep.pools = to_samples(lambda j: v.pool_rows.at[j], v.pool_all, v.pall_send, v.pall_recv)
        v.pool_all[sample] = v.pool_rows[sample]

    def image_product():
        for copy in pools + image_copies:
            copy.wait()
        keep.pooled = (jnp.sum(v.pool_slots[...], axis=0) / SAMPLE_AREA).astype(BF16)
        image = jnp.dot(
            jnp.broadcast_to(keep.pooled, (16, CHANS)), full[:, pl.ds(WIDE, HALF)], preferred_element_type=F32
        )
        v.images_half[c] = image[0:8]
        later.append(swap(v.images_half.at[c], v.images_half.at[c], 2))
        for copy in proj_copies:
            copy.wait()
        later.append(swap(proj.at[:, half_lanes], proj.at[:, half_lanes], 8))

    def image_forward():
        later[-2].wait_recv()
        halves = [v.images_half[0][0:1], v.images_half[1][0:1]]
        image_mean = mean_of(halves)
        apart = [h - image_mean for h in halves]
        keep.layer_scale = lax.rsqrt(jnp.full((1, HALF), mean_of([a * a for a in apart]) + EPSILON, F32))
        keep.layer_norm = [a * keep.layer_scale for a in apart]
        keep.relu_image = jnp.concatenate([silu(a) for a in keep.layer_norm], axis=1).astype(BF16)
        later[-1].wait_recv()
        keep.image_row = jnp.dot(
            jnp.broadcast_to(keep.relu_image, (16, FEAT)),
            proj[pl.ds(2 * FEAT, FEAT), pl.ds(lane, HALF)],
            preferred_element_type=F32,
        )[0:1]

    _, (s0, s1, s2, s3) = totals(
        0, [down(point), down(point * point), down(atrous), down(atrous * atrous)], (image_product, image_forward)
    )
    centre_p, scale_p = finish(s0, s1)
    centre_a, scale_a = finish(s2, s3)
    v.norm_p[...] = (point - centre_p) * scale_p
    v.norm_a[...] = (v.centre[...] - centre_a) * scale_a
    relu = v.relu
    relu[c, :, pl.ds(0, HALF)] = jnp.where(inside, silu(v.norm_p[...]), 0.0).astype(BF16)
    relu[c, :, pl.ds(HALF, HALF)] = jnp.where(inside, silu(v.norm_a[...]), 0.0).astype(BF16)
    swap_relu = swap(relu.at[c], relu.at[c], 3)

    def mix_term(k):
        total = None
        for b in range(2):
            first = pl.multiple_of(k * HALF + b * FEAT, HALF)
            term = jnp.dot(
                relu[k, :, pl.ds(b * HALF, HALF)],
                proj[pl.ds(first, HALF), pl.ds(lane, HALF)],
                preferred_element_type=F32,
            )
            total = term if total is None else total + term
        return total

    mixed = mix_term(c) + keep.image_row
    swap_relu.wait()
    mixed = jnp.where(inside, mixed + mix_term(1 - c), 0.0)
    v.mixed[...] = mixed

    def to_rows(source, slots, k):
        return [
            push(source, slots.at[1], v.halo_send.at[k], v.halo_recv.at[k], z_peer(z, 2)),
            push(source, slots.at[0], v.halo_send.at[k + 1], v.halo_recv.at[k + 1], z_peer(z, -2)),
        ]

    def slope_point():
        v.norm_send[...] = v.norm_a[...].astype(BF16)
        keep.norms = to_rows(v.norm_send, v.norm_halo, 2)
        send_pools()
        v.slope_p[...] = silu_slope(v.norm_p[...])

    def slope_atrous():
        v.slope_a[...] = silu_slope(v.norm_a[...])

    blank = jnp.zeros((1, HALF), F32)
    (mixed_sample, _, _, _), (s0, s1, _, _) = totals(
        1, [down(mixed), down(mixed * mixed), blank, blank], (slope_point, slope_atrous)
    )
    centre_m, scale_m = finish(s0, s1)
    norm_mix = (v.mixed[...] - centre_m) * scale_m
    v.mixed[...] = norm_mix
    later[1].wait_recv()
    sigma = lax.logistic(norm_mix)
    upstream = jnp.where(inside, v.cot[...].astype(F32) * (sigma * (1.0 + norm_mix * (1.0 - sigma))), 0.0)
    v.upstream[...] = upstream

    def make_result():
        result = silu(v.mixed[...]).astype(BF16)
        v.result_send[0] = result[:BLOCK]
        v.result_send[1] = result[BLOCK:]
        keep.result = swap(v.result_send.at[1 - c], v.result_half, 4)

    def store_result():
        keep.result.wait_recv()
        for r in range(ROWS):
            rows = pl.ds(r * PITCH, COLS)
            v.out_result[r, :, pl.ds(lane, HALF)] = v.result_send[c, rows, :]
            v.out_result[r, :, pl.ds(other_lane, HALF)] = v.result_half[rows, :]

    (up_sample, _, _, _), (s0, s1, _, _) = totals(
        2, [down(upstream), down(upstream * norm_mix), blank, blank], (make_result, store_result)
    )
    mean_u = s0 / TOTAL_AREA
    mean_un = s1 / TOTAL_AREA
    grad_mix = jnp.where(inside, (v.upstream[...] - mean_u - v.mixed[...] * mean_un) * scale_m, 0.0)
    mix, columns = v.mix, v.columns
    mix[c] = grad_mix.astype(BF16)
    swap_mix = swap(mix.at[c], mix.at[c], 5)
    norm_sample = (mixed_sample - SAMPLE_AREA * centre_m) * scale_m
    column_total = (up_sample - SAMPLE_AREA * mean_u - mean_un * norm_sample) * scale_m
    columns[c] = jnp.broadcast_to(column_total, (8, HALF))
    swap_columns = swap(columns.at[c], columns.at[c], 6)

    def back_term(first, k):
        return lax.dot_general(
            mix[k],
            proj[pl.ds(pl.multiple_of(first + lane, HALF), HALF), pl.ds(pl.multiple_of(k * HALF, HALF), HALF)],
            (((1,), (1,)), ((), ())),
            preferred_element_type=F32,
        )

    back_p = back_term(0, c)
    back_a = back_term(FEAT, c)
    swap_mix.wait()
    up_point = (back_p + back_term(0, 1 - c)) * v.slope_p[...]
    up_atrous = (back_a + back_term(FEAT, 1 - c)) * v.slope_a[...]
    v.slope_p[...] = up_point
    v.slope_a[...] = up_atrous

    def image_backward():
        v.up_send[...] = v.slope_a[...].astype(BF16)
        keep.ups = to_rows(v.up_send, v.up_halo, 4)
        swap_columns.wait()
        column_b = jnp.concatenate([columns[0][0:1], columns[1][0:1]], axis=1).astype(BF16)
        back_image = lax.dot_general(
            jnp.broadcast_to(column_b, (16, FEAT)),
            proj[pl.ds(2 * FEAT, FEAT), :],
            (((1,), (1,)), ((), ())),
            preferred_element_type=F32,
        )
        layer_norm = keep.layer_norm
        up_image = [back_image[0:1, k * HALF : (k + 1) * HALF] * silu_slope(layer_norm[k]) for k in range(2)]
        mean_up = mean_of(up_image)
        mean_up_norm = mean_of([up_image[k] * layer_norm[k] for k in range(2)])
        image_grad = jnp.concatenate(
            [(up_image[k] - mean_up - layer_norm[k] * mean_up_norm) * keep.layer_scale for k in range(2)], axis=1
        )
        v.image_grad[...] = jnp.broadcast_to(image_grad.astype(BF16).astype(F32), (8, FEAT))
        keep.images = to_samples(lambda j: v.image_grad, v.image_all, v.image_send, v.image_recv)
        v.image_all[sample] = v.image_grad[...]

    def proj_gradient():
        for k in range(2):
            part = lax.dot_general(
                relu[k], mix[c], (((0,), (0,)), ((), ())), preferred_element_type=F32
            ) * FACTOR
            v.proj_part[pl.ds(k * HALF, HALF), :] = part[:HALF].astype(BF16)
            v.proj_part[pl.ds(FEAT + k * HALF, HALF), :] = part[HALF:].astype(BF16)
        once = lax.broadcasted_iota(jnp.int32, (16, FEAT), 0) == 0
        gate = jnp.where(z == 0, FACTOR, 0.0).astype(F32)
        outer = lax.dot_general(
            jnp.where(once, jnp.broadcast_to(keep.relu_image.astype(F32), (16, FEAT)), 0.0).astype(BF16),
            jnp.broadcast_to(columns[c][0:1], (16, HALF)).astype(BF16),
            (((0,), (0,)), ((), ())),
            preferred_element_type=F32,
        )
        v.proj_part[pl.ds(2 * FEAT, FEAT), :] = (outer * gate).astype(BF16)

    _, (s0, s1, s2, s3) = totals(
        3,
        [down(up_point), down(up_point * v.norm_p[...]), down(up_atrous), down(up_atrous * v.norm_a[...])],
        (image_backward, proj_gradient),
    )

    def back_norm(up, norm, first, second, scale):
        grad = (up - first / TOTAL_AREA - norm * (second / TOTAL_AREA)) * scale
        return jnp.where(inside, grad, 0.0)

    grad_atrous = back_norm(v.slope_a[...], v.norm_a[...], s2, s3, scale_a)
    grad_copies = [
        push(
            v.proj_part.at[pl.ds(pl.multiple_of(lax.rem(sample + k, 16) * 48, 16), 48), :], v.proj_slots.at[sample],
            v.pgrad_send.at[k - 1], v.pgrad_recv.at[k - 1], sample_peer(sample, k),
        )
        for k in range(1, 16)
    ]
    v.proj_slots[sample] = v.proj_part[own_rows, :]
    cols = v.cols
    cols[pl.ds(0, SPOTS), pl.ds(0, HALF)] = back_norm(v.slope_p[...], v.norm_p[...], s0, s1, scale_p).astype(BF16)

    def fill(r, source):
        for s in (-1, 0, 1):
            t = 1 + 3 * (r + 1) + (s + 1)
            cols[pl.ds(0, SPOTS), pl.ds(t * HALF, HALF)] = moved(source, -RATE * s, column).astype(BF16)

    fill(0, grad_atrous)
    for copy in keep.norms + keep.ups:
        copy.wait()

    def came_rows(k):
        return back_norm(v.up_halo[k].astype(F32), v.norm_halo[k].astype(F32), s2, s3, scale_a)

    fill(1, jnp.where(z >= 2, came_rows(1), zero))
    fill(-1, jnp.where(z < 6, came_rows(0), zero))

    partial, opposite, beside = v.partial, v.opposite, v.beside

    def weight_block(dy):
        base = lax.rem(y + dy + 4, 4) * 512

        def weight_part(k, carry):
            at = pl.ds(pl.multiple_of(base + k * FEAT, FEAT), FEAT)
            part = jnp.dot(v.flipped[at, :], cols[...], preferred_element_type=F32)
            partial[at, :] = (part * FACTOR).astype(BF16)
            return carry

        lax.fori_loop(0, 2, weight_part, 0)

    count = [0]
    done = []

    class Ring:
        def __init__(self, slot, axis, base, index):
            self.slot, self.axis, self.base, self.index = slot, axis, base, index

        def rows(self, o, start, size):
            return pl.ds(pl.multiple_of(self.index(o) * SHARD + self.base + start, 32), size)

        def put(self, src, dst, d):
            k = count[0]
            count[0] += 1
            copy = push(src, dst, v.ring_send.at[k], v.ring_recv.at[k], along(self.axis, y, x, d))
            done.append(copy)
            return copy

        def far(self):
            s = self.slot
            self.m0 = self.put(partial.at[self.rows(2, 0, 32), :], opposite.at[s, 0], 1)
            self.m1 = self.put(partial.at[self.rows(2, 32, 32), :], opposite.at[s, 1], -1)

        def near_up(self):
            self.m2 = self.put(partial.at[self.rows(1, 32, 32), :], beside.at[self.slot, 0, pl.ds(32, 32), :], 1)

        def near_down(self):
            self.m3 = self.put(partial.at[self.rows(-1, 0, 32), :], beside.at[self.slot, 1, pl.ds(0, 32), :], -1)

        def relay(self):
            s = self.slot
            self.m0.wait_recv()
            at = self.rows(1, 0, 32)
            partial[at, :] = (partial[at, :].astype(F32) + opposite[s, 0].astype(F32)).astype(BF16)
            self.m4 = self.put(partial.at[at, :], beside.at[s, 0, pl.ds(0, 32), :], 1)
            self.m1.wait_recv()
            at = self.rows(-1, 32, 32)
            partial[at, :] = (partial[at, :].astype(F32) + opposite[s, 1].astype(F32)).astype(BF16)
            self.m5 = self.put(partial.at[at, :], beside.at[s, 1, pl.ds(32, 32), :], -1)

        def close(self):
            s = self.slot
            for m in (self.m2, self.m3, self.m4, self.m5):
                m.wait_recv()
            at = self.rows(0, 0, 64)
            partial[at, :] = (
                partial[at, :].astype(F32) + beside[s, 0].astype(F32) + beside[s, 1].astype(F32)
            ).astype(BF16)

    def block(dy, dx):
        return lax.rem(y + dy + 4, 4) * 4 + lax.rem(x + dx + 4, 4)

    order = (2, 1, -1, 0)
    by_y = [Ring(n, "y", 0, functools.partial(lambda a, o: block(o, a), a)) for n, a in enumerate(order)]
    by_x = [Ring(4 + n, "x", 64, functools.partial(lambda a, o: block(a, o), a)) for n, a in enumerate(order)]
    last = [
        Ring(8, "x", 0, lambda o: block(0, o)),
        Ring(9, "y", 64, lambda o: block(o, 0)),
    ]
    for n, dy in enumerate(order):
        weight_block(dy)
        by_x[n].far()
        if dy == 2:
            for ring in by_y:
                ring.far()
        if dy == 1:
            for ring in by_y:
                ring.near_up()
        if dy == -1:
            for ring in by_y:
                ring.near_down()
        by_x[n].near_up()
        by_x[n].near_down()

    half_grad = v.image_grad[:, pl.ds(lane, HALF)]
    grad_rows = jnp.concatenate([half_grad, half_grad], axis=0).astype(BF16)

    def input_part(k, carry):
        at = pl.ds(pl.multiple_of(k * FEAT, FEAT), FEAT)
        part = lax.dot_general(
            cols[pl.ds(0, SPOTS), :], full[at, pl.ds(0, WIDE)], (((1,), (1,)), ((), ())), preferred_element_type=F32
        )
        pool = lax.dot_general(
            grad_rows, full[at, pl.ds(WIDE, HALF)], (((1,), (1,)), ((), ())), preferred_element_type=F32
        )[0:1] / SAMPLE_AREA
        part = part + pool
        v.pair[0] = part[:BLOCK]
        v.pair[1] = part[BLOCK:]
        v.own[k] = v.pair[c]
        v.away[k] = v.pair[1 - c].astype(BF16)
        return carry

    lax.fori_loop(0, 4, input_part, 0)
    for n in range(4):
        by_x[n].relay()
        by_y[n].relay()
    lax.fori_loop(4, 8, input_part, 0)
    swap_input = swap(v.away, v.came, 7)
    for n in range(4):
        by_y[n].close()
        by_x[n].close()
        if n == 0:
            for ring in last:
                ring.far()
        if n == 1:
            for ring in last:
                ring.near_up()
        if n == 2:
            for ring in last:
                ring.near_down()
    for ring in last:
        ring.relay()

    for copy in grad_copies:
        copy.wait()
    v.proj_sum[...] = jnp.sum(v.proj_slots[...].astype(F32), axis=0).astype(BF16)

    def to_levels(src, dst, send, recv):
        return [push(src, dst, send.at[k - 1], recv.at[k - 1], z_peer(z, k)) for k in range(1, 8)]

    spread = to_levels(v.proj_sum, v.proj_all.at[z], v.spread_send, v.spread_recv)
    v.proj_all[z] = v.proj_sum[...]

    for ring in last:
        ring.close()
    here = sample * SHARD
    z_copies = [
        push(
            partial.at[pl.ds(pl.multiple_of(here + lax.rem(z + k, 8) * 16, 16), 16), :],
            v.z_slots.at[z], v.zsum_send.at[k - 1], v.zsum_recv.at[k - 1], z_peer(z, k),
        )
        for k in range(1, 8)
    ]
    v.z_slots[z] = partial[pl.ds(pl.multiple_of(here + z * 16, 16), 16), :]

    swap_input.wait()
    for k in range(CHANS // FEAT):
        total = (v.own[k] + v.came[k].astype(F32)).astype(BF16)
        for r in range(ROWS):
            v.out_input[r, :, pl.ds(k * FEAT, FEAT)] = total[r * PITCH : r * PITCH + COLS]

    for copy in z_copies:
        copy.wait()
    v.z_sum[...] = jnp.sum(v.z_slots[...].astype(F32), axis=0).astype(BF16)
    my_rows = pl.ds(pl.multiple_of(z * 16, 16), 16)
    joined = v.joined
    all_copies = to_levels(v.z_sum, joined.at[c, my_rows, :], v.all_send, v.all_recv)
    joined[c, my_rows, :] = v.z_sum[...]

    for copy in keep.pools + keep.images:
        copy.wait()
    v.out_image[...] = (
        lax.dot_general(
            v.pool_all[...][:, 0, :].astype(BF16), v.image_all[...][:, 0, :].astype(BF16),
            (((0,), (0,)), ((), ())), preferred_element_type=F32,
        )
        * FACTOR
    )
    for copy in spread:
        copy.wait()
    v.proj_half[c] = jnp.sum(v.proj_all[...].astype(F32), axis=0)
    swap_proj = swap(v.proj_half.at[c], v.proj_half.at[c], 9)
    for copy in ring_sent + later + done:
        copy.wait_send()
    keep.result.wait_send()
    for copy in all_copies:
        copy.wait()
    swap_joined = swap(joined.at[c], joined.at[c], 10)

    def store(k):
        out = pl.ds(pl.multiple_of(k * HALF, HALF), HALF)
        v.out_point[:, out] = joined[k, :, pl.ds(0, HALF)].astype(F32)
        for t in range(9):
            out = pl.ds(pl.multiple_of(t * FEAT + k * HALF, HALF), HALF)
            v.out_atrous[:, out] = joined[k, :, pl.ds((t + 1) * HALF, HALF)].astype(F32)

    store(c)
    swap_proj.wait()
    for k in range(2):
        v.out_proj[:, pl.ds(k * HALF, HALF)] = v.proj_half[k]
    swap_joined.wait()
    store(1 - c)


def finish_kernel(*refs):
    ins, outs, rooms, (sems_in, sems_out) = refs[:6], refs[6:12], refs[12:18], refs[18:]
    arriving = [pltpu.make_async_copy(ins[k], rooms[k], sems_in.at[k]) for k in range(6)]
    leaving = [pltpu.make_async_copy(rooms[k], outs[k], sems_out.at[k]) for k in range(6)]
    for copy in arriving:
        copy.start()
    for k in range(6):
        arriving[k].wait()
        leaving[k].start()
    for copy in leaving:
        copy.wait()


VMEM = pl.BlockSpec(memory_space=pltpu.VMEM)
ANY = pl.BlockSpec(memory_space=pl.ANY)


def dma(*shape):
    return pltpu.SemaphoreType.DMA(shape)


def sized(dtype, *shape):
    return jax.ShapeDtypeStruct(shape, dtype)


ARGS = ("images", "w_point", "w_atrous", "w_image", "w_proj", "cotangent")
OUTS = (
    ("out_result", sized(BF16, ROWS, COLS, FEAT)),
    ("out_input", sized(BF16, ROWS, COLS, CHANS)),
    ("out_point", sized(F32, SHARD, FEAT)),
    ("out_atrous", sized(F32, SHARD, 9 * FEAT)),
    ("out_image", sized(F32, SHARD, FEAT)),
    ("out_proj", sized(F32, 48, FEAT)),
)
SCRATCH = (
    ("stage", (ROWS, COLS, CHANS), BF16),
    ("cot_stage", (ROWS, COLS, FEAT), BF16),
    ("spots", (DEPTH, CHANS), BF16),
    ("flipped", (CHANS, DEPTH), BF16),
    ("full", (CHANS, WIDER), BF16),
    ("proj", (3 * FEAT, FEAT), BF16),
    ("taps", (TAPS, SPOTS, HALF), F32),
    ("pool_src", (1, CHANS), F32),
    ("pool_slots", (8, 1, CHANS), F32),
    ("pool_rows", (16, 8, SHARD), F32),
    ("pool_all", (16, 8, SHARD), F32),
    ("image_grad", (8, FEAT), F32),
    ("image_all", (16, 8, FEAT), F32),
    ("images_half", (2, 8, HALF), F32),
    ("outer", (2, SPOTS, HALF), BF16),
    ("halo", (2, SPOTS, HALF), BF16),
    ("centre", (SPOTS, HALF), F32),
    ("norm_p", (SPOTS, HALF), F32),
    ("norm_a", (SPOTS, HALF), F32),
    ("slope_p", (SPOTS, HALF), F32),
    ("slope_a", (SPOTS, HALF), F32),
    ("mixed", (SPOTS, HALF), F32),
    ("upstream", (SPOTS, HALF), F32),
    ("relu", (2, SPOTS, FEAT), BF16),
    ("mix", (2, SPOTS, HALF), BF16),
    ("columns", (2, 8, HALF), F32),
    ("cot", (SPOTS, HALF), BF16),
    ("cot_send", (BLOCK, HALF), BF16),
    ("result_send", (2, BLOCK, HALF), BF16),
    ("result_half", (BLOCK, HALF), BF16),
    ("ar_src", (4, 4, HALF), F32),
    ("ar_mid", (4, 4, HALF), F32),
    ("ar_z", (4, 8, 4, HALF), F32),
    ("ar_xy", (4, 16, 4, HALF), F32),
    ("proj_part", (3 * FEAT, HALF), BF16),
    ("proj_slots", (16, 48, HALF), BF16),
    ("proj_sum", (48, HALF), BF16),
    ("proj_all", (8, 48, HALF), BF16),
    ("proj_half", (2, 48, HALF), F32),
    ("norm_send", (SPOTS, HALF), BF16),
    ("norm_halo", (2, SPOTS, HALF), BF16),
    ("up_send", (SPOTS, HALF), BF16),
    ("up_halo", (2, SPOTS, HALF), BF16),
    ("cols", (DEPTH, WIDE), BF16),
    ("partial", (CHANS, WIDE), BF16),
    ("opposite", (10, 2, 32, WIDE), BF16),
    ("beside", (10, 2, 64, WIDE), BF16),
    ("pair", (2, BLOCK, FEAT), F32),
    ("own", (8, BLOCK, FEAT), F32),
    ("away", (8, BLOCK, FEAT), BF16),
    ("came", (8, BLOCK, FEAT), BF16),
    ("z_slots", (8, 16, WIDE), BF16),
    ("z_sum", (16, WIDE), BF16),
    ("joined", (2, SHARD, WIDE), BF16),
)
SEMAPHORES = (
    ("local", (14,)),
    ("core", (11,)),
    ("gather", (40,)),
    ("level", (30,)),
    ("wimage", (15,)),
    ("proj", (15,)),
    ("pool", (7,)),
    ("pall", (15,)),
    ("image", (15,)),
    ("halo", (6,)),
    ("z", (4, 7)),
    ("xy", (4, 15)),
    ("pgrad", (15,)),
    ("ring", (60,)),
    ("zsum", (7,)),
    ("spread", (7,)),
    ("all", (7,)),
)


def on_device(images, w_point, w_atrous, w_image, w_proj, cotangent):
    names = list(ARGS) + [n for n, _ in OUTS] + [n for n, _, _ in SCRATCH]
    scratch = [pltpu.VMEM(shape, dtype) for _, shape, dtype in SCRATCH]
    for name, shape in SEMAPHORES:
        kinds = ("local",) if name == "local" else (name + "_send", name + "_recv")
        for kind in kinds:
            names.append(kind)
            scratch.append(dma(*shape))
    outs = pl.pallas_call(
        functools.partial(whole_kernel, tuple(names)),
        out_shape=[shape for _, shape in OUTS],
        in_specs=[ANY] * 6,
        out_specs=[VMEM] * 6,
        scratch_shapes=scratch,
        compiler_params=pltpu.CompilerParams(
            collective_id=0, has_side_effects=True, vmem_limit_bytes=60 << 20
        ),
        name="whole",
    )(images[0], w_point, w_atrous, w_image, w_proj, cotangent[0])
    outs = pl.pallas_call(
        finish_kernel,
        out_shape=[shape for _, shape in OUTS],
        in_specs=[ANY] * 6,
        out_specs=[ANY] * 6,
        scratch_shapes=[pltpu.VMEM(shape.shape, shape.dtype) for _, shape in OUTS] + [dma(6), dma(6)],
        compiler_params=pltpu.CompilerParams(vmem_limit_bytes=60 << 20),
        name="finish",
    )(*outs)
    return (outs[0][None], outs[1][None], *outs[2:])


def solution(mesh):
    finer = Mesh(mesh.devices.reshape(8, 2, 4, 4), STRIP + SAMPLE)
    placed = (
        P(SAMPLE, STRIP, None, None),
        P(SAMPLE, None),
        P(SAMPLE, None),
        P(SAMPLE, None),
        P(SAMPLE, None),
        P(SAMPLE, STRIP, None, None),
    )
    return jax.shard_map(
        on_device,
        mesh=finer,
        in_specs=placed,
        out_specs=(
            P(SAMPLE, STRIP, None, None),
            P(SAMPLE, STRIP, None, None),
            P(SAMPLE, None),
            P(SAMPLE, None),
            P(SAMPLE, None),
            P(SAMPLE, None),
        ),
        check_vma=False,
    )
```
